256 devices in a mesh: pair: 2 (over core), seq: 32 (over x, z), asset: 4 (over y).
Axes of the slice: x: 4, y: 4, z: 8, core: 2. Of those that a mesh axis runs over, the one named last changes fastest.
Arguments:
- latents: float32 [4, 8, 4096], P('asset', None, 'seq'), may hold values from -6 to 6
- voxel_coords: int32 [4, 3, 4096], P('asset', None, 'seq'), may hold values from 0 to 63
- owner_map: int32 [4, 4096, 1], P('asset', 'seq'), may hold values from 0 to 31; in each aligned block of 128 rows (0 to 127, 128 to 255, ..., all dimensions but the last counted through in order) at most 8 rows name the same one
- step_time: float32 [4], P('asset'), may hold values from 0.2 to 0.5
- modulation: float32 [4, 2, 5, 1024], P('asset', 'pair'), may hold values from -3 to 3
- in_proj: float32 [8, 1024], replicated, may hold values from -2 to 2
- qkv_proj: bfloat16 [1024, 1536], replicated, may hold values from -0.1875 to 0.1875
- norm_gain: float32 [2, 512], replicated, may hold values from 1.5 to 3
- out_proj: bfloat16 [512, 1024], replicated, may hold values from -0.25 to 0.25
- head_proj: float32 [1024, 8], replicated, may hold values from -0.1875 to 0.1875
- decoder_projection: float32 [8, 768], replicated, may hold values from -2 to 2
- border_blocks: int32 [4, 32, 2, 8], P('asset', 'seq'), may hold values from 0 to 15
- kernel_map: int32 [4, 32, 27, 1024], P('asset', 'seq'), may hold values from 0 to 512
- conv_weight: bfloat16 [27, 768, 192], P(None, None, 'pair'), may hold values from -0.0390625 to 0.0390625
Outputs:
- owned_latents: float32 [4, 32, 8, 256], P('asset', 'seq')
- decoded: bfloat16 [4, 32, 1024, 192], P('asset', 'seq', None, 'pair')
The draws below stay inside these ranges and needn't reach their ends.
Inputs may be any that keep to these rules, and one draw needn't show every extreme that they name: `owner_map`: in each aligned block of 128 tokens (the tokens of one device) no owner is named by more than 8 tokens. `kernel_map`: rows below 256 are the owner's slots, the next 128 come from the owner below, the next 128 from the owner above, and 512 is the zero row.
All inputs are finite; a program needn't handle non-finite values.
Results may differ from the reference program's by a relative error of at most 0.0075.
Values may be sent and summed in bfloat16 or wider, within the bound.
A program may use at most 128 MiB of HBM per device.

```python
import math
import jax
import jax.numpy as jnp
import numpy as np
from jax import lax

D = 1024
HEADS = 8
HEAD = 64
LAT = 8
DEC = 768
OUTC = 192
KOFF = 27
BLK = 16
HB = 8
RES = 64
TOK_DEV = 128
ASSETS = 4
SEQ_LEN = 4096
CAP = 8
SLOTS = 256
HALO = 128
TABLE = 512
FINE = 1024
HW = 512
N_SEQ = 32


def touch_ends(array, stream_key, smallest, top_value):
    extent = array.shape
    spot = [jax.random.randint(jax.random.fold_in(stream_key, axis), (), 0, extent[axis]) for axis in range(len(extent))]
    array = array.at[tuple(spot)].set(smallest)
    longest = extent.index(max(extent))
    spot[longest] = (spot[longest] + 1) % extent[longest]
    return array.at[tuple(spot)].set(top_value)


def steps_of(key, shape, cuts, smallest, top_value):
    level, own = 1.0, jax.random.fold_in(key, 6)
    for dim, blocks in cuts:
        heights = jnp.exp(jax.random.uniform(jax.random.fold_in(own, dim), (blocks,), jnp.float32, smallest / len(cuts), top_value / len(cuts)))
        level = level * jnp.repeat(heights, shape[dim] // blocks).reshape([-1 if axis == dim else 1 for axis in range(len(shape))])
    return level


def routed_block(rng, own, number, rows, count, top, reach, slope):
    order = jax.random.permutation(rng, count)
    packed, common = portions_of(count, rows * top, reach, slope, True), portions_of(count, rows * top, reach, slope, False)
    places = jnp.arange(count)

    def named(sizes, turn):
        used = int((sizes > 0).sum())
        fixed = max(1, used // 4)
        passed = fixed + (places - fixed + turn * (used - fixed)) % max(1, count - fixed)
        return jnp.zeros((count,), jnp.int32).at[order[jnp.where(places < fixed, places, passed)]].set(jnp.asarray(sizes, jnp.int32))

    sizes = jnp.where(number % 4 == 0, named(packed, number // 4), named(common, number - number // 4 - 1))
    mixed = jax.random.permutation(jax.random.fold_in(own, 3), count)
    source_of, sink = mixed[0:count // 2 * 2:2], mixed[1:count // 2 * 2:2]
    room = jnp.minimum(sizes[source_of] - 1, reach - sizes[sink]) // 2
    room = jnp.where((source_of == order[0]) | (sink == order[0]) | (sizes[sink] == 0), 0, jnp.maximum(room, 0))
    passed = jax.random.randint(jax.random.fold_in(own, 4), (count // 2,), 0, 1 << 20) % (room + 1)
    sizes = sizes.at[source_of].add(-passed).at[sink].add(passed)
    labels = jnp.searchsorted(jnp.cumsum(sizes), jnp.arange(rows * top), side="right").astype(jnp.int32)
    listing = labels.reshape(top, rows).T
    listing = listing[jax.random.permutation(jax.random.fold_in(own, 1), rows)]
    turn = jax.random.randint(jax.random.fold_in(own, 2), (rows, 1), 0, top)
    return jnp.take_along_axis(listing, (jnp.arange(top)[None, :] + turn) % top, axis=1)


def portions_of(count, total, most, slope, full):
    portions = [(1 << 20) // math.isqrt(standing ** slope) + 1 for standing in range(1, count + 1)]
    largest = most if full else min(most, max(-(-total // count), total * portions[0] // sum(portions)))
    least = 1 if total - largest >= count - 1 else 0
    counts, surplus = [largest] + [least] * (count - 1), total - largest - least * (count - 1)
    while surplus > 0:
        movable = [i for i in range(1, count) if counts[i] < largest] or [i for i in range(1, count) if counts[i] < most]
        pool, remaining = sum([portions[i] for i in movable]), surplus
        for i in movable:
            extra = min(most - counts[i], max(1, remaining * portions[i] // pool), surplus)
            counts[i] = counts[i] + extra
            surplus = surplus - extra
    return np.array(counts)


def centred(rng, extent, scale, bound, shards=(), held_as=jnp.bfloat16):
    values = jax.random.normal(rng, extent, jnp.float32) * scale
    if len(shards) > 0:
        values = steps_of(rng, extent, shards, -0.22, 0.18) * values
    return jnp.clip(values, min=-bound, max=bound).astype(held_as)


def setup_inputs(seed: int = 0) -> dict:
    key_of = jax.random.split(jax.random.key(seed), 15)
    latents = centred(key_of[0], (ASSETS, LAT, SEQ_LEN), 1.0, 6.0, ((0, 4), (2, 32)), jnp.float32)
    voxel_coords = touch_ends(jax.random.randint(key_of[1], (ASSETS, 3, SEQ_LEN), 0, RES), jax.random.fold_in(key_of[1], 1), 0, RES - 1).astype(jnp.int32)
    owner_map_keys = jax.random.split(jax.random.fold_in(key_of[2], 1), ASSETS * SEQ_LEN // TOK_DEV)
    owner_map_turns = jax.random.permutation(jax.random.fold_in(key_of[2], 3), ASSETS * SEQ_LEN // TOK_DEV)
    owner_map = jax.vmap(lambda own, number: routed_block(jax.random.fold_in(key_of[2], 2), own, number, TOK_DEV, N_SEQ, 1, CAP, 2))(owner_map_keys, owner_map_turns).reshape((ASSETS, SEQ_LEN, 1))
    step_time = jnp.clip(0.2 + 0.3 * jax.random.uniform(key_of[3], (ASSETS,), jnp.float32) ** steps_of(key_of[3], (ASSETS,), ((0, 4),), -0.2, 0.2), 0.2, 0.5)
    modulation = centred(key_of[4], (ASSETS, 2, 5, D), 0.5, 3.0, ((0, 4), (1, 2)), jnp.float32)
    in_proj = centred(key_of[5], (LAT, D), LAT ** -0.5, 2.0, (), jnp.float32)
    qkv_proj = centred(key_of[6], (D, 3 * HW), D ** -0.5, 0.1875)
    norm_gain = jnp.clip(jax.random.uniform(key_of[7], (2, HW), jnp.float32, 1.5, 3.0), 1.5, 3.0)
    out_proj = centred(key_of[8], (HW, D), HW ** -0.5, 0.25)
    head_proj = centred(key_of[9], (D, LAT), D ** -0.5, 0.1875, (), jnp.float32)
    decoder_projection = centred(key_of[10], (LAT, DEC), LAT ** -0.5, 2.0, (), jnp.float32)
    border_blocks = touch_ends(jax.random.randint(key_of[11], (ASSETS, N_SEQ, 2, HB), 0, SLOTS // BLK), jax.random.fold_in(key_of[11], 1), 0, (SLOTS // BLK) - 1).astype(jnp.int32)
    kernel_map = touch_ends(jax.random.randint(key_of[12], (ASSETS, N_SEQ, KOFF, FINE), 0, TABLE + 1), jax.random.fold_in(key_of[12], 1), 0, TABLE).astype(jnp.int32)
    conv_weight = centred(key_of[13], (KOFF, DEC, OUTC), (KOFF * DEC) ** -0.5, 0.0390625, ((2, 2),))
    return dict(latents=latents, voxel_coords=voxel_coords, owner_map=owner_map, step_time=step_time, modulation=modulation, in_proj=in_proj, qkv_proj=qkv_proj, norm_gain=norm_gain, out_proj=out_proj, head_proj=head_proj, decoder_projection=decoder_projection, border_blocks=border_blocks, kernel_map=kernel_map, conv_weight=conv_weight)


EPSILON = 1e-06
GUIDANCE = 3.0
TOP_PRECISION = lax.Precision.HIGHEST

def layer_norm(values):
    center = values - lax.optimization_barrier(jnp.mean(values, axis=-1, keepdims=True))
    variance = lax.optimization_barrier(jnp.mean(center * center, axis=-1, keepdims=True))
    return center / jnp.sqrt(variance + EPSILON)

def position_table(coord_rows, model_width):
    freqs = model_width // 6
    steps = jnp.arange(freqs, dtype=jnp.float32) / freqs
    omegas = jnp.exp(-math.log(10000.0) * steps)
    angles = coord_rows.astype(jnp.float32)[:, :, None] * omegas[None, None, :]
    halves = jnp.concatenate([jnp.sin(angles), jnp.cos(angles)], axis=2)
    rows_out = jnp.transpose(halves, (1, 0, 2)).reshape(coord_rows.shape[1], 6 * freqs)
    return jnp.pad(rows_out, ((0, 0), (0, model_width - 6 * freqs)))

def head_norm(values, gains):
    row_count = values.shape[0]
    per_head = values.reshape(row_count, HEADS, HEAD)
    mean_square = lax.optimization_barrier(jnp.mean(per_head * per_head, axis=2, keepdims=True))
    return (per_head / jnp.sqrt(mean_square + EPSILON)).reshape(row_count, HEADS * HEAD) * gains

def attention(queries, keys_in, values_in):
    row_count = queries.shape[0]
    block_rows = math.gcd(row_count, 512)
    factor = HEAD ** (-0.5)
    key_heads = keys_in.reshape(row_count, HEADS, HEAD).astype(jnp.float32)
    value_head_rows = values_in.reshape(row_count, HEADS, HEAD).astype(jnp.float32)

    def one_block(query_block):
        scores = jnp.einsum('qhd,khd->hqk', query_block.astype(jnp.float32), key_heads) * factor
        exp_scores = jnp.exp(scores)
        rounded_count = lax.optimization_barrier(exp_scores.astype(jnp.bfloat16))
        numerator = jnp.einsum('hqk,khd->qhd', rounded_count.astype(jnp.float32), value_head_rows)
        denominator = lax.optimization_barrier(jnp.sum(exp_scores, axis=2)).T
        return (numerator / denominator[:, :, None]).astype(jnp.bfloat16)
    blocks_out = lax.map(one_block, queries.reshape(row_count // block_rows, block_rows, HEADS, HEAD))
    return blocks_out.reshape(row_count, HEADS * HEAD)

def branch_velocity(latent_block, coord_rows, modulation_rows, in_proj, qkv_proj, norm_gain, out_proj, head_proj):
    hidden = jnp.dot(latent_block.T, in_proj, precision=TOP_PRECISION) + position_table(coord_rows, D)
    normed = (layer_norm(hidden) * (1.0 + modulation_rows[1]) + modulation_rows[0]).astype(jnp.bfloat16)
    projected = jnp.dot(normed, qkv_proj, preferred_element_type=jnp.float32)
    inner_width = HEADS * HEAD
    queries = head_norm(projected[:, :inner_width], norm_gain[0]).astype(jnp.bfloat16)
    keys_in = head_norm(projected[:, inner_width:2 * inner_width], norm_gain[1]).astype(jnp.bfloat16)
    values_in = projected[:, 2 * inner_width:].astype(jnp.bfloat16)
    attended = attention(queries, keys_in, values_in)
    hidden = hidden + modulation_rows[2] * jnp.dot(attended, out_proj, preferred_element_type=jnp.float32)
    final = layer_norm(hidden) * (1.0 + modulation_rows[4]) + modulation_rows[3]
    return jnp.dot(final, head_proj, precision=TOP_PRECISION).T

def relayout(clean, owner_rows):
    owner_ids = jnp.arange(N_SEQ, dtype=jnp.int32)
    onehot = (owner_rows[:, None] == owner_ids[None, :]).astype(jnp.int32)
    onehot = onehot.reshape(N_SEQ, TOK_DEV, N_SEQ)
    ranks = lax.optimization_barrier(jnp.sum(onehot * (jnp.cumsum(onehot, axis=1).astype(jnp.int32) - 1), axis=2)).astype(jnp.int32)
    ranks = ranks.reshape(SEQ_LEN)
    sources = jnp.arange(SEQ_LEN, dtype=jnp.int32) // TOK_DEV
    slot_ids = (sources * CAP + ranks).astype(jnp.int32)
    owned_rows = jnp.zeros((N_SEQ, SLOTS, LAT), jnp.float32).at[owner_rows, slot_ids].set(clean.T)
    return jnp.transpose(owned_rows, (0, 2, 1))

def decode(owned_rows, border_rows, map_rows, decoder_projection, conv_weight):
    owner_count = owned_rows.shape[0]
    voxel_features = jax.nn.silu(jnp.einsum('pjw,jm->pwm', owned_rows, decoder_projection, precision=TOP_PRECISION)).astype(jnp.bfloat16)
    tiles = voxel_features.reshape(owner_count, SLOTS // BLK, BLK, DEC)
    border = jax.vmap(lambda tile_rows, chosen: tile_rows[chosen.reshape(-1)])(tiles, border_rows)
    border = border.reshape(owner_count, 2, HALO, DEC)
    empty_rows = jnp.zeros((1, HALO, DEC), jnp.bfloat16)
    received_below = jnp.concatenate([empty_rows, border[:-1, 1]], axis=0)
    from_above = jnp.concatenate([border[1:, 0], empty_rows], axis=0)
    zero_row = jnp.zeros((owner_count, 1, DEC), jnp.bfloat16)
    tables = jnp.concatenate([voxel_features, received_below, from_above, zero_row], axis=1)
    offsets = jnp.arange(KOFF, dtype=jnp.int32)[:, None]
    weight_full = conv_weight.astype(jnp.float32)

    def one_owner(inputs):
        rows_table, index_map = inputs
        products = jnp.einsum('rc,kco->kro', rows_table.astype(jnp.float32), weight_full)
        return lax.optimization_barrier(jnp.sum(products[offsets, index_map], axis=0)).astype(jnp.bfloat16)
    return lax.map(one_owner, (tables, map_rows))

def reference(latents, voxel_coords, owner_map, step_time, modulation, in_proj, qkv_proj, norm_gain, out_proj, head_proj, decoder_projection, border_blocks, kernel_map, conv_weight):
    owned_list = []
    decoded_list = []
    for asset_id in range(ASSETS):
        velocities = [branch_velocity(latents[asset_id], voxel_coords[asset_id], modulation[asset_id, branch], in_proj, qkv_proj, norm_gain, out_proj, head_proj) for branch in range(2)]
        guided = velocities[1] + GUIDANCE * (velocities[0] - velocities[1])
        clean = latents[asset_id] - step_time[asset_id] * guided
        owned_rows = relayout(clean, owner_map[asset_id, :, 0])
        owned_list.append(owned_rows)
        decoded_list.append(decode(owned_rows, border_blocks[asset_id], kernel_map[asset_id], decoder_projection, conv_weight))
    return (jnp.stack(owned_list), jnp.stack(decoded_list))
```

```python
import math

import jax
import jax.numpy as jnp
import numpy as np
from jax import lax
from jax.experimental import pallas as pl
from jax.experimental.pallas import tpu as pltpu
from jax.sharding import PartitionSpec as P

D = 1024
HEADS = 8
HEAD = 64
LAT = 8
DEC = 768
KOFF = 27
BLK = 16
RES = 64
TOK = 128
CAP = 8
SLOTS = 256
HALO = 128
FINE = 1024
HW = 512
NX = 4
NZ = 8
N_SEQ = 32
OUT_DEV = 96
GROUP = NX * TOK
FEAT = 256
EPSILON = 1e-06
GUIDANCE = 3.0
LOG2E = 1.4426950408889634
HI = lax.Precision.HIGHEST
F32 = jnp.float32
BF16 = jnp.bfloat16


def centred_position_table():
    freqs = D // 6
    omegas = np.exp(-math.log(10000.0) * (np.arange(freqs) / freqs))
    angles = np.arange(RES)[:, None] * omegas[None, :]
    halves = np.concatenate([np.sin(angles), np.cos(angles)], axis=1)
    table = np.zeros((3 * RES, D))
    for axis in range(3):
        table[axis * RES : (axis + 1) * RES, axis * 2 * freqs : (axis + 1) * 2 * freqs] = halves
    return (table - table.mean(axis=1, keepdims=True)).astype(np.float32)


def split(values):
    high = values.astype(BF16)
    return high, (values - high.astype(F32)).astype(BF16)


def mm(a, b):
    return lax.dot_general(a, b, (((1,), (0,)), ((), ())), preferred_element_type=F32)


def mm_nt(a, b):
    return lax.dot_general(a, b, (((1,), (1,)), ((), ())), preferred_element_type=F32)


def mm3(a, b, product=mm):
    a_high, a_low = split(a)
    b_high, b_low = split(b)
    return product(a_high, b_high) + (product(a_high, b_low) + product(a_low, b_high))


def exact(a, b):
    return jnp.dot(a, b, precision=HI, preferred_element_type=F32)


def iota(shape, dim):
    return lax.broadcasted_iota(jnp.int32, shape, dim)


def one_hots(rows, width):
    ids = iota((RES, width), 0).astype(F32)
    return [jnp.where(ids == rows[c : c + 1, :], 1.0, 0.0) for c in range(3)]


def flow_kernel(
    lat_ref, coord_ref, own_ref, step_ref, mod_ref, inp_ref, gain_ref, head_ref, bb_ref, tab_ref, wqkv_hbm, wout_hbm,
    x_ref, nb_ref,
    gath, stage, wqkv, wout, bkt, bv_high, bv_low, gmat, umat, hid_ref, ft_ref, acc, rank_ref, headt, sendbuf, rbuf,
    lsem, xs_sem, xr_sem, zs_sem, zr_sem, as_sem, ar_sem,
):
    me = lax.axis_index("seq")
    pair = lax.axis_index("pair")
    x_me = me // NZ
    z_me = me % NZ

    def x_copy(shift):
        peer = ((x_me + shift) % NX) * NZ + z_me
        return pltpu.make_async_remote_copy(
            src_ref=gath.at[z_me, x_me], dst_ref=gath.at[z_me, x_me],
            send_sem=xs_sem.at[shift - 1], recv_sem=xr_sem.at[shift - 1],
            device_id={"seq": peer}, device_id_type=pl.DeviceIdType.MESH)

    def z_copy(shift):
        peer = x_me * NZ + (z_me + shift) % NZ
        return pltpu.make_async_remote_copy(
            src_ref=gath.at[z_me], dst_ref=gath.at[z_me],
            send_sem=zs_sem.at[shift - 1], recv_sem=zr_sem.at[shift - 1],
            device_id={"seq": peer}, device_id_type=pl.DeviceIdType.MESH)

    def a_copy(core, shift):
        dest = (me + shift) % N_SEQ
        return pltpu.make_async_remote_copy(
            src_ref=sendbuf.at[dest], dst_ref=rbuf.at[pair, me],
            send_sem=as_sem.at[core, shift], recv_sem=ar_sem.at[core, shift],
            device_id={"pair": (pair + core) % 2, "seq": dest}, device_id_type=pl.DeviceIdType.MESH)

    barrier = pltpu.get_barrier_semaphore()

    def greet(shift, carry):
        dest = (me + shift) % N_SEQ
        for core in range(2):
            @pl.when((shift > 0) | (core > 0))
            def _():
                pl.semaphore_signal(barrier, inc=1, device_id={"pair": (pair + core) % 2, "seq": dest},
                                    device_id_type=pl.DeviceIdType.MESH)
        return carry

    lax.fori_loop(0, N_SEQ, greet, 0)

    load_qkv = pltpu.make_async_copy(wqkv_hbm, wqkv, lsem.at[0])
    load_qkv.start()
    load_out = pltpu.make_async_copy(wout_hbm, wout, lsem.at[1])
    load_out.start()

    lat = lat_ref[...]
    stage[...] = jnp.zeros((16, TOK), F32)
    stage[0:8, :] = lat
    stage[8:11, :] = coord_ref[...].astype(F32)
    stage[11:13, 0:8] = bb_ref[...].astype(F32)
    packet = stage[...]
    gath[z_me, x_me] = packet.astype(BF16)

    lat_high = lat.astype(BF16).astype(F32)
    lat_low = lat - lat_high
    zero8 = jnp.zeros((8, TOK), F32)
    own_feat = jnp.concatenate(
        one_hots(packet[8:11, :], TOK) + [lat_high, zero8, lat_low, jnp.zeros((40, TOK), F32)], axis=0)
    own_feat = own_feat.T.astype(BF16)
    table = tab_ref[...]
    inp = inp_ref[...]
    inp = inp - jnp.mean(inp, axis=1, keepdims=True)
    basis = jnp.concatenate(
        [table, inp, jnp.zeros((8, D), F32), inp, jnp.zeros((40, D), F32)], axis=0)
    basis_high, basis_low = split(basis)
    hidden = mm(own_feat, basis_high) + mm(own_feat, basis_low)
    hid_ref[...] = hidden
    center = hidden - jnp.mean(hidden, axis=1, keepdims=True)
    variance = jnp.mean(center * center, axis=1, keepdims=True)
    scale1 = 1.0 + mod_ref[1:2, :]
    normed = (center * lax.rsqrt(variance + EPSILON) * scale1 + mod_ref[0:1, :]).astype(BF16)

    own_rows = jnp.broadcast_to(own_ref[...], (TOK, TOK)).astype(F32)
    own_cols = own_rows.T
    earlier = (own_rows == own_cols) & (iota((TOK, TOK), 1) < iota((TOK, TOK), 0))
    rank = jnp.sum(jnp.where(earlier, 1.0, 0.0), axis=1, keepdims=True)
    rank_ref[...] = jnp.where(rank == ((iota((TOK, TOK), 1) // LAT) % CAP).astype(F32), 1.0, 0.0)

    pl.semaphore_wait(barrier, 2 * N_SEQ - 1)
    for shift in range(1, NX):
        x_copy(shift).start()

    spread = jnp.where((iota((LAT, TOK), 1) % LAT) == iota((LAT, TOK), 0), 1.0, 0.0)
    headt[...] = exact(head_ref[...], spread)
    gram = mm_nt(basis_high, basis_high) + (mm_nt(basis_high, basis_low) + mm_nt(basis_low, basis_high))
    gram_high, gram_low = split(gram * (1.0 / D))
    gmat[0:FEAT, :] = gram_high
    gmat[FEAT : 2 * FEAT, :] = gram_low

    shift_rows = jnp.where(iota((8, D), 0) < 2, jnp.broadcast_to(mod_ref[0:1, :], (8, D)), 0.0)
    scaled = jnp.concatenate(
        [table * scale1, inp * scale1, shift_rows, jnp.zeros((48, D), F32)], axis=0)
    scaled_high, scaled_low = split(scaled)
    load_qkv.wait()
    keys_of = mm(scaled_high, wqkv[:, HW : 2 * HW]) + mm(scaled_low, wqkv[:, HW : 2 * HW])
    keys_t_high, keys_t_low = split(keys_of.T)
    bkt[...] = keys_t_high

    queries = mm(normed, wqkv[:, 0:HW])
    squares = queries * queries
    sq_high, sq_low = split(squares)
    per_head = jnp.where(iota((HW, HW), 0) // HEAD == iota((HW, HW), 1) // HEAD, 1.0 / HEAD, 0.0).astype(BF16)
    mean_sq = mm(sq_high, per_head) + mm(sq_low, per_head)
    queries = (queries * lax.rsqrt(mean_sq + EPSILON) * gain_ref[0:1, :]).astype(BF16).astype(F32)
    queries = queries * (gain_ref[1:2, :] * (HEAD ** (-0.5) * LOG2E))
    first_half = iota((TOK, 2 * HEAD), 1) < HEAD
    for two in range(HEADS // 2):
        columns = slice(two * 2 * HEAD, (two + 1) * 2 * HEAD)
        both = queries[:, columns]
        for odd in range(2):
            mine = jnp.where(first_half if odd == 0 else ~first_half, both, 0.0)
            q_high, q_low = split(mine)
            k_high, k_low = keys_t_high[columns, :], keys_t_low[columns, :]
            umat[2 * two + odd] = (mm(q_high, k_high) + (mm(q_high, k_low) + mm(q_low, k_high))).astype(BF16)

    for shift in range(1, NX):
        x_copy(shift).wait_recv()
    for shift in range(1, NZ):
        z_copy(shift).start()

    values_of = mm(scaled_high, wqkv[:, 2 * HW : 3 * HW]) + mm(scaled_low, wqkv[:, 2 * HW : 3 * HW])
    bv_high[...], bv_low[...] = split(values_of)
    acc[...] = jnp.zeros((HEADS, TOK, FEAT), F32)

    def one_group(step, carry):
        back = jnp.where(step % 2 == 0, (NZ - step // 2) % NZ, (step + 1) // 2)

        @pl.when(step > 0)
        def _():
            source = (z_me + NZ - back) % NZ
            pltpu.make_async_remote_copy(
                src_ref=gath.at[source], dst_ref=gath.at[source],
                send_sem=zs_sem.at[back - 1], recv_sem=zr_sem.at[back - 1],
                device_id={"seq": me}, device_id_type=pl.DeviceIdType.MESH).wait_recv()

        group = (z_me + NZ - back) % NZ
        rows = jnp.concatenate([gath[group, i].astype(F32) for i in range(NX)], axis=1)
        hots = one_hots(rows[8:11, :], GROUP)
        rest = jnp.concatenate([rows[0:8, :], jnp.zeros((56, GROUP), F32)], axis=0)
        plain = jnp.concatenate(hots + [rest], axis=0)
        plain_high = plain.astype(BF16)
        image = mm(gmat[0:FEAT, :], plain_high) + mm(gmat[FEAT : 2 * FEAT, :], plain_high)
        var_eps = jnp.sum(image * plain, axis=0, keepdims=True) + EPSILON
        std = jnp.sqrt(var_eps)
        log_std = (0.5 * LOG2E) * jnp.log(var_eps)
        std_high = std.astype(BF16).astype(F32)
        which = iota((8, GROUP), 0)
        std_rows = jnp.where(which == 0, std_high, jnp.where(which == 1, std - std_high, 0.0))
        rest = jnp.concatenate([rows[0:8, :], std_rows, jnp.zeros((48, GROUP), F32)], axis=0)
        ft_ref[0 : 3 * RES, :] = plain_high[0 : 3 * RES, :]
        ft_ref[3 * RES : FEAT, :] = rest.astype(BF16)
        for head in range(HEADS):
            keys_h = mm(bkt[head * HEAD : (head + 1) * HEAD, :], ft_ref[...])
            mean_h = jnp.sum(keys_h * keys_h, axis=0, keepdims=True) * (1.0 / HEAD)
            inv = lax.rsqrt(mean_h + EPSILON * var_eps)
            scores = mm(umat[head], ft_ref[...]) * inv - log_std
            weights = jnp.exp2(scores).astype(BF16)
            acc[head] += mm_nt(weights, ft_ref[...])
        return carry

    lax.fori_loop(0, NZ, one_group, 0)

    load_out.wait()
    lane = iota((TOK, FEAT), 1)
    pieces = []
    for two in range(HEADS // 2):
        columns = slice(two * 2 * HEAD, (two + 1) * 2 * HEAD)
        halves = []
        for odd in range(2):
            total = acc[2 * two + odd]
            denom = jnp.sum(jnp.where((lane == 200) | (lane == 201), total, 0.0), axis=1, keepdims=True)
            t_high, t_low = split(total * (1.0 / denom))
            halves.append(mm(t_high, bv_high[:, columns])
                          + (mm(t_low, bv_high[:, columns]) + mm(t_high, bv_low[:, columns])))
        pieces.append(jnp.where(first_half, halves[0], halves[1]))
    attended = jnp.concatenate(pieces, axis=1).astype(BF16)
    hidden = hid_ref[...] + mod_ref[2:3, :] * mm(attended, wout[...])
    center = hidden - jnp.mean(hidden, axis=1, keepdims=True)
    variance = jnp.mean(center * center, axis=1, keepdims=True)
    final = center * lax.rsqrt(variance + EPSILON) * (1.0 + mod_ref[4:5, :]) + mod_ref[3:4, :]
    velocity = mm3(final, headt[...])

    lat_cols = jnp.concatenate([lat_ref[...]] * (TOK // LAT), axis=0).T
    when_step = step_ref[0]
    is_cond = pair == 0
    share = jnp.where(is_cond, 1.0, 0.0) * lat_cols + (
        when_step * jnp.where(is_cond, -GUIDANCE, GUIDANCE - 1.0)) * velocity
    share = share * rank_ref[...]
    own32 = jnp.broadcast_to(own_ref[...], (N_SEQ, TOK))
    owner = iota((N_SEQ, TOK), 0)
    here = exact(jnp.where(own32 == owner, 1.0, 0.0), share)
    below = exact(jnp.where(own32 == owner - 1, 1.0, 0.0), share)
    above = exact(jnp.where(own32 == owner + 1, 1.0, 0.0), share)
    sendbuf[:, 0, :] = jnp.where(iota((N_SEQ, TOK), 1) < LAT * CAP, here, below)
    sendbuf[:, 1, :] = above

    keep = pltpu.make_async_copy(sendbuf.at[me], rbuf.at[pair, me], lsem.at[2])
    keep.start()

    def send(shift, carry):
        for core in range(2):
            @pl.when((shift > 0) | (core > 0))
            def _():
                a_copy(core, shift).start()
        return carry

    lax.fori_loop(0, N_SEQ, send, 0)

    lower = jnp.maximum(me - 1, 0)
    upper = jnp.minimum(me + 1, N_SEQ - 1)
    nb_ref[0:1, :] = gath[lower % NZ, lower // NZ].astype(F32)[12:13, :]
    nb_ref[1:2, :] = gath[upper % NZ, upper // NZ].astype(F32)[11:12, :]
    nb_ref[2:8, :] = jnp.zeros((6, TOK), F32)

    for shift in range(1, NX):
        x_copy(shift).wait_send()
    for shift in range(1, NZ):
        z_copy(shift).wait_send()

    def arrive(shift, carry):
        for core in range(2):
            @pl.when((shift > 0) | (core > 0))
            def _():
                source = (me + N_SEQ - shift) % N_SEQ
                pltpu.make_async_remote_copy(
                    src_ref=sendbuf.at[source], dst_ref=rbuf.at[(pair + core) % 2, source],
                    send_sem=as_sem.at[core, shift], recv_sem=ar_sem.at[core, shift],
                    device_id={"pair": pair, "seq": me}, device_id_type=pl.DeviceIdType.MESH).wait()
        return carry

    keep.wait()
    lax.fori_loop(0, N_SEQ, arrive, 0)
    x_ref[...] = rbuf[0] + rbuf[1]


def conv_kernel(x_ref, nb_ref, km_ref, dproj_ref, w_ref, owned_ref, dec_ref, feats, wpair, kmt, acc):
    x0 = x_ref[:, 0, :]
    x1 = x_ref[:, 1, :]

    slot = iota((N_SEQ, SLOTS), 1)
    pick = jnp.where(slot // CAP == iota((N_SEQ, SLOTS), 0), 1.0, 0.0)
    wide = lax.dot_general(x0, pick, (((0,), (0,)), ((), ())), precision=HI, preferred_element_type=F32)
    row = iota((TOK, SLOTS), 0)
    wide = jnp.where((iota((TOK, SLOTS), 1) % CAP == row // LAT), wide, 0.0)
    fold = jnp.where(iota((LAT, TOK), 1) % LAT == iota((LAT, TOK), 0), 1.0, 0.0)
    owned_ref[...] = exact(fold, wide)

    lane = iota((SLOTS, TOK), 1)
    own_rows = jnp.where(lane // LAT == iota((SLOTS, TOK), 0) // N_SEQ, jnp.concatenate([x0] * CAP, axis=0), 0.0)
    sub = iota((HALO, TOK), 0)
    lane = iota((HALO, TOK), 1)
    parts = [own_rows]
    for side, x_side in ((0, x0), (1, x1)):
        blocks = jnp.broadcast_to(nb_ref[side : side + 1, :], (HALO, TOK))
        chosen = jnp.sum(jnp.where(lane == sub // BLK, blocks, 0.0), axis=1, keepdims=True)
        source = chosen * (BLK // CAP) + ((iota((HALO, 1), 0) % BLK) // CAP).astype(F32)
        pick = jnp.where(iota((HALO, N_SEQ), 1).astype(F32) == source, 1.0, 0.0)
        rows = exact(pick, x_side)
        offset = CAP if side == 0 else 0
        parts.append(jnp.where(lane // LAT == sub % CAP + offset, rows, 0.0))
    latents = jnp.concatenate(parts, axis=0)
    proj = jnp.concatenate([dproj_ref[...]] * (TOK // LAT), axis=0)
    value = mm3(latents, proj)
    feats[...] = (value / (1.0 + jnp.exp(-value))).astype(BF16)

    kmt[...] = jnp.concatenate([km_ref[...].astype(F32), jnp.zeros((TOK - KOFF, FINE), F32)], axis=0).T
    acc[...] = jnp.zeros((FINE, TOK), F32)
    place = iota((1, 2 * SLOTS), 1)
    slots = jnp.where(place < SLOTS, (place % N_SEQ) * CAP + place // N_SEQ, place).astype(F32)
    for j in range(2):
        wpair[j] = jnp.zeros((DEC, 2 * TOK), BF16)

    def products(offset):
        wpair[0, :, 0:OUT_DEV] = w_ref[offset]
        return mm(feats[...], wpair[0, :, 0:TOK]).astype(BF16)

    def one_offset(offset, carry):
        prod = products(offset)
        for m in range(4):
            rows = slice(m * 256, (m + 1) * 256)
            index = kmt[rows, 0:1]
            hot = jnp.where(index == slots, 1.0, 0.0).astype(BF16)
            acc[rows, :] += mm(hot, prod)
        kmt[...] = pltpu.roll(kmt[...], TOK - 1, 1)
        return carry

    lax.fori_loop(0, KOFF, one_offset, 0)
    dec_ref[...] = acc[:, 0:OUT_DEV].astype(BF16)


def vmem(count):
    return [pl.BlockSpec(memory_space=pltpu.VMEM)] * count


def per_device(
    latents, voxel_coords, owner_map, step_time, modulation, in_proj, qkv_proj, norm_gain, out_proj, head_proj,
    decoder_projection, border_blocks, kernel_map, conv_weight,
):
    table = jnp.asarray(centred_position_table())
    dma = pltpu.SemaphoreType.DMA
    gathered, borders = pl.pallas_call(
        flow_kernel,
        out_shape=(jax.ShapeDtypeStruct((N_SEQ, 2, TOK), F32), jax.ShapeDtypeStruct((8, TOK), F32)),
        in_specs=vmem(3) + [pl.BlockSpec(memory_space=pltpu.SMEM)] + vmem(6) + [pl.BlockSpec(memory_space=pl.ANY)] * 2,
        out_specs=tuple(vmem(2)),
        scratch_shapes=[
            pltpu.VMEM((NZ, NX, 16, TOK), BF16),
            pltpu.VMEM((16, TOK), F32),
            pltpu.VMEM((D, 3 * HW), BF16),
            pltpu.VMEM((HW, D), BF16),
            pltpu.VMEM((HW, FEAT), BF16),
            pltpu.VMEM((FEAT, HW), BF16),
            pltpu.VMEM((FEAT, HW), BF16),
            pltpu.VMEM((2 * FEAT, FEAT), BF16),
            pltpu.VMEM((HEADS, TOK, FEAT), BF16),
            pltpu.VMEM((TOK, D), F32),
            pltpu.VMEM((FEAT, GROUP), BF16),
            pltpu.VMEM((HEADS, TOK, FEAT), F32),
            pltpu.VMEM((TOK, TOK), F32),
            pltpu.VMEM((D, TOK), F32),
            pltpu.VMEM((N_SEQ, 2, TOK), F32),
            pltpu.VMEM((2, N_SEQ, 2, TOK), F32),
            dma((3,)), dma((NX - 1,)), dma((NX - 1,)), dma((NZ - 1,)), dma((NZ - 1,)),
            dma((2, N_SEQ)), dma((2, N_SEQ)),
        ],
        compiler_params=pltpu.CompilerParams(collective_id=0, has_side_effects=True, vmem_limit_bytes=40 << 20),
        name="flow",
    )(
        latents[0], voxel_coords[0], owner_map.reshape(1, TOK), step_time, modulation[0, 0], in_proj, norm_gain,
        head_proj, border_blocks[0, 0], table, qkv_proj, out_proj,
    )
    owned, decoded = pl.pallas_call(
        conv_kernel,
        out_shape=(jax.ShapeDtypeStruct((LAT, SLOTS), F32), jax.ShapeDtypeStruct((FINE, OUT_DEV), BF16)),
        in_specs=vmem(5),
        out_specs=tuple(vmem(2)),
        scratch_shapes=[
            pltpu.VMEM((2 * SLOTS, DEC), BF16),
            pltpu.VMEM((2, DEC, 2 * TOK), BF16),
            pltpu.VMEM((FINE, TOK), F32),
            pltpu.VMEM((FINE, TOK), F32),
        ],
        compiler_params=pltpu.CompilerParams(vmem_limit_bytes=40 << 20),
        name="conv",
    )(gathered, borders, kernel_map[0, 0], decoder_projection, conv_weight)
    return owned[None, None], decoded[None, None]


def solution(mesh):
    placed = (
        P("asset", None, "seq"),
        P("asset", None, "seq"),
        P("asset", "seq", None),
        P("asset"),
        P("asset", "pair", None, None),
        P(),
        P(),
        P(),
        P(),
        P(),
        P(),
        P("asset", "seq", None, None),
        P("asset", "seq", None, None),
        P(None, None, "pair"),
    )
    return jax.shard_map(
        per_device,
        mesh=mesh,
        in_specs=placed,
        out_specs=(P("asset", "seq", None, None), P("asset", "seq", None, "pair")),
        check_vma=False,
    )
```

```python
import math

import jax
import jax.numpy as jnp
import numpy as np
from jax import lax
from jax.experimental import pallas as pl
from jax.experimental.pallas import tpu as pltpu
from jax.sharding import PartitionSpec as P

D = 1024
HEADS = 8
HEAD = 64
LAT = 8
DEC = 768
KOFF = 27
BLK = 16
RES = 64
TOK = 128
CAP = 8
SLOTS = 256
HALO = 128
FINE = 1024
HW = 512
NX = 4
NZ = 8
N_SEQ = 32
OUT_DEV = 96
GROUP = NX * TOK
FEAT = 256
EPSILON = 1e-06
GUIDANCE = 3.0
LOG2E = 1.4426950408889634
HI = lax.Precision.HIGHEST
F32 = jnp.float32
BF16 = jnp.bfloat16


def centred_position_table():
    freqs = D // 6
    omegas = np.exp(-math.log(10000.0) * (np.arange(freqs) / freqs))
    angles = np.arange(RES)[:, None] * omegas[None, :]
    halves = np.concatenate([np.sin(angles), np.cos(angles)], axis=1)
    table = np.zeros((3 * RES, D))
    for axis in range(3):
        table[axis * RES : (axis + 1) * RES, axis * 2 * freqs : (axis + 1) * 2 * freqs] = halves
    return (table - table.mean(axis=1, keepdims=True)).astype(np.float32)


def split(values):
    high = values.astype(BF16)
    return high, (values - high.astype(F32)).astype(BF16)


def mm(a, b):
    return lax.dot_general(a, b, (((1,), (0,)), ((), ())), preferred_element_type=F32)


def mm_nt(a, b):
    return lax.dot_general(a, b, (((1,), (1,)), ((), ())), preferred_element_type=F32)


def mm3(a, b, product=mm):
    a_high, a_low = split(a)
    b_high, b_low = split(b)
    return product(a_high, b_high) + (product(a_high, b_low) + product(a_low, b_high))


def exact(a, b):
    return jnp.dot(a, b, precision=HI, preferred_element_type=F32)


def iota(shape, dim):
    return lax.broadcasted_iota(jnp.int32, shape, dim)


def one_hots(rows, width):
    ids = iota((RES, width), 0).astype(F32)
    return [jnp.where(ids == rows[c : c + 1, :], 1.0, 0.0) for c in range(3)]


def flow_kernel(
    lat_hbm, coord_hbm, own_hbm, step_ref, mod_hbm, inp_hbm, gain_hbm, head_hbm, bb_hbm, tabh_hbm, tabl_hbm, wqkv_hbm,
    wout_hbm,
    x_ref, nb_ref,
    lat_ref, coord_ref, own_ref, mod_ref, inp_ref, gain_ref, head_ref, bb_ref, tabh, tabl, wqkv, wout,
    gath, stage, bkt, bv_high, bv_low, umat, hid_ref, ft_ref, p_ref, acc, vel_ref, vel_in, sendbuf, rbuf,
    lsem, gs_sem, gr_sem, ps_sem, pr_sem, as_sem, ar_sem,
):
    me = lax.axis_index("seq")
    pair = lax.axis_index("pair")
    other = 1 - pair
    x_me = me // NZ
    z_me = me % NZ
    mesh_ids = pl.DeviceIdType.MESH

    barrier = pltpu.get_barrier_semaphore()
    for shift in range(1, N_SEQ):
        pl.semaphore_signal(barrier, inc=1, device_id={"seq": (me + shift) % N_SEQ}, device_id_type=mesh_ids)
    pl.semaphore_signal(barrier, inc=1, device_id={"pair": other}, device_id_type=mesh_ids)

    loads = [
        pltpu.make_async_copy(source, target, lsem.at[number])
        for number, (source, target) in enumerate((
            (lat_hbm, lat_ref), (coord_hbm, coord_ref), (own_hbm, own_ref), (mod_hbm, mod_ref), (inp_hbm, inp_ref),
            (gain_hbm, gain_ref), (head_hbm, head_ref), (bb_hbm, bb_ref), (tabh_hbm, tabh), (tabl_hbm, tabl),
            (wqkv_hbm, wqkv), (wout_hbm, wout)))
    ]
    for load in loads:
        load.start()
    for load in loads[:10]:
        load.wait()

    lat = lat_ref[...]
    stage[...] = jnp.zeros((16, TOK), F32)
    stage[0:8, :] = lat
    for axis in range(3):
        stage[8 + axis : 9 + axis, :] = coord_ref[axis].astype(F32)
    stage[11:12, 0:8] = bb_ref[0:1, :].astype(F32)
    stage[11:12, 8:16] = bb_ref[1:2, :].astype(F32)
    lat_high = lat.astype(BF16).astype(F32)
    zero8 = jnp.zeros((8, TOK), F32)
    own_feat = jnp.concatenate(
        one_hots(stage[8:11, :], TOK) + [lat_high, zero8, lat - lat_high, jnp.zeros((40, TOK), F32)], axis=0)
    own_feat = own_feat.T.astype(BF16)
    inp = inp_ref[...]
    inp = inp - jnp.mean(inp, axis=1, keepdims=True)
    inp_rows = jnp.concatenate([inp, jnp.zeros((8, D), F32), inp, jnp.zeros((40, D), F32)], axis=0)
    rows_high, rows_low = split(inp_rows)
    basis_high = jnp.concatenate([tabh[...], rows_high], axis=0)
    basis_low = jnp.concatenate([tabl[...], rows_low], axis=0)
    hidden = mm(own_feat, basis_high) + mm(own_feat, basis_low)
    hid_ref[...] = hidden
    center = hidden - jnp.mean(hidden, axis=1, keepdims=True)
    variance = jnp.mean(center * center, axis=1, keepdims=True)
    std = jnp.broadcast_to(jnp.sqrt(variance + EPSILON), (TOK, TOK)).T[0:1, :]
    std_high = std.astype(BF16).astype(F32)
    stage[12:13, :] = std_high
    stage[13:14, :] = std - std_high
    gath[me] = stage[...].astype(BF16)

    def g_copy(shift):
        return pltpu.make_async_remote_copy(
            src_ref=gath.at[me], dst_ref=gath.at[me], send_sem=gs_sem.at[shift], recv_sem=gr_sem.at[shift],
            device_id={"seq": (me + shift) % N_SEQ}, device_id_type=mesh_ids)

    pl.semaphore_wait(barrier, N_SEQ)
    for shift in range(1, N_SEQ):
        g_copy(shift).start()

    scale1 = 1.0 + mod_ref[1]
    normed = (center * lax.rsqrt(variance + EPSILON) * scale1 + mod_ref[0]).astype(BF16)
    shift_rows = jnp.where(iota((8, D), 0) < 2, jnp.broadcast_to(mod_ref[0], (8, D)), 0.0)
    scaled = jnp.concatenate(
        [(tabh[...].astype(F32) + tabl[...].astype(F32)) * scale1, inp * scale1, shift_rows, jnp.zeros((48, D), F32)],
        axis=0)
    scaled_high, scaled_low = split(scaled)
    loads[10].wait()
    keys_of = mm(scaled_high, wqkv[:, HW : 2 * HW]) + mm(scaled_low, wqkv[:, HW : 2 * HW])
    keys_t_high, keys_t_low = split(keys_of.T)
    bkt[...] = keys_t_high
    queries = mm(normed, wqkv[:, 0:HW])
    sq_high, sq_low = split(queries * queries)
    per_head = jnp.where(iota((HW, HW), 0) // HEAD == iota((HW, HW), 1) // HEAD, 1.0 / HEAD, 0.0).astype(BF16)
    mean_sq = mm(sq_high, per_head) + mm(sq_low, per_head)
    queries = (queries * lax.rsqrt(mean_sq + EPSILON) * gain_ref[0:1, :]).astype(BF16).astype(F32)
    queries = queries * (gain_ref[1:2, :] * (HEAD ** (-0.5) * LOG2E))
    first_half = iota((TOK, 2 * HEAD), 1) < HEAD
    for two in range(HEADS // 2):
        columns = slice(two * 2 * HEAD, (two + 1) * 2 * HEAD)
        both = queries[:, columns]
        mine = jnp.concatenate([jnp.where(first_half, both, 0.0), jnp.where(first_half, 0.0, both)], axis=0)
        q_high, q_low = split(mine)
        k_high, k_low = keys_t_high[columns, :], keys_t_low[columns, :]
        umat[two * 256 : (two + 1) * 256, :] = (
            mm(q_high, k_high) + (mm(q_high, k_low) + mm(q_low, k_high))).astype(BF16)
    values_of = mm(scaled_high, wqkv[:, 2 * HW : 3 * HW]) + mm(scaled_low, wqkv[:, 2 * HW : 3 * HW])
    bv_high[...], bv_low[...] = split(values_of)
    acc[...] = jnp.zeros((HEADS * TOK, FEAT), F32)

    def one_group(step, carry):
        back = jnp.where(step % 2 == 0, (NZ - step // 2) % NZ, (step + 1) // 2)
        z_from = (z_me + NZ - back) % NZ
        parts = []
        for x_back in range(NX):
            source = ((x_me + NX - x_back) % NX) * NZ + z_from
            shift = (me + N_SEQ - source) % N_SEQ

            @pl.when((step > 0) | (x_back > 0))
            def _():
                pltpu.make_async_remote_copy(
                    src_ref=gath.at[source], dst_ref=gath.at[source], send_sem=gs_sem.at[shift],
                    recv_sem=gr_sem.at[shift], device_id={"seq": me}, device_id_type=mesh_ids).wait_recv()

        for x_back in range(NX):
            source = ((x_me + NX - x_back) % NX) * NZ + z_from
            parts.append(gath[source].astype(F32))
        rows = jnp.concatenate(parts, axis=1)
        std = rows[12:13, :] + rows[13:14, :]
        log_std = LOG2E * jnp.log(std)
        which = iota((8, GROUP), 0)
        std_rows = jnp.where(which == 0, rows[12:13, :], jnp.where(which == 1, rows[13:14, :], 0.0))
        ft_ref[...] = jnp.concatenate(
            one_hots(rows[8:11, :], GROUP) + [rows[0:8, :], std_rows, jnp.zeros((48, GROUP), F32)], axis=0).astype(BF16)
        keys = mm(bkt[...], ft_ref[...])
        scores = mm(umat[...], ft_ref[...])
        for head in range(HEADS):
            keys_h = keys[head * HEAD : (head + 1) * HEAD, :]
            mean_h = jnp.sum(keys_h * keys_h, axis=0, keepdims=True) * (1.0 / HEAD)
            inv = lax.rsqrt(mean_h + EPSILON * (std * std))
            p_ref[head * TOK : (head + 1) * TOK, :] = jnp.exp2(
                scores[head * TOK : (head + 1) * TOK, :] * inv - log_std).astype(BF16)
        acc[...] += mm_nt(p_ref[...], ft_ref[...])
        return carry

    lax.fori_loop(0, NZ, one_group, 0)

    loads[11].wait()
    lane = iota((TOK, FEAT), 1)
    pieces = []
    for two in range(HEADS // 2):
        columns = slice(two * 2 * HEAD, (two + 1) * 2 * HEAD)
        halves = []
        for odd in range(2):
            head = 2 * two + odd
            total = acc[head * TOK : (head + 1) * TOK, :]
            denom = jnp.sum(jnp.where((lane == 200) | (lane == 201), total, 0.0), axis=1, keepdims=True)
            halves.append(total * (1.0 / denom))
        t_high, t_low = split(jnp.concatenate(halves, axis=0))
        found = mm(t_high, bv_high[:, columns]) + (mm(t_low, bv_high[:, columns]) + mm(t_high, bv_low[:, columns]))
        pieces.append(jnp.where(first_half, found[0:TOK, :], found[TOK : 2 * TOK, :]))
    attended = jnp.concatenate(pieces, axis=1).astype(BF16)
    hidden = hid_ref[...] + mod_ref[2] * mm(attended, wout[...])
    center = hidden - jnp.mean(hidden, axis=1, keepdims=True)
    variance = jnp.mean(center * center, axis=1, keepdims=True)
    final = center * lax.rsqrt(variance + EPSILON) * (1.0 + mod_ref[4]) + mod_ref[3]
    vel_ref[...] = mm3(head_ref[...], final, mm_nt)
    swap = pltpu.make_async_remote_copy(
        src_ref=vel_ref, dst_ref=vel_in, send_sem=ps_sem, recv_sem=pr_sem,
        device_id={"pair": other}, device_id_type=mesh_ids)
    swap.start()

    own_rows = jnp.broadcast_to(own_ref[...], (TOK, TOK)).astype(F32)
    own_cols = own_rows.T
    earlier = (own_rows == own_cols) & (iota((TOK, TOK), 0) < iota((TOK, TOK), 1))
    rank = jnp.sum(jnp.where(earlier, 1.0, 0.0), axis=0, keepdims=True)
    ranked = rank == ((iota((TOK, TOK), 0) // LAT) % CAP).astype(F32)
    own96 = jnp.broadcast_to(own_ref[...], (3 * N_SEQ, TOK))
    owner = iota((3 * N_SEQ, TOK), 0)
    owner = jnp.where(owner < N_SEQ, owner, jnp.where(owner < 2 * N_SEQ, owner - N_SEQ - 1, owner - 2 * N_SEQ + 1))
    dispatch = jnp.where(own96 == owner, 1.0, 0.0).astype(BF16)
    swap.wait()
    mine, theirs = vel_ref[...], vel_in[...]
    is_cond = pair == 0
    cond = jnp.where(is_cond, mine, theirs)
    uncond = jnp.where(is_cond, theirs, mine)
    clean = lat_ref[...] - step_ref[0] * (uncond + GUIDANCE * (cond - uncond))
    wide = jnp.where(ranked, jnp.concatenate([clean] * (TOK // LAT), axis=0), 0.0)
    wide_high, wide_low = split(wide)
    packed = mm_nt(dispatch, wide_high) + mm_nt(dispatch, wide_low)
    sendbuf[:, 0, :] = jnp.where(
        iota((N_SEQ, TOK), 1) < LAT * CAP, packed[0:N_SEQ, :], packed[N_SEQ : 2 * N_SEQ, :])
    sendbuf[:, 1, :] = packed[2 * N_SEQ :, :]

    keep = pltpu.make_async_copy(sendbuf.at[me], rbuf.at[me], lsem.at[12])
    keep.start()
    for shift in range(1, N_SEQ):
        dest = (me + shift) % N_SEQ
        pltpu.make_async_remote_copy(
            src_ref=sendbuf.at[dest], dst_ref=rbuf.at[me], send_sem=as_sem.at[shift], recv_sem=ar_sem.at[shift],
            device_id={"seq": dest}, device_id_type=mesh_ids).start()

    lower = jnp.maximum(me - 1, 0)
    upper = jnp.minimum(me + 1, N_SEQ - 1)
    nb_ref[0:1, :] = gath[lower].astype(F32)[11:12, :]
    nb_ref[1:2, :] = gath[upper].astype(F32)[11:12, :]
    nb_ref[2:8, :] = jnp.zeros((6, TOK), F32)
    for shift in range(1, N_SEQ):
        g_copy(shift).wait_send()
    keep.wait()
    for shift in range(1, N_SEQ):
        source = (me + N_SEQ - shift) % N_SEQ
        pltpu.make_async_remote_copy(
            src_ref=sendbuf.at[source], dst_ref=rbuf.at[source], send_sem=as_sem.at[shift], recv_sem=ar_sem.at[shift],
            device_id={"seq": me}, device_id_type=mesh_ids).wait()
    x_ref[...] = rbuf[...]


TRIPLE = 3
PARTS = KOFF // TRIPLE


def conv_kernel(
    x_ref, nb_ref, km_hbm, dproj_hbm, wt_hbm, owned_ref, dec_ref, km_ref, dproj_ref, wt, feats, prod_a, prod_b, acc, lsem
):
    loads = [
        pltpu.make_async_copy(source, target, lsem.at[number])
        for number, (source, target) in enumerate(((dproj_hbm, dproj_ref), (km_hbm, km_ref), (wt_hbm, wt)))
    ]
    for load in loads:
        load.start()
    x0 = x_ref[:, 0, :]
    x1 = x_ref[:, 1, :]

    pick = jnp.where(iota((N_SEQ, SLOTS), 1) // CAP == iota((N_SEQ, SLOTS), 0), 1.0, 0.0).astype(BF16)
    x0_high, x0_low = split(x0.T)
    x1_high, x1_low = split(x1)
    spread = mm(x0_high, pick) + mm(x0_low, pick)
    spread = jnp.where(iota((TOK, SLOTS), 1) % CAP == iota((TOK, SLOTS), 0) // LAT, spread, 0.0)
    owned = spread[0:LAT, :]
    for rank in range(1, CAP):
        owned = owned + spread[rank * LAT : (rank + 1) * LAT, :]
    owned_ref[...] = owned

    lane = iota((SLOTS, TOK), 1)
    own_rows = jnp.where(lane // LAT == iota((SLOTS, TOK), 0) // N_SEQ, jnp.concatenate([x0] * CAP, axis=0), 0.0)
    sub = iota((HALO, TOK), 0)
    lane = iota((HALO, TOK), 1)
    parts = [own_rows]
    x0_high, x0_low = split(x0)
    for side, halves in ((0, (x0_high, x0_low)), (1, (x1_high, x1_low))):
        blocks = jnp.broadcast_to(nb_ref[side : side + 1, :], (HALO, TOK))
        first = 8 if side == 0 else 0
        chosen = jnp.sum(jnp.where(lane == sub // BLK + first, blocks, 0.0), axis=1, keepdims=True)
        source = chosen * (BLK // CAP) + ((iota((HALO, 1), 0) % BLK) // CAP).astype(F32)
        pick = jnp.where(iota((HALO, N_SEQ), 1).astype(F32) == source, 1.0, 0.0).astype(BF16)
        rows = mm(pick, halves[0]) + mm(pick, halves[1])
        offset = CAP if side == 0 else 0
        parts.append(jnp.where(lane // LAT == sub % CAP + offset, rows, 0.0))
    latents = jnp.concatenate(parts, axis=0)
    loads[0].wait()
    proj = jnp.concatenate([dproj_ref[...]] * (TOK // LAT), axis=0).T
    value = mm3(proj, latents, mm_nt)
    feats[...] = (value / (1.0 + jnp.exp(-value))).astype(BF16)
    acc[...] = jnp.zeros((OUT_DEV, FINE), F32)
    loads[1].wait()
    loads[2].wait()

    def products(part, target):
        for i in range(TRIPLE):
            target[i] = mm(wt[part * TRIPLE + i], feats[...])

    def gather(part, source):
        for i in range(TRIPLE):
            index = km_ref[part * TRIPLE + i]
            index = jnp.where(index < SLOTS, (index % CAP) * N_SEQ + index // CAP, index)
            for block in range(FINE // TOK):
                columns = slice(block * TOK, (block + 1) * TOK)
                here = index[:, columns]
                spot = jnp.broadcast_to(here % TOK, (OUT_DEV, TOK))
                chunk = jnp.broadcast_to(here // TOK, (OUT_DEV, TOK))
                value = jnp.zeros((OUT_DEV, TOK), F32)
                for c in range(4):
                    found = jnp.take_along_axis(
                        source[i, :, c * TOK : (c + 1) * TOK], spot, axis=1, mode="promise_in_bounds")
                    value = jnp.where(chunk == c, found, value)
                acc[:, columns] += value

    products(0, prod_a)

    def two_parts(i, carry):
        products(2 * i + 1, prod_b)
        gather(2 * i, prod_a)
        products(2 * i + 2, prod_a)
        gather(2 * i + 1, prod_b)
        return carry

    lax.fori_loop(0, PARTS // 2, two_parts, 0)
    gather(PARTS - 1, prod_a)
    dec_ref[...] = acc[...].astype(BF16)


def vmem(count):
    return [pl.BlockSpec(memory_space=pltpu.VMEM)] * count


def hbm(count):
    return [pl.BlockSpec(memory_space=pltpu.HBM)] * count


def per_device(
    latents, voxel_coords, owner_map, step_time, modulation, in_proj, qkv_proj, norm_gain, out_proj, head_proj,
    decoder_projection, border_blocks, kernel_map, conv_weight,
):
    table = centred_position_table()
    table_high = table.astype(jnp.bfloat16)
    table_low = (table - table_high.astype(np.float32)).astype(jnp.bfloat16)
    dma = pltpu.SemaphoreType.DMA
    gathered, borders = pl.pallas_call(
        flow_kernel,
        out_shape=(jax.ShapeDtypeStruct((N_SEQ, 2, TOK), F32), jax.ShapeDtypeStruct((8, TOK), F32)),
        in_specs=hbm(3) + [pl.BlockSpec(memory_space=pltpu.SMEM)] + hbm(9),
        out_specs=tuple(vmem(2)),
        scratch_shapes=[
            pltpu.VMEM((LAT, TOK), F32),
            pltpu.VMEM((3, 1, TOK), jnp.int32),
            pltpu.VMEM((1, TOK), jnp.int32),
            pltpu.VMEM((5, 1, D), F32),
            pltpu.VMEM((LAT, D), F32),
            pltpu.VMEM((2, HW), F32),
            pltpu.VMEM((LAT, D), F32),
            pltpu.VMEM((2, 8), jnp.int32),
            pltpu.VMEM((3 * RES, D), BF16),
            pltpu.VMEM((3 * RES, D), BF16),
            pltpu.VMEM((D, 3 * HW), BF16),
            pltpu.VMEM((HW, D), BF16),
            pltpu.VMEM((N_SEQ, 16, TOK), BF16),
            pltpu.VMEM((16, TOK), F32),
            pltpu.VMEM((HW, FEAT), BF16),
            pltpu.VMEM((FEAT, HW), BF16),
            pltpu.VMEM((FEAT, HW), BF16),
            pltpu.VMEM((HEADS * TOK, FEAT), BF16),
            pltpu.VMEM((TOK, D), F32),
            pltpu.VMEM((FEAT, GROUP), BF16),
            pltpu.VMEM((HEADS * TOK, GROUP), BF16),
            pltpu.VMEM((HEADS * TOK, FEAT), F32),
            pltpu.VMEM((LAT, TOK), F32),
            pltpu.VMEM((LAT, TOK), F32),
            pltpu.VMEM((N_SEQ, 2, TOK), F32),
            pltpu.VMEM((N_SEQ, 2, TOK), F32),
            dma((13,)), dma((N_SEQ,)), dma((N_SEQ,)), dma, dma, dma((N_SEQ,)), dma((N_SEQ,)),
        ],
        compiler_params=pltpu.CompilerParams(collective_id=0, has_side_effects=True, vmem_limit_bytes=67043328),
        name="flow",
    )(
        latents[0], jnp.transpose(voxel_coords, (1, 0, 2)), owner_map.reshape(1, TOK), step_time,
        modulation.reshape(5, 1, D), in_proj, norm_gain, head_proj.T, border_blocks[0, 0], jnp.asarray(table_high),
        jnp.asarray(table_low), qkv_proj, out_proj,
    )
    owned, decoded = pl.pallas_call(
        conv_kernel,
        out_shape=(jax.ShapeDtypeStruct((LAT, SLOTS), F32), jax.ShapeDtypeStruct((OUT_DEV, FINE), BF16)),
        in_specs=vmem(2) + hbm(3),
        out_specs=tuple(vmem(2)),
        scratch_shapes=[
            pltpu.VMEM((KOFF, 1, FINE), jnp.int32),
            pltpu.VMEM((LAT, DEC), F32),
            pltpu.VMEM((KOFF, OUT_DEV, DEC), BF16),
            pltpu.VMEM((DEC, 2 * SLOTS), BF16),
            pltpu.VMEM((TRIPLE, OUT_DEV, 2 * SLOTS), F32),
            pltpu.VMEM((TRIPLE, OUT_DEV, 2 * SLOTS), F32),
            pltpu.VMEM((OUT_DEV, FINE), F32),
            dma((3,)),
        ],
        compiler_params=pltpu.CompilerParams(vmem_limit_bytes=67043328),
        name="conv",
    )(gathered, borders, kernel_map.reshape(KOFF, 1, FINE), decoder_projection, jnp.swapaxes(conv_weight, 1, 2))
    return owned[None, None], decoded.T[None, None]


def solution(mesh):
    placed = (
        P("asset", None, "seq"),
        P("asset", None, "seq"),
        P("asset", "seq", None),
        P("asset"),
        P("asset", "pair", None, None),
        P(),
        P(),
        P(),
        P(),
        P(),
        P(),
        P("asset", "seq", None, None),
        P("asset", "seq", None, None),
        P(None, None, "pair"),
    )
    return jax.shard_map(
        per_device,
        mesh=mesh,
        in_specs=placed,
        out_specs=(P("asset", "seq", None, None), P("asset", "seq", None, "pair")),
        check_vma=False,
    )
```

```python
import math

import jax
import jax.numpy as jnp
import numpy as np
from jax import lax
from jax.experimental import pallas as pl
from jax.experimental.pallas import tpu as pltpu
from jax.sharding import PartitionSpec as P

D = 1024
HEADS = 8
HEAD = 64
LAT = 8
DEC = 768
KOFF = 27
BLK = 16
RES = 64
TOK = 128
CAP = 8
SLOTS = 256
HALO = 128
FINE = 1024
HW = 512
NX = 4
NZ = 8
N_SEQ = 32
OUT_DEV = 96
GROUP = NX * TOK
FEAT = 256
EPSILON = 1e-06
GUIDANCE = 3.0
LOG2E = 1.4426950408889634
HI = lax.Precision.HIGHEST
F32 = jnp.float32
BF16 = jnp.bfloat16


def centred_position_table():
    freqs = D // 6
    omegas = np.exp(-math.log(10000.0) * (np.arange(freqs) / freqs))
    angles = np.arange(RES)[:, None] * omegas[None, :]
    halves = np.concatenate([np.sin(angles), np.cos(angles)], axis=1)
    table = np.zeros((3 * RES, D))
    for axis in range(3):
        table[axis * RES : (axis + 1) * RES, axis * 2 * freqs : (axis + 1) * 2 * freqs] = halves
    return (table - table.mean(axis=1, keepdims=True)).astype(np.float32)


def split(values):
    high = values.astype(BF16)
    return high, (values - high.astype(F32)).astype(BF16)


def mm(a, b):
    return lax.dot_general(a, b, (((1,), (0,)), ((), ())), preferred_element_type=F32)


def mm_nt(a, b):
    return lax.dot_general(a, b, (((1,), (1,)), ((), ())), preferred_element_type=F32)


def mm3(a, b, product=mm):
    a_high, a_low = split(a)
    b_high, b_low = split(b)
    return product(a_high, b_high) + (product(a_high, b_low) + product(a_low, b_high))


def exact(a, b):
    return jnp.dot(a, b, precision=HI, preferred_element_type=F32)


def iota(shape, dim):
    return lax.broadcasted_iota(jnp.int32, shape, dim)


def one_hots(rows, width):
    ids = iota((RES, width), 0).astype(F32)
    return [jnp.where(ids == rows[c : c + 1, :], 1.0, 0.0) for c in range(3)]


def flow_kernel(
    lat_hbm, coord_hbm, own_hbm, step_ref, mod_hbm, inp_hbm, gain_hbm, head_hbm, bb_hbm, tabh_hbm, tabl_hbm, wqkv_hbm,
    wout_hbm,
    x_ref, nb_ref,
    lat_ref, coord_ref, own_ref, mod_ref, inp_ref, gain_ref, head_ref, bb_ref, tabh, tabl, wqkv, wout,
    gath, stage, bkt, bv_high, bv_low, umat, hid_ref, ft_ref, p_ref, acc, vel_ref, vel_in, sendbuf, rbuf,
    lsem, gs_sem, gr_sem, ps_sem, pr_sem, as_sem, ar_sem,
):
    me = lax.axis_index("seq")
    pair = lax.axis_index("pair")
    other = 1 - pair
    x_me = me // NZ
    z_me = me % NZ
    mesh_ids = pl.DeviceIdType.MESH

    barrier = pltpu.get_barrier_semaphore()
    for shift in range(1, N_SEQ):
        pl.semaphore_signal(barrier, inc=1, device_id={"seq": (me + shift) % N_SEQ}, device_id_type=mesh_ids)
    pl.semaphore_signal(barrier, inc=1, device_id={"pair": other}, device_id_type=mesh_ids)

    loads = [
        pltpu.make_async_copy(source, target, lsem.at[number])
        for number, (source, target) in enumerate((
            (lat_hbm, lat_ref), (coord_hbm, coord_ref), (own_hbm, own_ref), (mod_hbm, mod_ref), (inp_hbm, inp_ref),
            (gain_hbm, gain_ref), (head_hbm, head_ref), (bb_hbm, bb_ref), (tabh_hbm, tabh), (tabl_hbm, tabl),
            (wqkv_hbm, wqkv), (wout_hbm, wout)))
    ]
    for load in loads:
        load.start()
    for load in loads[:10]:
        load.wait()

    lat = lat_ref[...]
    stage[...] = jnp.zeros((16, TOK), F32)
    stage[0:8, :] = lat
    for axis in range(3):
        stage[8 + axis : 9 + axis, :] = coord_ref[axis].astype(F32)
    stage[11:12, 0:8] = bb_ref[0:1, :].astype(F32)
    stage[11:12, 8:16] = bb_ref[1:2, :].astype(F32)
    lat_high = lat.astype(BF16).astype(F32)
    zero8 = jnp.zeros((8, TOK), F32)
    own_feat = jnp.concatenate(
        one_hots(stage[8:11, :], TOK) + [lat_high, zero8, lat - lat_high, jnp.zeros((40, TOK), F32)], axis=0)
    own_feat = own_feat.T.astype(BF16)
    inp = inp_ref[...]
    inp = inp - jnp.mean(inp, axis=1, keepdims=True)
    inp_rows = jnp.concatenate([inp, jnp.zeros((8, D), F32), inp, jnp.zeros((40, D), F32)], axis=0)
    rows_high, rows_low = split(inp_rows)
    basis_high = jnp.concatenate([tabh[...], rows_high], axis=0)
    basis_low = jnp.concatenate([tabl[...], rows_low], axis=0)
    hidden = mm(own_feat, basis_high) + mm(own_feat, basis_low)
    hid_ref[...] = hidden
    center = hidden - jnp.mean(hidden, axis=1, keepdims=True)
    variance = jnp.mean(center * center, axis=1, keepdims=True)
    std = jnp.broadcast_to(jnp.sqrt(variance + EPSILON), (TOK, TOK)).T[0:1, :]
    std_high = std.astype(BF16).astype(F32)
    stage[12:13, :] = std_high
    stage[13:14, :] = std - std_high
    gath[me] = stage[...].astype(BF16)

    def g_copy(shift):
        return pltpu.make_async_remote_copy(
            src_ref=gath.at[me], dst_ref=gath.at[me], send_sem=gs_sem.at[shift], recv_sem=gr_sem.at[shift],
            device_id={"seq": (me + shift) % N_SEQ}, device_id_type=mesh_ids)

    pl.semaphore_wait(barrier, N_SEQ)
    for shift in range(1, N_SEQ):
        g_copy(shift).start()

    scale1 = 1.0 + mod_ref[1]
    normed = (center * lax.rsqrt(variance + EPSILON) * scale1 + mod_ref[0]).astype(BF16)
    shift_rows = jnp.where(iota((8, D), 0) < 2, jnp.broadcast_to(mod_ref[0], (8, D)), 0.0)
    scaled = jnp.concatenate(
        [(tabh[...].astype(F32) + tabl[...].astype(F32)) * scale1, inp * scale1, shift_rows, jnp.zeros((48, D), F32)],
        axis=0)
    scaled_high, scaled_low = split(scaled)
    loads[10].wait()
    keys_of = mm(scaled_high, wqkv[:, HW : 2 * HW]) + mm(scaled_low, wqkv[:, HW : 2 * HW])
    keys_t_high, keys_t_low = split(keys_of.T)
    bkt[...] = keys_t_high
    queries = mm(normed, wqkv[:, 0:HW])
    sq_high, sq_low = split(queries * queries)
    per_head = jnp.where(iota((HW, HW), 0) // HEAD == iota((HW, HW), 1) // HEAD, 1.0 / HEAD, 0.0).astype(BF16)
    mean_sq = mm(sq_high, per_head) + mm(sq_low, per_head)
    queries = (queries * lax.rsqrt(mean_sq + EPSILON) * gain_ref[0:1, :]).astype(BF16).astype(F32)
    queries = queries * (gain_ref[1:2, :] * (HEAD ** (-0.5) * LOG2E))
    first_half = iota((TOK, 2 * HEAD), 1) < HEAD
    for two in range(HEADS // 2):
        columns = slice(two * 2 * HEAD, (two + 1) * 2 * HEAD)
        both = queries[:, columns]
        mine = jnp.concatenate([jnp.where(first_half, both, 0.0), jnp.where(first_half, 0.0, both)], axis=0)
        q_high, q_low = split(mine)
        k_high, k_low = keys_t_high[columns, :], keys_t_low[columns, :]
        umat[two * 256 : (two + 1) * 256, :] = (
            mm(q_high, k_high) + (mm(q_high, k_low) + mm(q_low, k_high))).astype(BF16)
    values_of = mm(scaled_high, wqkv[:, 2 * HW : 3 * HW]) + mm(scaled_low, wqkv[:, 2 * HW : 3 * HW])
    bv_high[...], bv_low[...] = split(values_of)
    acc[...] = jnp.zeros((HEADS * TOK, FEAT), F32)

    def one_group(step, carry):
        back = jnp.where(step % 2 == 0, (NZ - step // 2) % NZ, (step + 1) // 2)
        z_from = (z_me + NZ - back) % NZ
        parts = []
        for x_back in range(NX):
            source = ((x_me + NX - x_back) % NX) * NZ + z_from
            shift = (me + N_SEQ - source) % N_SEQ

            @pl.when((step > 0) | (x_back > 0))
            def _():
                pltpu.make_async_remote_copy(
                    src_ref=gath.at[source], dst_ref=gath.at[source], send_sem=gs_sem.at[shift],
                    recv_sem=gr_sem.at[shift], device_id={"seq": me}, device_id_type=mesh_ids).wait_recv()

        for x_back in range(NX):
            source = ((x_me + NX - x_back) % NX) * NZ + z_from
            parts.append(gath[source].astype(F32))
        rows = jnp.concatenate(parts, axis=1)
        std = rows[12:13, :] + rows[13:14, :]
        log_std = LOG2E * jnp.log(std)
        which = iota((8, GROUP), 0)
        std_rows = jnp.where(which == 0, rows[12:13, :], jnp.where(which == 1, rows[13:14, :], 0.0))
        ft_ref[...] = jnp.concatenate(
            one_hots(rows[8:11, :], GROUP) + [rows[0:8, :], std_rows, jnp.zeros((48, GROUP), F32)], axis=0).astype(BF16)
        keys = mm(bkt[...], ft_ref[...])
        scores = mm(umat[...], ft_ref[...])
        for head in range(HEADS):
            keys_h = keys[head * HEAD : (head + 1) * HEAD, :]
            mean_h = jnp.sum(keys_h * keys_h, axis=0, keepdims=True) * (1.0 / HEAD)
            inv = lax.rsqrt(mean_h + EPSILON * (std * std))
            p_ref[head * TOK : (head + 1) * TOK, :] = jnp.exp2(
                scores[head * TOK : (head + 1) * TOK, :] * inv - log_std).astype(BF16)
        acc[...] += mm_nt(p_ref[...], ft_ref[...])
        return carry

    lax.fori_loop(0, NZ, one_group, 0)

    loads[11].wait()
    lane = iota((TOK, FEAT), 1)
    pieces = []
    for two in range(HEADS // 2):
        columns = slice(two * 2 * HEAD, (two + 1) * 2 * HEAD)
        halves = []
        for odd in range(2):
            head = 2 * two + odd
            total = acc[head * TOK : (head + 1) * TOK, :]
            denom = jnp.sum(jnp.where((lane == 200) | (lane == 201), total, 0.0), axis=1, keepdims=True)
            halves.append(total * (1.0 / denom))
        t_high, t_low = split(jnp.concatenate(halves, axis=0))
        found = mm(t_high, bv_high[:, columns]) + (mm(t_low, bv_high[:, columns]) + mm(t_high, bv_low[:, columns]))
        pieces.append(jnp.where(first_half, found[0:TOK, :], found[TOK : 2 * TOK, :]))
    attended = jnp.concatenate(pieces, axis=1).astype(BF16)
    hidden = hid_ref[...] + mod_ref[2] * mm(attended, wout[...])
    center = hidden - jnp.mean(hidden, axis=1, keepdims=True)
    variance = jnp.mean(center * center, axis=1, keepdims=True)
    final = center * lax.rsqrt(variance + EPSILON) * (1.0 + mod_ref[4]) + mod_ref[3]
    vel_ref[...] = mm3(head_ref[...], final, mm_nt)
    swap = pltpu.make_async_remote_copy(
        src_ref=vel_ref, dst_ref=vel_in, send_sem=ps_sem, recv_sem=pr_sem,
        device_id={"pair": other}, device_id_type=mesh_ids)
    swap.start()

    own_rows = jnp.broadcast_to(own_ref[...], (TOK, TOK)).astype(F32)
    own_cols = own_rows.T
    earlier = (own_rows == own_cols) & (iota((TOK, TOK), 0) < iota((TOK, TOK), 1))
    rank = jnp.sum(jnp.where(earlier, 1.0, 0.0), axis=0, keepdims=True)
    ranked = rank == ((iota((TOK, TOK), 0) // LAT) % CAP).astype(F32)
    own96 = jnp.broadcast_to(own_ref[...], (3 * N_SEQ, TOK))
    owner = iota((3 * N_SEQ, TOK), 0)
    owner = jnp.where(owner < N_SEQ, owner, jnp.where(owner < 2 * N_SEQ, owner - N_SEQ - 1, owner - 2 * N_SEQ + 1))
    dispatch = jnp.where(own96 == owner, 1.0, 0.0).astype(BF16)
    swap.wait()
    mine, theirs = vel_ref[...], vel_in[...]
    is_cond = pair == 0
    cond = jnp.where(is_cond, mine, theirs)
    uncond = jnp.where(is_cond, theirs, mine)
    clean = lat_ref[...] - step_ref[0] * (uncond + GUIDANCE * (cond - uncond))
    wide = jnp.where(ranked, jnp.concatenate([clean] * (TOK // LAT), axis=0), 0.0)
    wide_high, wide_low = split(wide)
    packed = mm_nt(dispatch, wide_high) + mm_nt(dispatch, wide_low)
    sendbuf[:, 0, :] = jnp.where(
        iota((N_SEQ, TOK), 1) < LAT * CAP, packed[0:N_SEQ, :], packed[N_SEQ : 2 * N_SEQ, :])
    sendbuf[:, 1, :] = packed[2 * N_SEQ :, :]

    keep = pltpu.make_async_copy(sendbuf.at[me], rbuf.at[me], lsem.at[12])
    keep.start()
    for shift in range(1, N_SEQ):
        dest = (me + shift) % N_SEQ
        pltpu.make_async_remote_copy(
            src_ref=sendbuf.at[dest], dst_ref=rbuf.at[me], send_sem=as_sem.at[shift], recv_sem=ar_sem.at[shift],
            device_id={"seq": dest}, device_id_type=mesh_ids).start()

    lower = jnp.maximum(me - 1, 0)
    upper = jnp.minimum(me + 1, N_SEQ - 1)
    nb_ref[0:1, :] = gath[lower].astype(F32)[11:12, :]
    nb_ref[1:2, :] = gath[upper].astype(F32)[11:12, :]
    nb_ref[2:8, :] = jnp.zeros((6, TOK), F32)
    for shift in range(1, N_SEQ):
        g_copy(shift).wait_send()
    keep.wait()
    for shift in range(1, N_SEQ):
        source = (me + N_SEQ - shift) % N_SEQ
        pltpu.make_async_remote_copy(
            src_ref=sendbuf.at[source], dst_ref=rbuf.at[source], send_sem=as_sem.at[shift], recv_sem=ar_sem.at[shift],
            device_id={"seq": me}, device_id_type=mesh_ids).wait()
    x_ref[...] = rbuf[...]


TRIPLE = 3
PARTS = KOFF // TRIPLE
BLOCKS = FINE // TOK
SHARED = 0


def conv_kernel(
    x_ref, nb_ref, km_hbm, dproj_hbm, wt_hbm, owned_ref, dec_ref, km_ref, dproj_ref, wt, feats, spot_ref, chunk_ref,
    near_ref, far_ref, prod_a, prod_b, acc_x, acc_m, lsem
):
    loads = [
        pltpu.make_async_copy(source, target, lsem.at[number])
        for number, (source, target) in enumerate(((dproj_hbm, dproj_ref), (km_hbm, km_ref), (wt_hbm, wt)))
    ]
    for load in loads:
        load.start()
    x0 = x_ref[:, 0, :]
    x1 = x_ref[:, 1, :]

    pick = jnp.where(iota((N_SEQ, SLOTS), 1) // CAP == iota((N_SEQ, SLOTS), 0), 1.0, 0.0).astype(BF16)
    xt_high, xt_low = split(x0.T)
    spread = mm(xt_high, pick) + mm(xt_low, pick)
    spread = jnp.where(iota((TOK, SLOTS), 1) % CAP == iota((TOK, SLOTS), 0) // LAT, spread, 0.0)
    owned = spread[0:LAT, :]
    for rank in range(1, CAP):
        owned = owned + spread[rank * LAT : (rank + 1) * LAT, :]
    owned_ref[...] = owned

    lane = iota((SLOTS, TOK), 1)
    own_rows = jnp.where(lane // LAT == iota((SLOTS, TOK), 0) // N_SEQ, jnp.concatenate([x0] * CAP, axis=0), 0.0)
    sub = iota((HALO, TOK), 0)
    lane = iota((HALO, TOK), 1)
    parts = [own_rows]
    for side, x_side in ((0, x0), (1, x1)):
        blocks = jnp.broadcast_to(nb_ref[side : side + 1, :], (HALO, TOK))
        first = 8 if side == 0 else 0
        chosen = jnp.sum(jnp.where(lane == sub // BLK + first, blocks, 0.0), axis=1, keepdims=True)
        source = chosen * (BLK // CAP) + ((iota((HALO, 1), 0) % BLK) // CAP).astype(F32)
        pick = jnp.where(iota((HALO, N_SEQ), 1).astype(F32) == source, 1.0, 0.0).astype(BF16)
        x_high, x_low = split(x_side)
        rows = mm(pick, x_high) + mm(pick, x_low)
        offset = CAP if side == 0 else 0
        parts.append(jnp.where(lane // LAT == sub % CAP + offset, rows, 0.0))
    l_high, l_low = split(jnp.concatenate(parts, axis=0))
    loads[0].wait()
    p_high, p_low = split(dproj_ref[...])
    p_high = jnp.concatenate([p_high.astype(F32)] * (TOK // LAT), axis=0).astype(BF16)
    p_low = jnp.concatenate([p_low.astype(F32)] * (TOK // LAT), axis=0).astype(BF16)
    value = mm(jnp.concatenate([l_high, l_low], axis=1), jnp.concatenate([p_high, p_high], axis=0)) + mm(l_high, p_low)
    half = value * 0.5
    feats[...] = (half * jnp.tanh(half) + half).astype(BF16)
    acc_x[...] = jnp.zeros((OUT_DEV, FINE), F32)
    acc_m[...] = jnp.zeros((OUT_DEV, FINE), F32)
    loads[1].wait()
    index = km_ref[...]
    index = jnp.where(index < SLOTS, ((index & (CAP - 1)) << 5) + (index >> 3), index)
    spot_ref[...] = index & (TOK - 1)
    chunk_ref[...] = index >> 7
    near_ref[...] = jnp.minimum(index, 300).astype(F32)
    far_ref[...] = jnp.where(index >= SLOTS, jnp.minimum(index - SLOTS, 300), 300).astype(F32)
    loads[2].wait()

    def product(part, half, target):
        rows = pl.ds(pl.multiple_of(part * (TRIPLE * OUT_DEV), TRIPLE * OUT_DEV), TRIPLE * OUT_DEV)
        table = slice(half * SLOTS, (half + 1) * SLOTS)
        target[:, table] = mm_nt(wt[rows, :], feats[table, :])

    def by_gather(number, source, block):
        columns = slice(block * TOK, (block + 1) * TOK)
        spot = jnp.broadcast_to(spot_ref[number, block : block + 1, :], (OUT_DEV, TOK))
        chunk = jnp.broadcast_to(chunk_ref[number, block : block + 1, :], (OUT_DEV, TOK))
        value = jnp.zeros((OUT_DEV, TOK), F32)
        for c in range(4):
            found = jnp.take_along_axis(source[:, c * TOK : (c + 1) * TOK], spot, axis=1, mode="promise_in_bounds")
            value = jnp.where(chunk == c, found, value)
        acc_x[:, columns] += value

    first_ids = iota((16, TOK), 0).astype(F32).astype(BF16)

    def hot_rows(number, blocks):
        columns = []
        for block in blocks:
            rows = []
            for which in (near_ref, far_ref):
                row = jnp.broadcast_to(which[number, block : block + 1, :], (16, TOK)).astype(BF16) - first_ids
                for j in range(SLOTS // 16):
                    rows.append(jnp.where(row == jnp.bfloat16(16 * j), jnp.bfloat16(1), jnp.bfloat16(0)))
            columns.append(jnp.concatenate(rows, axis=0))
        return jnp.concatenate(columns, axis=1)

    def pick_rows(part, source, target):
        first = part * TRIPLE
        for quarter in range(4):
            blocks = (2 * quarter, 2 * quarter + 1)
            columns = slice(quarter * 2 * TOK, (quarter + 1) * 2 * TOK)
            if target is not None and quarter % 2 == 0:
                product(part + 1, quarter // 2, target)
            found = mm(source[2 * OUT_DEV :, :].astype(BF16), hot_rows(first + 2, blocks))
            if quarter >= SHARED:
                found += mm(source[OUT_DEV : 2 * OUT_DEV, :].astype(BF16), hot_rows(first + 1, blocks))
            acc_m[:, columns] += found
            for block in blocks:
                by_gather(first, source.at[0:OUT_DEV], block)
                if quarter < SHARED:
                    by_gather(first + 1, source.at[OUT_DEV : 2 * OUT_DEV], block)

    for half in range(2):
        product(0, half, prod_a)

    def two_parts(i, carry):
        pick_rows(2 * i, prod_a, prod_b)
        pick_rows(2 * i + 1, prod_b, prod_a)
        return carry

    lax.fori_loop(0, PARTS // 2, two_parts, 0)
    pick_rows(PARTS - 1, prod_a, None)
    dec_ref[...] = (acc_x[...] + acc_m[...]).astype(BF16)


def vmem(count):
    return [pl.BlockSpec(memory_space=pltpu.VMEM)] * count


def hbm(count):
    return [pl.BlockSpec(memory_space=pltpu.HBM)] * count


def per_device(
    latents, voxel_coords, owner_map, step_time, modulation, in_proj, qkv_proj, norm_gain, out_proj, head_proj,
    decoder_projection, border_blocks, kernel_map, conv_weight,
):
    table = centred_position_table()
    table_high = table.astype(jnp.bfloat16)
    table_low = (table - table_high.astype(np.float32)).astype(jnp.bfloat16)
    dma = pltpu.SemaphoreType.DMA
    gathered, borders = pl.pallas_call(
        flow_kernel,
        out_shape=(jax.ShapeDtypeStruct((N_SEQ, 2, TOK), F32), jax.ShapeDtypeStruct((8, TOK), F32)),
        in_specs=hbm(3) + [pl.BlockSpec(memory_space=pltpu.SMEM)] + hbm(9),
        out_specs=tuple(vmem(2)),
        scratch_shapes=[
            pltpu.VMEM((LAT, TOK), F32),
            pltpu.VMEM((3, 1, TOK), jnp.int32),
            pltpu.VMEM((1, TOK), jnp.int32),
            pltpu.VMEM((5, 1, D), F32),
            pltpu.VMEM((LAT, D), F32),
            pltpu.VMEM((2, HW), F32),
            pltpu.VMEM((LAT, D), F32),
            pltpu.VMEM((2, 8), jnp.int32),
            pltpu.VMEM((3 * RES, D), BF16),
            pltpu.VMEM((3 * RES, D), BF16),
            pltpu.VMEM((D, 3 * HW), BF16),
            pltpu.VMEM((HW, D), BF16),
            pltpu.VMEM((N_SEQ, 16, TOK), BF16),
            pltpu.VMEM((16, TOK), F32),
            pltpu.VMEM((HW, FEAT), BF16),
            pltpu.VMEM((FEAT, HW), BF16),
            pltpu.VMEM((FEAT, HW), BF16),
            pltpu.VMEM((HEADS * TOK, FEAT), BF16),
            pltpu.VMEM((TOK, D), F32),
            pltpu.VMEM((FEAT, GROUP), BF16),
            pltpu.VMEM((HEADS * TOK, GROUP), BF16),
            pltpu.VMEM((HEADS * TOK, FEAT), F32),
            pltpu.VMEM((LAT, TOK), F32),
            pltpu.VMEM((LAT, TOK), F32),
            pltpu.VMEM((N_SEQ, 2, TOK), F32),
            pltpu.VMEM((N_SEQ, 2, TOK), F32),
            dma((13,)), dma((N_SEQ,)), dma((N_SEQ,)), dma, dma, dma((N_SEQ,)), dma((N_SEQ,)),
        ],
        compiler_params=pltpu.CompilerParams(collective_id=0, has_side_effects=True, vmem_limit_bytes=67043328),
        name="flow",
    )(
        latents[0], jnp.transpose(voxel_coords, (1, 0, 2)), owner_map.reshape(1, TOK), step_time,
        modulation.reshape(5, 1, D), in_proj, norm_gain, head_proj.T, border_blocks[0, 0], jnp.asarray(table_high),
        jnp.asarray(table_low), qkv_proj, out_proj,
    )
    owned, decoded = pl.pallas_call(
        conv_kernel,
        out_shape=(jax.ShapeDtypeStruct((LAT, SLOTS), F32), jax.ShapeDtypeStruct((OUT_DEV, FINE), BF16)),
        in_specs=vmem(2) + hbm(3),
        out_specs=tuple(vmem(2)),
        scratch_shapes=[
            pltpu.VMEM((KOFF, BLOCKS, TOK), jnp.int32),
            pltpu.VMEM((LAT, DEC), F32),
            pltpu.VMEM((KOFF * OUT_DEV, DEC), BF16),
            pltpu.VMEM((2 * SLOTS, DEC), BF16),
            pltpu.VMEM((KOFF, BLOCKS, TOK), jnp.int32),
            pltpu.VMEM((KOFF, BLOCKS, TOK), jnp.int32),
            pltpu.VMEM((KOFF, BLOCKS, TOK), F32),
            pltpu.VMEM((KOFF, BLOCKS, TOK), F32),
            pltpu.VMEM((TRIPLE * OUT_DEV, 2 * SLOTS), F32),
            pltpu.VMEM((TRIPLE * OUT_DEV, 2 * SLOTS), F32),
            pltpu.VMEM((OUT_DEV, FINE), F32),
            pltpu.VMEM((OUT_DEV, FINE), F32),
            dma((3,)),
        ],
        compiler_params=pltpu.CompilerParams(vmem_limit_bytes=67043328),
        name="conv",
    )(gathered, borders, kernel_map.reshape(KOFF, BLOCKS, TOK), decoder_projection, jnp.swapaxes(conv_weight, 1, 2).reshape(KOFF * OUT_DEV, DEC))
    return owned[None, None], decoded.T[None, None]


def solution(mesh):
    placed = (
        P("asset", None, "seq"),
        P("asset", None, "seq"),
        P("asset", "seq", None),
        P("asset"),
        P("asset", "pair", None, None),
        P(),
        P(),
        P(),
        P(),
        P(),
        P(),
        P("asset", "seq", None, None),
        P("asset", "seq", None, None),
        P(None, None, "pair"),
    )
    return jax.shard_map(
        per_device,
        mesh=mesh,
        in_specs=placed,
        out_specs=(P("asset", "seq", None, None), P("asset", "seq", None, "pair")),
        check_vma=False,
    )
```

```python
import math

import jax
import jax.numpy as jnp
import numpy as np
from jax import lax
from jax.experimental import pallas as pl
from jax.experimental.pallas import tpu as pltpu
from jax.sharding import PartitionSpec as P

D = 1024
HEADS = 8
HEAD = 64
LAT = 8
DEC = 768
KOFF = 27
BLK = 16
RES = 64
TOK = 128
CAP = 8
SLOTS = 256
HALO = 128
FINE = 1024
HW = 512
NX = 4
NZ = 8
N_SEQ = 32
OUT_DEV = 96
GROUP = NX * TOK
FEAT = 256
EPSILON = 1e-06
GUIDANCE = 3.0
LOG2E = 1.4426950408889634
F32 = jnp.float32
BF16 = jnp.bfloat16


def centred_position_table():
    freqs = D // 6
    omegas = np.exp(-math.log(10000.0) * (np.arange(freqs) / freqs))
    angles = np.arange(RES)[:, None] * omegas[None, :]
    halves = np.concatenate([np.sin(angles), np.cos(angles)], axis=1)
    table = np.zeros((3 * RES, D))
    for axis in range(3):
        table[axis * RES : (axis + 1) * RES, axis * 2 * freqs : (axis + 1) * 2 * freqs] = halves
    return (table - table.mean(axis=1, keepdims=True)).astype(np.float32)


def split(values):
    high = values.astype(BF16)
    return high, (values - high.astype(F32)).astype(BF16)


def mm(a, b):
    return lax.dot_general(a, b, (((1,), (0,)), ((), ())), preferred_element_type=F32)


def mm_nt(a, b):
    return lax.dot_general(a, b, (((1,), (1,)), ((), ())), preferred_element_type=F32)


def iota(shape, dim):
    return lax.broadcasted_iota(jnp.int32, shape, dim)


def one_hots(rows, width):
    ids = iota((RES, width), 0).astype(F32)
    return [jnp.where(ids == rows[c : c + 1, :], 1.0, 0.0) for c in range(3)]


def flow_kernel(
    lat_hbm, coord_hbm, own_hbm, step_ref, mod_hbm, inp_hbm, gain_hbm, head_hbm, bb_hbm, tabh_hbm, tabl_hbm, wqkv_hbm,
    wout_hbm, wt_hbm, km_hbm,
    x_ref, nb_ref, wt_ref, spot_ref, chunk_ref, near_ref, far_ref,
    lat_ref, coord_ref, own_ref, mod_ref, inp_ref, gain_ref, head_ref, bb_ref, tabh, tabl, wqkv, wout, km_ref,
    gath, stage, scaled, bkt, bv, umat, hid_ref, ft_ref, fs_ref, p_ref, acc, hp_high, hp_low, hp_const, vel_ref, vel_in,
    sendbuf, rbuf,
    lsem, gs_sem, gr_sem, ps_sem, pr_sem, as_sem, ar_sem,
):
    me = lax.axis_index("seq")
    pair = lax.axis_index("pair")
    other = 1 - pair
    x_me = me // NZ
    z_me = me % NZ
    mesh_ids = pl.DeviceIdType.MESH

    loads = [
        pltpu.make_async_copy(source, target, lsem.at[number])
        for number, (source, target) in enumerate((
            (lat_hbm, lat_ref), (coord_hbm, coord_ref), (own_hbm, own_ref), (mod_hbm, mod_ref), (inp_hbm, inp_ref),
            (gain_hbm, gain_ref), (head_hbm, head_ref), (bb_hbm, bb_ref), (tabh_hbm, tabh), (tabl_hbm, tabl),
            (wqkv_hbm, wqkv), (wout_hbm, wout), (km_hbm, km_ref), (wt_hbm, wt_ref)))
    ]
    for load in loads[:12]:
        load.start()

    barrier = pltpu.get_barrier_semaphore()
    for shift in range(1, N_SEQ):
        pl.semaphore_signal(barrier, inc=1, device_id={"seq": (me + shift) % N_SEQ}, device_id_type=mesh_ids)
    pl.semaphore_signal(barrier, inc=1, device_id={"pair": other}, device_id_type=mesh_ids)
    for load in loads[:10]:
        load.wait()

    lat = lat_ref[...]
    stage[...] = jnp.zeros((16, TOK), F32)
    stage[0:8, :] = lat
    for axis in range(3):
        stage[8 + axis : 9 + axis, :] = coord_ref[axis].astype(F32)
    stage[11:12, 0:8] = bb_ref[0:1, :].astype(F32)
    stage[11:12, 8:16] = bb_ref[1:2, :].astype(F32)
    lat_high = lat.astype(BF16).astype(F32)
    zero8 = jnp.zeros((8, TOK), F32)
    own_feat = jnp.concatenate(
        one_hots(stage[8:11, :], TOK) + [lat_high, zero8, lat - lat_high, jnp.zeros((40, TOK), F32)], axis=0)
    own_feat = own_feat.T.astype(BF16)
    inp = inp_ref[...]
    inp = inp - jnp.mean(inp, axis=1, keepdims=True)
    inp_rows = jnp.concatenate([inp, jnp.zeros((8, D), F32), inp, jnp.zeros((40, D), F32)], axis=0)
    rows_high, rows_low = split(inp_rows)
    basis_high = jnp.concatenate([tabh[...], rows_high], axis=0)
    basis_low = jnp.concatenate([tabl[...], rows_low], axis=0)
    hidden = mm(own_feat, basis_high) + mm(own_feat, basis_low)
    hid_ref[...] = hidden
    center = hidden - jnp.mean(hidden, axis=1, keepdims=True)
    variance = jnp.mean(center * center, axis=1, keepdims=True)
    std = jnp.broadcast_to(jnp.sqrt(variance + EPSILON), (TOK, TOK)).T[0:1, :]
    std_high = std.astype(BF16).astype(F32)
    stage[12:13, :] = std_high
    stage[13:14, :] = std - std_high
    gath[me] = stage[...].astype(BF16)

    def g_copy(shift):
        return pltpu.make_async_remote_copy(
            src_ref=gath.at[me], dst_ref=gath.at[me], send_sem=gs_sem.at[shift], recv_sem=gr_sem.at[shift],
            device_id={"seq": (me + shift) % N_SEQ}, device_id_type=mesh_ids)

    pl.semaphore_wait(barrier, N_SEQ)
    for shift in range(1, N_SEQ):
        g_copy(shift).start()

    scale1 = 1.0 + mod_ref[1]
    normed = (center * lax.rsqrt(variance + EPSILON) * scale1 + mod_ref[0]).astype(BF16)
    for axis in range(3):
        rows = slice(axis * RES, (axis + 1) * RES)
        scaled[rows, :] = ((tabh[rows, :].astype(F32) + tabl[rows, :].astype(F32)) * scale1).astype(BF16)
    shift_rows = jnp.where(iota((8, D), 0) < 2, jnp.broadcast_to(mod_ref[0], (8, D)), 0.0)
    scaled[3 * RES :, :] = jnp.concatenate([inp * scale1, shift_rows, jnp.zeros((48, D), F32)], axis=0).astype(BF16)
    loads[10].wait()
    queries = mm(normed, wqkv[:, 0:HW])
    per_head = jnp.where(iota((HW, HW), 0) // HEAD == iota((HW, HW), 1) // HEAD, 1.0 / HEAD, 0.0).astype(BF16)
    mean_sq = mm((queries * queries).astype(BF16), per_head)
    queries = queries * lax.rsqrt(mean_sq + EPSILON) * (
        gain_ref[0:1, :] * gain_ref[1:2, :] * (HEAD ** (-0.5) * LOG2E))
    bkt[...] = mm(scaled[...], wqkv[:, HW : 2 * HW]).T.astype(BF16)
    first_half = iota((TOK, 2 * HEAD), 1) < HEAD
    for two in range(HEADS // 2):
        columns = slice(two * 2 * HEAD, (two + 1) * 2 * HEAD)
        both = queries[:, columns]
        mine = jnp.concatenate([jnp.where(first_half, both, 0.0), jnp.where(first_half, 0.0, both)], axis=0)
        umat[two * 256 : (two + 1) * 256, :] = mm(mine.astype(BF16), bkt[columns, :]).astype(BF16)
    bv[...] = mm(scaled[...], wqkv[:, 2 * HW : 3 * HW]).astype(BF16)
    head_scaled = head_ref[...] * (1.0 + mod_ref[4])
    hp_high[...], hp_low[...] = split(head_scaled)
    hp_const[...] = jnp.broadcast_to(jnp.sum(head_ref[...] * mod_ref[3], axis=1, keepdims=True), (LAT, TOK))
    acc[...] = jnp.zeros((HEADS * TOK, FEAT), F32)
    loads[12].start()
    loads[13].start()

    def arrived(z_back, first):
        sources = []
        z_from = (z_me + NZ - z_back) % NZ
        for x_back in range(NX):
            source = ((x_me + NX - x_back) % NX) * NZ + z_from
            shift = (me + N_SEQ - source) % N_SEQ
            sources.append(source)

            def wait():
                pltpu.make_async_remote_copy(
                    src_ref=gath.at[source], dst_ref=gath.at[source], send_sem=gs_sem.at[shift],
                    recv_sem=gr_sem.at[shift], device_id={"seq": me}, device_id_type=mesh_ids).wait_recv()

            if x_back == 0 and first is not None:
                pl.when(first)(wait)
            else:
                wait()
        return sources

    def one_group(step, carry):
        sources = arrived((NZ - step) % NZ, step > 0) + arrived(step + 1, None)
        rows = jnp.concatenate([gath[source].astype(F32) for source in sources], axis=1)
        std_high, std_low = rows[12:13, :], rows[13:14, :]
        std = std_high + std_low
        inv_std = 1.0 / std
        which = iota((8, 2 * GROUP), 0)
        ids = iota((RES, 2 * GROUP), 0).astype(F32)
        for c in range(3):
            hit = ids == rows[8 + c : 9 + c, :]
            ft_ref[c * RES : (c + 1) * RES, :] = jnp.where(hit, 1.0, 0.0).astype(BF16)
            fs_ref[c * RES : (c + 1) * RES, :] = jnp.where(hit, inv_std, 0.0).astype(BF16)
        std_rows = jnp.where(which == 0, std_high, jnp.where(which == 1, std_low, 0.0))
        pad = jnp.zeros((48, 2 * GROUP), F32)
        ft_ref[3 * RES :, :] = jnp.concatenate([rows[0:8, :], std_rows, pad], axis=0).astype(BF16)
        fs_ref[3 * RES :, :] = jnp.concatenate(
            [rows[0:8, :] * inv_std, jnp.where(which == 0, 1.0, 0.0), pad], axis=0).astype(BF16)
        keys = mm(bkt[...], ft_ref[...])
        scores = mm(umat[...], ft_ref[...])
        for head in range(HEADS):
            keys_h = keys[head * HEAD : (head + 1) * HEAD, :]
            mean_h = jnp.sum(keys_h * keys_h, axis=0, keepdims=True) * (1.0 / HEAD)
            inv = lax.rsqrt(mean_h + EPSILON * (std * std))
            p_ref[head * TOK : (head + 1) * TOK, :] = jnp.exp2(scores[head * TOK : (head + 1) * TOK, :] * inv).astype(BF16)
        acc[...] += mm_nt(p_ref[...], fs_ref[...])
        return carry

    lax.fori_loop(0, NZ // 2, one_group, 0)

    loads[11].wait()
    lane = iota((TOK, FEAT), 1)
    pieces = []
    for two in range(HEADS // 2):
        columns = slice(two * 2 * HEAD, (two + 1) * 2 * HEAD)
        halves = []
        for odd in range(2):
            head = 2 * two + odd
            total = acc[head * TOK : (head + 1) * TOK, :]
            denom = jnp.sum(jnp.where(lane == 200, total, 0.0), axis=1, keepdims=True)
            halves.append((total * (1.0 / denom)).astype(BF16))
        found = mm(jnp.concatenate(halves, axis=0), bv[:, columns])
        pieces.append(jnp.where(first_half, found[0:TOK, :], found[TOK : 2 * TOK, :]))
    attended = jnp.concatenate(pieces, axis=1).astype(BF16)
    width = 256
    total = jnp.zeros((TOK, 1), F32)
    for part in range(D // width):
        columns = slice(part * width, (part + 1) * width)
        piece = hid_ref[:, columns] + mod_ref[2][:, columns] * mm(attended, wout[:, columns])
        hid_ref[:, columns] = piece
        total = total + jnp.sum(piece, axis=1, keepdims=True)
    mean = total * (1.0 / D)
    square = jnp.zeros((TOK, 1), F32)
    velocity = jnp.zeros((LAT, TOK), F32)
    for part in range(D // width):
        columns = slice(part * width, (part + 1) * width)
        center = hid_ref[:, columns] - mean
        square = square + jnp.sum(center * center, axis=1, keepdims=True)
        c_high, c_low = split(center)
        velocity = velocity + (mm_nt(hp_high[:, columns], c_high)
                               + (mm_nt(hp_high[:, columns], c_low) + mm_nt(hp_low[:, columns], c_high)))
    inv_dev = jnp.broadcast_to(lax.rsqrt(square * (1.0 / D) + EPSILON), (TOK, TOK)).T[0:1, :]
    vel_ref[...] = velocity * inv_dev + hp_const[...]
    swap = pltpu.make_async_remote_copy(
        src_ref=vel_ref, dst_ref=vel_in, send_sem=ps_sem, recv_sem=pr_sem,
        device_id={"pair": other}, device_id_type=mesh_ids)
    swap.start()

    own_rows = jnp.broadcast_to(own_ref[...], (TOK, TOK)).astype(F32)
    own_cols = own_rows.T
    earlier = (own_rows == own_cols) & (iota((TOK, TOK), 0) < iota((TOK, TOK), 1))
    rank = jnp.sum(jnp.where(earlier, 1.0, 0.0), axis=0, keepdims=True)
    ranked = rank == ((iota((TOK, TOK), 0) // LAT) % CAP).astype(F32)
    own96 = jnp.broadcast_to(own_ref[...], (3 * N_SEQ, TOK))
    owner = iota((3 * N_SEQ, TOK), 0)
    owner = jnp.where(owner < N_SEQ, owner, jnp.where(owner < 2 * N_SEQ, owner - N_SEQ - 1, owner - 2 * N_SEQ + 1))
    dispatch = jnp.where(own96 == owner, 1.0, 0.0).astype(BF16)
    for shift in range(1, N_SEQ):
        g_copy(shift).wait_send()
    swap.wait()
    mine, theirs = vel_ref[...], vel_in[...]
    is_cond = pair == 0
    cond = jnp.where(is_cond, mine, theirs)
    uncond = jnp.where(is_cond, theirs, mine)
    clean = lat_ref[...] - step_ref[0] * (uncond + GUIDANCE * (cond - uncond))
    wide = jnp.where(ranked, jnp.concatenate([clean] * (TOK // LAT), axis=0), 0.0)
    wide_high, wide_low = split(wide)
    packed = mm_nt(dispatch, wide_high) + mm_nt(dispatch, wide_low)
    sendbuf[:, 0, :] = jnp.where(
        iota((N_SEQ, TOK), 1) < LAT * CAP, packed[0:N_SEQ, :], packed[N_SEQ : 2 * N_SEQ, :])
    sendbuf[:, 1, :] = packed[2 * N_SEQ :, :]

    for shift in range(1, N_SEQ):
        dest = (me + shift) % N_SEQ
        pltpu.make_async_remote_copy(
            src_ref=sendbuf.at[dest], dst_ref=rbuf.at[me], send_sem=as_sem.at[shift], recv_sem=ar_sem.at[shift],
            device_id={"seq": dest}, device_id_type=mesh_ids).start()
    keep = pltpu.make_async_copy(sendbuf.at[me], rbuf.at[me], lsem.at[14])
    keep.start()

    lower = jnp.maximum(me - 1, 0)
    upper = jnp.minimum(me + 1, N_SEQ - 1)
    nb_ref[0:1, :] = gath[lower].astype(F32)[11:12, :]
    nb_ref[1:2, :] = gath[upper].astype(F32)[11:12, :]
    nb_ref[2:8, :] = jnp.zeros((6, TOK), F32)
    loads[12].wait()
    index = km_ref[...]
    index = jnp.where(index < SLOTS, ((index & (CAP - 1)) << 5) + (index >> 3), index)
    spot_ref[...] = index & (TOK - 1)
    chunk_ref[...] = index >> 7
    near_ref[...] = jnp.minimum(index, 300).astype(F32)
    far_ref[...] = jnp.where(index >= SLOTS, jnp.minimum(index - SLOTS, 300), 300).astype(F32)
    loads[13].wait()
    keep.wait()
    for shift in range(1, N_SEQ):
        source = (me + N_SEQ - shift) % N_SEQ
        pltpu.make_async_remote_copy(
            src_ref=sendbuf.at[source], dst_ref=rbuf.at[source], send_sem=as_sem.at[shift], recv_sem=ar_sem.at[shift],
            device_id={"seq": me}, device_id_type=mesh_ids).wait()
    x_ref[...] = rbuf[...]


TRIPLE = 3
PARTS = KOFF // TRIPLE
BLOCKS = FINE // TOK
SHARED = 0


def conv_kernel(
    x_ref, nb_ref, wt, spot_ref, chunk_ref, near_ref, far_ref, dproj_hbm, owned_ref, dec_ref, dproj_ref, feats, prod_a,
    prod_b, acc_x, acc_m, lsem
):
    load = pltpu.make_async_copy(dproj_hbm, dproj_ref, lsem)
    load.start()
    x0 = x_ref[:, 0, :]
    x1 = x_ref[:, 1, :]

    pick = jnp.where(iota((N_SEQ, SLOTS), 1) // CAP == iota((N_SEQ, SLOTS), 0), 1.0, 0.0).astype(BF16)
    xt_high, xt_low = split(x0.T)
    spread = mm(xt_high, pick) + mm(xt_low, pick)
    spread = jnp.where(iota((TOK, SLOTS), 1) % CAP == iota((TOK, SLOTS), 0) // LAT, spread, 0.0)
    owned = spread[0:LAT, :]
    for rank in range(1, CAP):
        owned = owned + spread[rank * LAT : (rank + 1) * LAT, :]
    owned_ref[...] = owned

    lane = iota((SLOTS, TOK), 1)
    own_rows = jnp.where(lane // LAT == iota((SLOTS, TOK), 0) // N_SEQ, jnp.concatenate([x0] * CAP, axis=0), 0.0)
    sub = iota((HALO, TOK), 0)
    lane = iota((HALO, TOK), 1)
    parts = [own_rows]
    for side, x_side in ((0, x0), (1, x1)):
        blocks = jnp.broadcast_to(nb_ref[side : side + 1, :], (HALO, TOK))
        first = 8 if side == 0 else 0
        chosen = jnp.sum(jnp.where(lane == sub // BLK + first, blocks, 0.0), axis=1, keepdims=True)
        source = chosen * (BLK // CAP) + ((iota((HALO, 1), 0) % BLK) // CAP).astype(F32)
        pick = jnp.where(iota((HALO, N_SEQ), 1).astype(F32) == source, 1.0, 0.0).astype(BF16)
        x_high, x_low = split(x_side)
        rows = mm(pick, x_high) + mm(pick, x_low)
        offset = CAP if side == 0 else 0
        parts.append(jnp.where(lane // LAT == sub % CAP + offset, rows, 0.0))
    l_high, l_low = split(jnp.concatenate(parts, axis=0))
    load.wait()
    p_high, p_low = split(dproj_ref[...])
    p_high = jnp.concatenate([p_high.astype(F32)] * (TOK // LAT), axis=0).astype(BF16)
    p_low = jnp.concatenate([p_low.astype(F32)] * (TOK // LAT), axis=0).astype(BF16)
    value = mm(jnp.concatenate([l_high, l_low], axis=1), jnp.concatenate([p_high, p_high], axis=0)) + mm(l_high, p_low)
    half = value * 0.5
    feats[...] = (half * jnp.tanh(half) + half).astype(BF16)
    acc_x[...] = jnp.zeros((OUT_DEV, FINE), F32)
    acc_m[...] = jnp.zeros((OUT_DEV, FINE), F32)

    def product(part, half, target):
        rows = pl.ds(pl.multiple_of(part * (TRIPLE * OUT_DEV), TRIPLE * OUT_DEV), TRIPLE * OUT_DEV)
        table = slice(half * SLOTS, (half + 1) * SLOTS)
        target[:, table] = mm_nt(wt[rows, :], feats[table, :])

    def by_gather(number, source, block):
        columns = slice(block * TOK, (block + 1) * TOK)
        spot = jnp.broadcast_to(spot_ref[number, block : block + 1, :], (OUT_DEV, TOK))
        chunk = jnp.broadcast_to(chunk_ref[number, block : block + 1, :], (OUT_DEV, TOK))
        value = jnp.zeros((OUT_DEV, TOK), F32)
        for c in range(4):
            found = jnp.take_along_axis(source[:, c * TOK : (c + 1) * TOK], spot, axis=1, mode="promise_in_bounds")
            value = jnp.where(chunk == c, found, value)
        acc_x[:, columns] += value

    first_ids = iota((16, TOK), 0).astype(F32).astype(BF16)

    def hot_rows(number, blocks):
        columns = []
        for block in blocks:
            rows = []
            for which in (near_ref, far_ref):
                row = jnp.broadcast_to(which[number, block : block + 1, :], (16, TOK)).astype(BF16) - first_ids
                for j in range(SLOTS // 16):
                    rows.append(jnp.where(row == jnp.bfloat16(16 * j), jnp.bfloat16(1), jnp.bfloat16(0)))
            columns.append(jnp.concatenate(rows, axis=0))
        return jnp.concatenate(columns, axis=1)

    def pick_rows(part, source, target):
        first = part * TRIPLE
        for quarter in range(4):
            blocks = (2 * quarter, 2 * quarter + 1)
            columns = slice(quarter * 2 * TOK, (quarter + 1) * 2 * TOK)
            if target is not None and quarter % 2 == 0:
                product(part + 1, quarter // 2, target)
            found = mm(source[2 * OUT_DEV :, :].astype(BF16), hot_rows(first + 2, blocks))
            if quarter >= SHARED:
                found += mm(source[OUT_DEV : 2 * OUT_DEV, :].astype(BF16), hot_rows(first + 1, blocks))
            acc_m[:, columns] += found
            for block in blocks:
                by_gather(first, source.at[0:OUT_DEV], block)
                if quarter < SHARED:
                    by_gather(first + 1, source.at[OUT_DEV : 2 * OUT_DEV], block)

    for half in range(2):
        product(0, half, prod_a)

    def two_parts(i, carry):
        pick_rows(2 * i, prod_a, prod_b)
        pick_rows(2 * i + 1, prod_b, prod_a)
        return carry

    lax.fori_loop(0, PARTS // 2, two_parts, 0)
    pick_rows(PARTS - 1, prod_a, None)
    dec_ref[...] = (acc_x[...] + acc_m[...]).astype(BF16)


def vmem(count):
    return [pl.BlockSpec(memory_space=pltpu.VMEM)] * count


def in_hbm(*arrays):
    return [pltpu.with_memory_space_constraint(array, pltpu.HBM) for array in arrays]


def hbm(count):
    return [pl.BlockSpec(memory_space=pltpu.HBM)] * count


def per_device(
    latents, voxel_coords, owner_map, step_time, modulation, in_proj, qkv_proj, norm_gain, out_proj, head_proj,
    decoder_projection, border_blocks, kernel_map, conv_weight,
):
    table = centred_position_table()
    table_high = table.astype(jnp.bfloat16)
    table_low = (table - table_high.astype(np.float32)).astype(jnp.bfloat16)
    dma = pltpu.SemaphoreType.DMA
    conv_table = jax.ShapeDtypeStruct((KOFF, BLOCKS, TOK), jnp.int32)
    conv_row = jax.ShapeDtypeStruct((KOFF, BLOCKS, TOK), F32)
    handed = pl.pallas_call(
        flow_kernel,
        out_shape=(
            jax.ShapeDtypeStruct((N_SEQ, 2, TOK), F32), jax.ShapeDtypeStruct((8, TOK), F32),
            jax.ShapeDtypeStruct((KOFF * OUT_DEV, DEC), BF16), conv_table, conv_table, conv_row, conv_row),
        in_specs=hbm(3) + [pl.BlockSpec(memory_space=pltpu.SMEM)] + hbm(11),
        out_specs=tuple(vmem(7)),
        scratch_shapes=[
            pltpu.VMEM((LAT, TOK), F32),
            pltpu.VMEM((3, 1, TOK), jnp.int32),
            pltpu.VMEM((1, TOK), jnp.int32),
            pltpu.VMEM((5, 1, D), F32),
            pltpu.VMEM((LAT, D), F32),
            pltpu.VMEM((2, HW), F32),
            pltpu.VMEM((LAT, D), F32),
            pltpu.VMEM((2, 8), jnp.int32),
            pltpu.VMEM((3 * RES, D), BF16),
            pltpu.VMEM((3 * RES, D), BF16),
            pltpu.VMEM((D, 3 * HW), BF16),
            pltpu.VMEM((HW, D), BF16),
            pltpu.VMEM((KOFF, BLOCKS, TOK), jnp.int32),
            pltpu.VMEM((N_SEQ, 16, TOK), BF16),
            pltpu.VMEM((16, TOK), F32),
            pltpu.VMEM((FEAT, D), BF16),
            pltpu.VMEM((HW, FEAT), BF16),
            pltpu.VMEM((FEAT, HW), BF16),
            pltpu.VMEM((HEADS * TOK, FEAT), BF16),
            pltpu.VMEM((TOK, D), F32),
            pltpu.VMEM((FEAT, 2 * GROUP), BF16),
            pltpu.VMEM((FEAT, 2 * GROUP), BF16),
            pltpu.VMEM((HEADS * TOK, 2 * GROUP), BF16),
            pltpu.VMEM((HEADS * TOK, FEAT), F32),
            pltpu.VMEM((LAT, D), BF16),
            pltpu.VMEM((LAT, D), BF16),
            pltpu.VMEM((LAT, TOK), F32),
            pltpu.VMEM((LAT, TOK), F32),
            pltpu.VMEM((LAT, TOK), F32),
            pltpu.VMEM((N_SEQ, 2, TOK), F32),
            pltpu.VMEM((N_SEQ, 2, TOK), F32),
            dma((15,)), dma((N_SEQ,)), dma((N_SEQ,)), dma, dma, dma((N_SEQ,)), dma((N_SEQ,)),
        ],
        compiler_params=pltpu.CompilerParams(collective_id=0, has_side_effects=True, vmem_limit_bytes=40 << 20),
        name="flow",
    )(*in_hbm(
        latents[0], jnp.transpose(voxel_coords, (1, 0, 2)), owner_map.reshape(1, TOK)), step_time, *in_hbm(
        modulation.reshape(5, 1, D), in_proj, norm_gain, head_proj.T, border_blocks[0, 0], jnp.asarray(table_high),
        jnp.asarray(table_low), qkv_proj, out_proj,
        jnp.swapaxes(conv_weight, 1, 2).reshape(KOFF * OUT_DEV, DEC), kernel_map.reshape(KOFF, BLOCKS, TOK)),
    )
    owned, decoded = pl.pallas_call(
        conv_kernel,
        out_shape=(jax.ShapeDtypeStruct((LAT, SLOTS), F32), jax.ShapeDtypeStruct((OUT_DEV, FINE), BF16)),
        in_specs=vmem(7) + hbm(1),
        out_specs=tuple(vmem(2)),
        scratch_shapes=[
            pltpu.VMEM((LAT, DEC), F32),
            pltpu.VMEM((2 * SLOTS, DEC), BF16),
            pltpu.VMEM((TRIPLE * OUT_DEV, 2 * SLOTS), F32),
            pltpu.VMEM((TRIPLE * OUT_DEV, 2 * SLOTS), F32),
            pltpu.VMEM((OUT_DEV, FINE), F32),
            pltpu.VMEM((OUT_DEV, FINE), F32),
            dma,
        ],
        compiler_params=pltpu.CompilerParams(vmem_limit_bytes=40 << 20),
        name="conv",
    )(*handed, *in_hbm(decoder_projection))
    return owned[None, None], decoded.T[None, None]


def solution(mesh):
    placed = (
        P("asset", None, "seq"),
        P("asset", None, "seq"),
        P("asset", "seq", None),
        P("asset"),
        P("asset", "pair", None, None),
        P(),
        P(),
        P(),
        P(),
        P(),
        P(),
        P("asset", "seq", None, None),
        P("asset", "seq", None, None),
        P(None, None, "pair"),
    )
    return jax.shard_map(
        per_device,
        mesh=mesh,
        in_specs=placed,
        out_specs=(P("asset", "seq", None, None), P("asset", "seq", None, "pair")),
        check_vma=False,
    )
```

```python
import math

import jax
import jax.numpy as jnp
import numpy as np
from jax import lax
from jax.experimental import pallas as pl
from jax.experimental.pallas import tpu as pltpu
from jax.sharding import PartitionSpec as P

D = 1024
HEADS = 8
HEAD = 64
LAT = 8
DEC = 768
KOFF = 27
BLK = 16
RES = 64
TOK = 128
CAP = 8
SLOTS = 256
HALO = 128
FINE = 1024
HW = 512
NX = 4
NZ = 8
N_SEQ = 32
OUT_DEV = 96
GROUP = NX * TOK
FEAT = 256
TILES = ((0,), (1, 7), (2, 6), (3, 5), (4,))
EPSILON = 1e-06
GUIDANCE = 3.0
LOG2E = 1.4426950408889634
F32 = jnp.float32
BF16 = jnp.bfloat16


def centred_position_table():
    freqs = D // 6
    omegas = np.exp(-math.log(10000.0) * (np.arange(freqs) / freqs))
    angles = np.arange(RES)[:, None] * omegas[None, :]
    halves = np.concatenate([np.sin(angles), np.cos(angles)], axis=1)
    table = np.zeros((3 * RES, D))
    for axis in range(3):
        table[axis * RES : (axis + 1) * RES, axis * 2 * freqs : (axis + 1) * 2 * freqs] = halves
    return (table - table.mean(axis=1, keepdims=True)).astype(np.float32)


def split(values):
    high = values.astype(BF16)
    return high, (values - high.astype(F32)).astype(BF16)


def mm(a, b):
    return lax.dot_general(a, b, (((1,), (0,)), ((), ())), preferred_element_type=F32)


def mm_nt(a, b):
    return lax.dot_general(a, b, (((1,), (1,)), ((), ())), preferred_element_type=F32)


def iota(shape, dim):
    return lax.broadcasted_iota(jnp.int32, shape, dim)


def one_hots(rows, width):
    ids = iota((RES, width), 0).astype(F32)
    return [jnp.where(ids == rows[c : c + 1, :], 1.0, 0.0) for c in range(3)]


def flow_kernel(
    lat_hbm, coord_hbm, own_hbm, step_ref, mod_hbm, inp_hbm, gain_hbm, head_hbm, bb_hbm, tabh_hbm, tabl_hbm, wqkv_hbm,
    wout_hbm, wt_hbm, km_hbm,
    x_ref, nb_ref, wt_ref, spot_ref, chunk_ref, near_ref, far_ref,
    lat_ref, coord_ref, own_ref, mod_ref, inp_ref, gain_ref, head_ref, bb_ref, tabh, tabl, wqkv, wout, km_ref,
    gath, stage, scaled, bkt, bv, umat, hid_ref, ft_ref, fs_ref, p_ref, acc, hp_high, hp_low, hp_const, vel_ref, vel_in,
    sendbuf, rbuf,
    lsem, gs_sem, gr_sem, ps_sem, pr_sem, as_sem, ar_sem,
):
    me = lax.axis_index("seq")
    pair = lax.axis_index("pair")
    other = 1 - pair
    x_me = me // NZ
    z_me = me % NZ
    mesh_ids = pl.DeviceIdType.MESH

    loads = [
        pltpu.make_async_copy(source, target, lsem.at[number])
        for number, (source, target) in enumerate((
            (lat_hbm, lat_ref), (coord_hbm, coord_ref), (own_hbm, own_ref), (mod_hbm, mod_ref), (inp_hbm, inp_ref),
            (gain_hbm, gain_ref), (head_hbm, head_ref), (bb_hbm, bb_ref), (tabh_hbm, tabh), (tabl_hbm, tabl),
            (wqkv_hbm, wqkv), (wout_hbm, wout), (km_hbm, km_ref), (wt_hbm, wt_ref)))
    ]
    for load in loads[:12]:
        load.start()

    barrier = pltpu.get_barrier_semaphore()
    for shift in range(1, N_SEQ):
        pl.semaphore_signal(barrier, inc=1, device_id={"seq": (me + shift) % N_SEQ}, device_id_type=mesh_ids)
    pl.semaphore_signal(barrier, inc=1, device_id={"pair": other}, device_id_type=mesh_ids)
    for load in loads[:10]:
        load.wait()

    lat = lat_ref[...]
    stage[...] = jnp.zeros((16, TOK), F32)
    stage[0:8, :] = lat
    for axis in range(3):
        stage[8 + axis : 9 + axis, :] = coord_ref[axis].astype(F32)
    stage[11:12, 0:8] = bb_ref[0:1, :].astype(F32)
    stage[11:12, 8:16] = bb_ref[1:2, :].astype(F32)
    lat_high = lat.astype(BF16).astype(F32)
    zero8 = jnp.zeros((8, TOK), F32)
    own_feat = jnp.concatenate(
        one_hots(stage[8:11, :], TOK) + [lat_high, zero8, lat - lat_high, jnp.zeros((40, TOK), F32)], axis=0)
    own_feat = own_feat.T.astype(BF16)
    inp = inp_ref[...]
    inp = inp - jnp.mean(inp, axis=1, keepdims=True)
    inp_rows = jnp.concatenate([inp, jnp.zeros((8, D), F32), inp, jnp.zeros((40, D), F32)], axis=0)
    rows_high, rows_low = split(inp_rows)
    basis_high = jnp.concatenate([tabh[...], rows_high], axis=0)
    basis_low = jnp.concatenate([tabl[...], rows_low], axis=0)
    hidden = mm(own_feat, basis_high) + mm(own_feat, basis_low)
    hid_ref[...] = hidden
    center = hidden - jnp.mean(hidden, axis=1, keepdims=True)
    variance = jnp.mean(center * center, axis=1, keepdims=True)
    std = jnp.broadcast_to(jnp.sqrt(variance + EPSILON), (TOK, TOK)).T[0:1, :]
    std_high = std.astype(BF16).astype(F32)
    stage[12:13, :] = std_high
    stage[13:14, :] = std - std_high
    gath[me] = stage[...].astype(BF16)

    def g_copy(shift):
        return pltpu.make_async_remote_copy(
            src_ref=gath.at[me], dst_ref=gath.at[me], send_sem=gs_sem.at[shift], recv_sem=gr_sem.at[shift],
            device_id={"seq": (me + shift) % N_SEQ}, device_id_type=mesh_ids)

    pl.semaphore_wait(barrier, N_SEQ)
    for shift in range(1, N_SEQ):
        g_copy(shift).start()

    scale1 = 1.0 + mod_ref[1]
    normed = (center * lax.rsqrt(variance + EPSILON) * scale1 + mod_ref[0]).astype(BF16)
    for axis in range(3):
        rows = slice(axis * RES, (axis + 1) * RES)
        scaled[rows, :] = ((tabh[rows, :].astype(F32) + tabl[rows, :].astype(F32)) * scale1).astype(BF16)
    shift_rows = jnp.where(iota((8, D), 0) < 2, jnp.broadcast_to(mod_ref[0], (8, D)), 0.0)
    scaled[3 * RES :, :] = jnp.concatenate([inp * scale1, shift_rows, jnp.zeros((48, D), F32)], axis=0).astype(BF16)
    loads[10].wait()
    queries = mm(normed, wqkv[:, 0:HW])
    per_head = jnp.where(iota((HW, HW), 0) // HEAD == iota((HW, HW), 1) // HEAD, 1.0 / HEAD, 0.0).astype(BF16)
    mean_sq = mm((queries * queries).astype(BF16), per_head)
    queries = queries * lax.rsqrt(mean_sq + EPSILON) * (
        gain_ref[0:1, :] * gain_ref[1:2, :] * (HEAD ** (-0.5) * LOG2E))
    bkt[...] = mm(scaled[...], wqkv[:, HW : 2 * HW]).T.astype(BF16)
    first_half = iota((TOK, 2 * HEAD), 1) < HEAD
    for two in range(HEADS // 2):
        columns = slice(two * 2 * HEAD, (two + 1) * 2 * HEAD)
        both = queries[:, columns]
        mine = jnp.concatenate([jnp.where(first_half, both, 0.0), jnp.where(first_half, 0.0, both)], axis=0)
        umat[two * 256 : (two + 1) * 256, :] = mm(mine.astype(BF16), bkt[columns, :]).astype(BF16)
    bv[...] = mm(scaled[...], wqkv[:, 2 * HW : 3 * HW]).astype(BF16)
    head_scaled = head_ref[...] * (1.0 + mod_ref[4])
    hp_high[...], hp_low[...] = split(head_scaled)
    hp_const[...] = jnp.broadcast_to(jnp.sum(head_ref[...] * mod_ref[3], axis=1, keepdims=True), (LAT, TOK))
    loads[12].start()
    loads[13].start()

    def features(number):
        sources = []
        for z_back in TILES[number]:
            for x_back in range(NX):
                source = ((x_me + NX - x_back) % NX) * NZ + (z_me + NZ - z_back) % NZ
                shift = (me + N_SEQ - source) % N_SEQ
                sources.append(source)
                if x_back > 0 or z_back > 0:
                    pltpu.make_async_remote_copy(
                        src_ref=gath.at[source], dst_ref=gath.at[source], send_sem=gs_sem.at[shift],
                        recv_sem=gr_sem.at[shift], device_id={"seq": me}, device_id_type=mesh_ids).wait_recv()
        width = TOK * len(sources)
        rows = jnp.concatenate([gath[source].astype(F32) for source in sources], axis=1)
        std_high, std_low = rows[12:13, :], rows[13:14, :]
        std = std_high + std_low
        inv_std = 1.0 / std
        which = iota((8, width), 0)
        ids = iota((RES, width), 0).astype(F32)
        ft, fs = ft_ref.at[number % 2], fs_ref.at[number % 2]
        for c in range(3):
            hit = ids == rows[8 + c : 9 + c, :]
            ft[c * RES : (c + 1) * RES, 0:width] = jnp.where(hit, 1.0, 0.0).astype(BF16)
            fs[c * RES : (c + 1) * RES, 0:width] = jnp.where(hit, inv_std, 0.0).astype(BF16)
        std_rows = jnp.where(which == 0, std_high, jnp.where(which == 1, std_low, 0.0))
        pad = jnp.zeros((48, width), F32)
        ft[3 * RES :, 0:width] = jnp.concatenate([rows[0:8, :], std_rows, pad], axis=0).astype(BF16)
        fs[3 * RES :, 0:width] = jnp.concatenate(
            [rows[0:8, :] * inv_std, jnp.where(which == 0, 1.0, 0.0), pad], axis=0).astype(BF16)
        return width, EPSILON * (std * std)

    width, eps_var = features(0)
    for number in range(len(TILES)):
        ft, fs = ft_ref[number % 2, :, 0:width], fs_ref[number % 2, :, 0:width]
        used, used_var = width, eps_var
        if 2 <= number < len(TILES) - 1:
            width, eps_var = features(number + 1)
        keys = mm(bkt[...], ft)
        scores = mm(umat[...], ft)
        for head in range(HEADS):
            keys_h = keys[head * HEAD : (head + 1) * HEAD, :]
            mean_h = jnp.sum(keys_h * keys_h, axis=0, keepdims=True) * (1.0 / HEAD)
            inv = lax.rsqrt(mean_h + used_var)
            p_ref[head * TOK : (head + 1) * TOK, 0:used] = jnp.exp2(
                scores[head * TOK : (head + 1) * TOK, :] * inv).astype(BF16)
        if number < 2:
            width, eps_var = features(number + 1)
        found = mm_nt(p_ref[:, 0:used], fs)
        if number > 0:
            found += acc[...]
        acc[...] = found

    loads[11].wait()
    lane = iota((TOK, FEAT), 1)
    pieces = []
    for two in range(HEADS // 2):
        columns = slice(two * 2 * HEAD, (two + 1) * 2 * HEAD)
        halves = []
        for odd in range(2):
            head = 2 * two + odd
            total = acc[head * TOK : (head + 1) * TOK, :]
            denom = jnp.sum(jnp.where(lane == 200, total, 0.0), axis=1, keepdims=True)
            halves.append((total * (1.0 / denom)).astype(BF16))
        found = mm(jnp.concatenate(halves, axis=0), bv[:, columns])
        pieces.append(jnp.where(first_half, found[0:TOK, :], found[TOK : 2 * TOK, :]))
    attended = jnp.concatenate(pieces, axis=1).astype(BF16)
    width = 256
    total = jnp.zeros((TOK, 1), F32)
    for part in range(D // width):
        columns = slice(part * width, (part + 1) * width)
        piece = hid_ref[:, columns] + mod_ref[2][:, columns] * mm(attended, wout[:, columns])
        hid_ref[:, columns] = piece
        total = total + jnp.sum(piece, axis=1, keepdims=True)
    mean = total * (1.0 / D)
    square = jnp.zeros((TOK, 1), F32)
    velocity = jnp.zeros((LAT, TOK), F32)
    for part in range(D // width):
        columns = slice(part * width, (part + 1) * width)
        center = hid_ref[:, columns] - mean
        square = square + jnp.sum(center * center, axis=1, keepdims=True)
        c_high, c_low = split(center)
        velocity = velocity + (mm_nt(hp_high[:, columns], c_high)
                               + (mm_nt(hp_high[:, columns], c_low) + mm_nt(hp_low[:, columns], c_high)))
    inv_dev = jnp.broadcast_to(lax.rsqrt(square * (1.0 / D) + EPSILON), (TOK, TOK)).T[0:1, :]
    vel_ref[...] = velocity * inv_dev + hp_const[...]
    swap = pltpu.make_async_remote_copy(
        src_ref=vel_ref, dst_ref=vel_in, send_sem=ps_sem, recv_sem=pr_sem,
        device_id={"pair": other}, device_id_type=mesh_ids)
    swap.start()

    own_rows = jnp.broadcast_to(own_ref[...], (TOK, TOK)).astype(F32)
    own_cols = own_rows.T
    earlier = (own_rows == own_cols) & (iota((TOK, TOK), 0) < iota((TOK, TOK), 1))
    rank = jnp.sum(jnp.where(earlier, 1.0, 0.0), axis=0, keepdims=True)
    ranked = rank == ((iota((TOK, TOK), 0) // LAT) % CAP).astype(F32)
    own96 = jnp.broadcast_to(own_ref[...], (3 * N_SEQ, TOK))
    owner = iota((3 * N_SEQ, TOK), 0)
    owner = jnp.where(owner < N_SEQ, owner, jnp.where(owner < 2 * N_SEQ, owner - N_SEQ - 1, owner - 2 * N_SEQ + 1))
    dispatch = jnp.where(own96 == owner, 1.0, 0.0).astype(BF16)
    for shift in range(1, N_SEQ):
        g_copy(shift).wait_send()
    swap.wait()
    mine, theirs = vel_ref[...], vel_in[...]
    is_cond = pair == 0
    cond = jnp.where(is_cond, mine, theirs)
    uncond = jnp.where(is_cond, theirs, mine)
    clean = lat_ref[...] - step_ref[0] * (uncond + GUIDANCE * (cond - uncond))
    wide = jnp.where(ranked, jnp.concatenate([clean] * (TOK // LAT), axis=0), 0.0)
    wide_high, wide_low = split(wide)
    packed = mm_nt(dispatch, wide_high) + mm_nt(dispatch, wide_low)
    sendbuf[:, 0, :] = jnp.where(
        iota((N_SEQ, TOK), 1) < LAT * CAP, packed[0:N_SEQ, :], packed[N_SEQ : 2 * N_SEQ, :])
    sendbuf[:, 1, :] = packed[2 * N_SEQ :, :]

    for shift in range(1, N_SEQ):
        dest = (me + shift) % N_SEQ
        pltpu.make_async_remote_copy(
            src_ref=sendbuf.at[dest], dst_ref=rbuf.at[me], send_sem=as_sem.at[shift], recv_sem=ar_sem.at[shift],
            device_id={"seq": dest}, device_id_type=mesh_ids).start()
    keep = pltpu.make_async_copy(sendbuf.at[me], rbuf.at[me], lsem.at[14])
    keep.start()

    lower = jnp.maximum(me - 1, 0)
    upper = jnp.minimum(me + 1, N_SEQ - 1)
    nb_ref[0:1, :] = gath[lower].astype(F32)[11:12, :]
    nb_ref[1:2, :] = gath[upper].astype(F32)[11:12, :]
    nb_ref[2:8, :] = jnp.zeros((6, TOK), F32)
    loads[12].wait()
    index = km_ref[...]
    index = jnp.where(index < SLOTS, ((index & (CAP - 1)) << 5) + (index >> 3), index)
    spot_ref[...] = index & (TOK - 1)
    chunk_ref[...] = index >> 7
    near_ref[...] = jnp.minimum(index, 300).astype(F32)
    far_ref[...] = jnp.where(index >= SLOTS, jnp.minimum(index - SLOTS, 300), 300).astype(F32)
    loads[13].wait()
    keep.wait()
    for shift in range(1, N_SEQ):
        source = (me + N_SEQ - shift) % N_SEQ
        pltpu.make_async_remote_copy(
            src_ref=sendbuf.at[source], dst_ref=rbuf.at[source], send_sem=as_sem.at[shift], recv_sem=ar_sem.at[shift],
            device_id={"seq": me}, device_id_type=mesh_ids).wait()
    x_ref[...] = rbuf[...]


TRIPLE = 3
PARTS = KOFF // TRIPLE
BLOCKS = FINE // TOK
SHARED = 0


def conv_kernel(
    x_ref, nb_ref, wt, spot_ref, chunk_ref, near_ref, far_ref, dproj_hbm, owned_ref, dec_ref, dproj_ref, feats, prod_a,
    prod_b, acc_x, acc_m, lsem
):
    load = pltpu.make_async_copy(dproj_hbm, dproj_ref, lsem)
    load.start()
    x0 = x_ref[:, 0, :]
    x1 = x_ref[:, 1, :]

    pick = jnp.where(iota((N_SEQ, SLOTS), 1) // CAP == iota((N_SEQ, SLOTS), 0), 1.0, 0.0).astype(BF16)
    xt_high, xt_low = split(x0.T)
    spread = mm(xt_high, pick) + mm(xt_low, pick)
    spread = jnp.where(iota((TOK, SLOTS), 1) % CAP == iota((TOK, SLOTS), 0) // LAT, spread, 0.0)
    owned = spread[0:LAT, :]
    for rank in range(1, CAP):
        owned = owned + spread[rank * LAT : (rank + 1) * LAT, :]
    owned_ref[...] = owned

    lane = iota((SLOTS, TOK), 1)
    own_rows = jnp.where(lane // LAT == iota((SLOTS, TOK), 0) // N_SEQ, jnp.concatenate([x0] * CAP, axis=0), 0.0)
    sub = iota((HALO, TOK), 0)
    lane = iota((HALO, TOK), 1)
    parts = [own_rows]
    for side, x_side in ((0, x0), (1, x1)):
        blocks = jnp.broadcast_to(nb_ref[side : side + 1, :], (HALO, TOK))
        first = 8 if side == 0 else 0
        chosen = jnp.sum(jnp.where(lane == sub // BLK + first, blocks, 0.0), axis=1, keepdims=True)
        source = chosen * (BLK // CAP) + ((iota((HALO, 1), 0) % BLK) // CAP).astype(F32)
        pick = jnp.where(iota((HALO, N_SEQ), 1).astype(F32) == source, 1.0, 0.0).astype(BF16)
        x_high, x_low = split(x_side)
        rows = mm(pick, x_high) + mm(pick, x_low)
        offset = CAP if side == 0 else 0
        parts.append(jnp.where(lane // LAT == sub % CAP + offset, rows, 0.0))
    l_high, l_low = split(jnp.concatenate(parts, axis=0))
    load.wait()
    p_high, p_low = split(dproj_ref[...])
    p_high = jnp.concatenate([p_high.astype(F32)] * (TOK // LAT), axis=0).astype(BF16)
    p_low = jnp.concatenate([p_low.astype(F32)] * (TOK // LAT), axis=0).astype(BF16)
    value = mm(jnp.concatenate([l_high, l_low], axis=1), jnp.concatenate([p_high, p_high], axis=0)) + mm(l_high, p_low)
    half = value * 0.5
    feats[...] = (half * jnp.tanh(half) + half).astype(BF16)
    acc_x[...] = jnp.zeros((OUT_DEV, FINE), F32)
    acc_m[...] = jnp.zeros((OUT_DEV, FINE), F32)

    def product(part, half, target):
        rows = pl.ds(pl.multiple_of(part * (TRIPLE * OUT_DEV), TRIPLE * OUT_DEV), TRIPLE * OUT_DEV)
        table = slice(half * SLOTS, (half + 1) * SLOTS)
        target[:, table] = mm_nt(wt[rows, :], feats[table, :])

    def by_gather(number, source, block):
        columns = slice(block * TOK, (block + 1) * TOK)
        spot = jnp.broadcast_to(spot_ref[number, block : block + 1, :], (OUT_DEV, TOK))
        chunk = jnp.broadcast_to(chunk_ref[number, block : block + 1, :], (OUT_DEV, TOK))
        value = jnp.zeros((OUT_DEV, TOK), F32)
        for c in range(4):
            found = jnp.take_along_axis(source[:, c * TOK : (c + 1) * TOK], spot, axis=1, mode="promise_in_bounds")
            value = jnp.where(chunk == c, found, value)
        acc_x[:, columns] += value

    first_ids = iota((16, TOK), 0).astype(F32).astype(BF16)

    def hot_rows(number, blocks):
        columns = []
        for block in blocks:
            rows = []
            for which in (near_ref, far_ref):
                row = jnp.broadcast_to(which[number, block : block + 1, :], (16, TOK)).astype(BF16) - first_ids
                for j in range(SLOTS // 16):
                    rows.append(jnp.where(row == jnp.bfloat16(16 * j), jnp.bfloat16(1), jnp.bfloat16(0)))
            columns.append(jnp.concatenate(rows, axis=0))
        return jnp.concatenate(columns, axis=1)

    def pick_rows(part, source, target):
        first = part * TRIPLE
        for quarter in range(4):
            blocks = (2 * quarter, 2 * quarter + 1)
            columns = slice(quarter * 2 * TOK, (quarter + 1) * 2 * TOK)
            if target is not None and quarter % 2 == 0:
                product(part + 1, quarter // 2, target)
            found = mm(source[2 * OUT_DEV :, :].astype(BF16), hot_rows(first + 2, blocks))
            if quarter >= SHARED:
                found += mm(source[OUT_DEV : 2 * OUT_DEV, :].astype(BF16), hot_rows(first + 1, blocks))
            acc_m[:, columns] += found
            for block in blocks:
                by_gather(first, source.at[0:OUT_DEV], block)
                if quarter < SHARED:
                    by_gather(first + 1, source.at[OUT_DEV : 2 * OUT_DEV], block)

    for half in range(2):
        product(0, half, prod_a)

    def two_parts(i, carry):
        pick_rows(2 * i, prod_a, prod_b)
        pick_rows(2 * i + 1, prod_b, prod_a)
        return carry

    lax.fori_loop(0, PARTS // 2, two_parts, 0)
    pick_rows(PARTS - 1, prod_a, None)
    dec_ref[...] = (acc_x[...] + acc_m[...]).astype(BF16)


def vmem(count):
    return [pl.BlockSpec(memory_space=pltpu.VMEM)] * count


def in_hbm(*arrays):
    return [pltpu.with_memory_space_constraint(array, pltpu.HBM) for array in arrays]


def hbm(count):
    return [pl.BlockSpec(memory_space=pltpu.HBM)] * count


def per_device(
    latents, voxel_coords, owner_map, step_time, modulation, in_proj, qkv_proj, norm_gain, out_proj, head_proj,
    decoder_projection, border_blocks, kernel_map, conv_weight,
):
    table = centred_position_table()
    table_high = table.astype(jnp.bfloat16)
    table_low = (table - table_high.astype(np.float32)).astype(jnp.bfloat16)
    dma = pltpu.SemaphoreType.DMA
    conv_table = jax.ShapeDtypeStruct((KOFF, BLOCKS, TOK), jnp.int32)
    conv_row = jax.ShapeDtypeStruct((KOFF, BLOCKS, TOK), F32)
    handed = pl.pallas_call(
        flow_kernel,
        out_shape=(
            jax.ShapeDtypeStruct((N_SEQ, 2, TOK), F32), jax.ShapeDtypeStruct((8, TOK), F32),
            jax.ShapeDtypeStruct((KOFF * OUT_DEV, DEC), BF16), conv_table, conv_table, conv_row, conv_row),
        in_specs=hbm(3) + [pl.BlockSpec(memory_space=pltpu.SMEM)] + hbm(11),
        out_specs=tuple(vmem(7)),
        scratch_shapes=[
            pltpu.VMEM((LAT, TOK), F32),
            pltpu.VMEM((3, 1, TOK), jnp.int32),
            pltpu.VMEM((1, TOK), jnp.int32),
            pltpu.VMEM((5, 1, D), F32),
            pltpu.VMEM((LAT, D), F32),
            pltpu.VMEM((2, HW), F32),
            pltpu.VMEM((LAT, D), F32),
            pltpu.VMEM((2, 8), jnp.int32),
            pltpu.VMEM((3 * RES, D), BF16),
            pltpu.VMEM((3 * RES, D), BF16),
            pltpu.VMEM((D, 3 * HW), BF16),
            pltpu.VMEM((HW, D), BF16),
            pltpu.VMEM((KOFF, BLOCKS, TOK), jnp.int32),
            pltpu.VMEM((N_SEQ, 16, TOK), BF16),
            pltpu.VMEM((16, TOK), F32),
            pltpu.VMEM((FEAT, D), BF16),
            pltpu.VMEM((HW, FEAT), BF16),
            pltpu.VMEM((FEAT, HW), BF16),
            pltpu.VMEM((HEADS * TOK, FEAT), BF16),
            pltpu.VMEM((TOK, D), F32),
            pltpu.VMEM((2, FEAT, 2 * GROUP), BF16),
            pltpu.VMEM((2, FEAT, 2 * GROUP), BF16),
            pltpu.VMEM((HEADS * TOK, 2 * GROUP), BF16),
            pltpu.VMEM((HEADS * TOK, FEAT), F32),
            pltpu.VMEM((LAT, D), BF16),
            pltpu.VMEM((LAT, D), BF16),
            pltpu.VMEM((LAT, TOK), F32),
            pltpu.VMEM((LAT, TOK), F32),
            pltpu.VMEM((LAT, TOK), F32),
            pltpu.VMEM((N_SEQ, 2, TOK), F32),
            pltpu.VMEM((N_SEQ, 2, TOK), F32),
            dma((15,)), dma((N_SEQ,)), dma((N_SEQ,)), dma, dma, dma((N_SEQ,)), dma((N_SEQ,)),
        ],
        compiler_params=pltpu.CompilerParams(collective_id=0, has_side_effects=True, vmem_limit_bytes=40 << 20),
        name="flow",
    )(*in_hbm(
        latents[0], jnp.transpose(voxel_coords, (1, 0, 2)), owner_map.reshape(1, TOK)), step_time, *in_hbm(
        modulation.reshape(5, 1, D), in_proj, norm_gain, head_proj.T, border_blocks[0, 0], jnp.asarray(table_high),
        jnp.asarray(table_low), qkv_proj, out_proj,
        jnp.swapaxes(conv_weight, 1, 2).reshape(KOFF * OUT_DEV, DEC), kernel_map.reshape(KOFF, BLOCKS, TOK)),
    )
    owned, decoded = pl.pallas_call(
        conv_kernel,
        out_shape=(jax.ShapeDtypeStruct((LAT, SLOTS), F32), jax.ShapeDtypeStruct((OUT_DEV, FINE), BF16)),
        in_specs=vmem(7) + hbm(1),
        out_specs=tuple(vmem(2)),
        scratch_shapes=[
            pltpu.VMEM((LAT, DEC), F32),
            pltpu.VMEM((2 * SLOTS, DEC), BF16),
            pltpu.VMEM((TRIPLE * OUT_DEV, 2 * SLOTS), F32),
            pltpu.VMEM((TRIPLE * OUT_DEV, 2 * SLOTS), F32),
            pltpu.VMEM((OUT_DEV, FINE), F32),
            pltpu.VMEM((OUT_DEV, FINE), F32),
            dma,
        ],
        compiler_params=pltpu.CompilerParams(vmem_limit_bytes=40 << 20),
        name="conv",
    )(*handed, *in_hbm(decoder_projection))
    return owned[None, None], decoded.T[None, None]


def solution(mesh):
    placed = (
        P("asset", None, "seq"),
        P("asset", None, "seq"),
        P("asset", "seq", None),
        P("asset"),
        P("asset", "pair", None, None),
        P(),
        P(),
        P(),
        P(),
        P(),
        P(),
        P("asset", "seq", None, None),
        P("asset", "seq", None, None),
        P(None, None, "pair"),
    )
    return jax.shard_map(
        per_device,
        mesh=mesh,
        in_specs=placed,
        out_specs=(P("asset", "seq", None, None), P("asset", "seq", None, "pair")),
        check_vma=False,
    )
```

```python
import math

import jax
import jax.numpy as jnp
import numpy as np
from jax import lax
from jax.experimental import pallas as pl
from jax.experimental.pallas import tpu as pltpu
from jax.sharding import PartitionSpec as P

D = 1024
HEADS = 8
HEAD = 64
LAT = 8
DEC = 768
KOFF = 27
BLK = 16
RES = 64
TOK = 128
CAP = 8
SLOTS = 256
HALO = 128
FINE = 1024
HW = 512
NX = 4
NZ = 8
N_SEQ = 32
OUT_DEV = 96
GROUP = NX * TOK
FEAT = 256
TILES = ((0,), (1, 7), (2, 6), (3, 5), (4,))
HOPS = (4, 3)
EPSILON = 1e-06
GUIDANCE = 3.0
LOG2E = 1.4426950408889634
F32 = jnp.float32
BF16 = jnp.bfloat16


def centred_position_table():
    freqs = D // 6
    omegas = np.exp(-math.log(10000.0) * (np.arange(freqs) / freqs))
    angles = np.arange(RES)[:, None] * omegas[None, :]
    halves = np.concatenate([np.sin(angles), np.cos(angles)], axis=1)
    table = np.zeros((3 * RES, D))
    for axis in range(3):
        table[axis * RES : (axis + 1) * RES, axis * 2 * freqs : (axis + 1) * 2 * freqs] = halves
    return (table - table.mean(axis=1, keepdims=True)).astype(np.float32)


def split(values):
    high = values.astype(BF16)
    return high, (values - high.astype(F32)).astype(BF16)


def mm(a, b):
    return lax.dot_general(a, b, (((1,), (0,)), ((), ())), preferred_element_type=F32)


def mm_nt(a, b):
    return lax.dot_general(a, b, (((1,), (1,)), ((), ())), preferred_element_type=F32)


def iota(shape, dim):
    return lax.broadcasted_iota(jnp.int32, shape, dim)


def one_hots(rows, width):
    ids = iota((RES, width), 0).astype(F32)
    return [jnp.where(ids == rows[c : c + 1, :], 1.0, 0.0) for c in range(3)]


def flow_kernel(
    lat_hbm, coord_hbm, own_hbm, step_ref, mod_hbm, inp_hbm, gain_hbm, head_hbm, bb_hbm, tabh_hbm, tabl_hbm, wqkv_hbm,
    wout_hbm, wt_hbm, km_hbm,
    x_ref, nb_ref, wt_ref, spot_ref, chunk_ref, near_ref, far_ref,
    lat_ref, coord_ref, own_ref, mod_ref, inp_ref, gain_ref, head_ref, bb_ref, tabh, tabl, wqkv, wout, km_ref,
    gath, stage, scaled, bkt, bv, umat, hid_ref, ft_ref, fs_ref, p_ref, acc, hp_high, hp_low, hp_const, vel_ref, vel_in,
    sendbuf, rbuf,
    lsem, xs_sem, xr_sem, zs_sem, zr_sem, ps_sem, pr_sem, as_sem, ar_sem,
):
    me = lax.axis_index("seq")
    pair = lax.axis_index("pair")
    other = 1 - pair
    x_me = me // NZ
    z_me = me % NZ
    mesh_ids = pl.DeviceIdType.MESH

    loads = [
        pltpu.make_async_copy(source, target, lsem.at[number])
        for number, (source, target) in enumerate((
            (lat_hbm, lat_ref), (coord_hbm, coord_ref), (own_hbm, own_ref), (mod_hbm, mod_ref), (inp_hbm, inp_ref),
            (gain_hbm, gain_ref), (head_hbm, head_ref), (bb_hbm, bb_ref), (tabh_hbm, tabh), (tabl_hbm, tabl),
            (wqkv_hbm, wqkv), (wout_hbm, wout), (km_hbm, km_ref), (wt_hbm, wt_ref)))
    ]
    for load in loads[:12]:
        load.start()

    barrier = pltpu.get_barrier_semaphore()
    up, down = (z_me + 1) % NZ, (z_me + NZ - 1) % NZ
    near = [((x_me + shift) % NX) * NZ + z_me for shift in range(1, NX)] + [x_me * NZ + up, x_me * NZ + down]
    for peer in near:
        pl.semaphore_signal(barrier, inc=1, device_id={"seq": peer}, device_id_type=mesh_ids)
    pl.semaphore_signal(barrier, inc=1, device_id={"pair": other}, device_id_type=mesh_ids)
    for load in loads[:10]:
        load.wait()

    lat = lat_ref[...]
    stage[...] = jnp.zeros((16, TOK), F32)
    stage[0:8, :] = lat
    for axis in range(3):
        stage[8 + axis : 9 + axis, :] = coord_ref[axis].astype(F32)
    stage[11:12, 0:8] = bb_ref[0:1, :].astype(F32)
    stage[11:12, 8:16] = bb_ref[1:2, :].astype(F32)
    lat_high = lat.astype(BF16).astype(F32)
    zero8 = jnp.zeros((8, TOK), F32)
    own_feat = jnp.concatenate(
        one_hots(stage[8:11, :], TOK) + [lat_high, zero8, lat - lat_high, jnp.zeros((40, TOK), F32)], axis=0)
    own_feat = own_feat.T.astype(BF16)
    inp = inp_ref[...]
    inp = inp - jnp.mean(inp, axis=1, keepdims=True)
    inp_rows = jnp.concatenate([inp, jnp.zeros((8, D), F32), inp, jnp.zeros((40, D), F32)], axis=0)
    rows_high, rows_low = split(inp_rows)
    basis_high = jnp.concatenate([tabh[...], rows_high], axis=0)
    basis_low = jnp.concatenate([tabl[...], rows_low], axis=0)
    hidden = mm(own_feat, basis_high) + mm(own_feat, basis_low)
    hid_ref[...] = hidden
    center = hidden - jnp.mean(hidden, axis=1, keepdims=True)
    variance = jnp.mean(center * center, axis=1, keepdims=True)
    std = jnp.broadcast_to(jnp.sqrt(variance + EPSILON), (TOK, TOK)).T[0:1, :]
    std_high = std.astype(BF16).astype(F32)
    stage[12:13, :] = std_high
    stage[13:14, :] = std - std_high
    gath[z_me, x_me] = stage[...].astype(BF16)

    def x_copy(shift):
        return pltpu.make_async_remote_copy(
            src_ref=gath.at[z_me, x_me], dst_ref=gath.at[z_me, x_me], send_sem=xs_sem.at[shift - 1],
            recv_sem=xr_sem.at[shift - 1], device_id={"seq": near[shift - 1]}, device_id_type=mesh_ids)

    def x_arrival(shift):
        source = (x_me + NX - shift) % NX
        return pltpu.make_async_remote_copy(
            src_ref=gath.at[z_me, source], dst_ref=gath.at[z_me, source], send_sem=xs_sem.at[shift - 1],
            recv_sem=xr_sem.at[shift - 1], device_id={"seq": me}, device_id_type=mesh_ids)

    def z_copy(way, hop, arriving=False):
        gone = hop if arriving else hop - 1
        block = (z_me + NZ - gone) % NZ if way == 0 else (z_me + gone) % NZ
        return pltpu.make_async_remote_copy(
            src_ref=gath.at[block], dst_ref=gath.at[block], send_sem=zs_sem.at[way, hop - 1],
            recv_sem=zr_sem.at[way, hop - 1], device_id={"seq": me if arriving else near[3 + way]},
            device_id_type=mesh_ids)

    pl.semaphore_wait(barrier, len(near) + 1)
    for shift in range(1, NX):
        x_copy(shift).start()

    scale1 = 1.0 + mod_ref[1]
    normed = (center * lax.rsqrt(variance + EPSILON) * scale1 + mod_ref[0]).astype(BF16)
    for axis in range(3):
        rows = slice(axis * RES, (axis + 1) * RES)
        scaled[rows, :] = ((tabh[rows, :].astype(F32) + tabl[rows, :].astype(F32)) * scale1).astype(BF16)
    shift_rows = jnp.where(iota((8, D), 0) < 2, jnp.broadcast_to(mod_ref[0], (8, D)), 0.0)
    scaled[3 * RES :, :] = jnp.concatenate([inp * scale1, shift_rows, jnp.zeros((48, D), F32)], axis=0).astype(BF16)
    loads[10].wait()
    queries = mm(normed, wqkv[:, 0:HW])
    per_head = jnp.where(iota((HW, HW), 0) // HEAD == iota((HW, HW), 1) // HEAD, 1.0 / HEAD, 0.0).astype(BF16)
    mean_sq = mm((queries * queries).astype(BF16), per_head)
    queries = queries * lax.rsqrt(mean_sq + EPSILON) * (
        gain_ref[0:1, :] * gain_ref[1:2, :] * (HEAD ** (-0.5) * LOG2E))
    bkt[...] = mm(scaled[...], wqkv[:, HW : 2 * HW]).T.astype(BF16)
    first_half = iota((TOK, 2 * HEAD), 1) < HEAD
    for two in range(HEADS // 2):
        columns = slice(two * 2 * HEAD, (two + 1) * 2 * HEAD)
        both = queries[:, columns]
        mine = jnp.concatenate([jnp.where(first_half, both, 0.0), jnp.where(first_half, 0.0, both)], axis=0)
        umat[two * 256 : (two + 1) * 256, :] = mm(mine.astype(BF16), bkt[columns, :]).astype(BF16)
    bv[...] = mm(scaled[...], wqkv[:, 2 * HW : 3 * HW]).astype(BF16)
    head_scaled = head_ref[...] * (1.0 + mod_ref[4])
    hp_high[...], hp_low[...] = split(head_scaled)
    hp_const[...] = jnp.broadcast_to(jnp.sum(head_ref[...] * mod_ref[3], axis=1, keepdims=True), (LAT, TOK))
    loads[12].start()
    loads[13].start()

    def features(number):
        if number == 0:
            for shift in range(1, NX):
                x_arrival(shift).wait_recv()
        for way in range(2):
            if number > 0 and number <= HOPS[way]:
                z_copy(way, number, True).wait_recv()
            if number < HOPS[way]:
                z_copy(way, number + 1).start()
        sources = [((z_me + z) % NZ, x) for z in TILES[number] for x in range(NX)]
        width = TOK * len(sources)
        rows = jnp.concatenate([gath[z, x].astype(F32) for z, x in sources], axis=1)
        std_high, std_low = rows[12:13, :], rows[13:14, :]
        std = std_high + std_low
        inv_std = 1.0 / std
        which = iota((8, width), 0)
        ids = iota((RES, width), 0).astype(F32)
        ft, fs = ft_ref.at[number % 2], fs_ref.at[number % 2]
        for c in range(3):
            hit = ids == rows[8 + c : 9 + c, :]
            ft[c * RES : (c + 1) * RES, 0:width] = jnp.where(hit, 1.0, 0.0).astype(BF16)
            fs[c * RES : (c + 1) * RES, 0:width] = jnp.where(hit, inv_std, 0.0).astype(BF16)
        std_rows = jnp.where(which == 0, std_high, jnp.where(which == 1, std_low, 0.0))
        pad = jnp.zeros((48, width), F32)
        ft[3 * RES :, 0:width] = jnp.concatenate([rows[0:8, :], std_rows, pad], axis=0).astype(BF16)
        fs[3 * RES :, 0:width] = jnp.concatenate(
            [rows[0:8, :] * inv_std, jnp.where(which == 0, 1.0, 0.0), pad], axis=0).astype(BF16)
        return width, EPSILON * (std * std)

    width, eps_var = features(0)
    for number in range(len(TILES)):
        ft, fs = ft_ref[number % 2, :, 0:width], fs_ref[number % 2, :, 0:width]
        used, used_var = width, eps_var
        keys = mm(bkt[...], ft)
        scores = mm(umat[...], ft)
        for head in range(HEADS):
            keys_h = keys[head * HEAD : (head + 1) * HEAD, :]
            mean_h = jnp.sum(keys_h * keys_h, axis=0, keepdims=True) * (1.0 / HEAD)
            inv = lax.rsqrt(mean_h + used_var)
            p_ref[head * TOK : (head + 1) * TOK, 0:used] = jnp.exp2(
                scores[head * TOK : (head + 1) * TOK, :] * inv).astype(BF16)
        if number + 1 < len(TILES):
            width, eps_var = features(number + 1)
        found = mm_nt(p_ref[:, 0:used], fs)
        if number > 0:
            found += acc[...]
        acc[...] = found

    loads[11].wait()
    lane = iota((TOK, FEAT), 1)
    pieces = []
    for two in range(HEADS // 2):
        columns = slice(two * 2 * HEAD, (two + 1) * 2 * HEAD)
        halves = []
        for odd in range(2):
            head = 2 * two + odd
            total = acc[head * TOK : (head + 1) * TOK, :]
            denom = jnp.sum(jnp.where(lane == 200, total, 0.0), axis=1, keepdims=True)
            halves.append((total * (1.0 / denom)).astype(BF16))
        found = mm(jnp.concatenate(halves, axis=0), bv[:, columns])
        pieces.append(jnp.where(first_half, found[0:TOK, :], found[TOK : 2 * TOK, :]))
    attended = jnp.concatenate(pieces, axis=1).astype(BF16)
    width = 256
    total = jnp.zeros((TOK, 1), F32)
    for part in range(D // width):
        columns = slice(part * width, (part + 1) * width)
        piece = hid_ref[:, columns] + mod_ref[2][:, columns] * mm(attended, wout[:, columns])
        hid_ref[:, columns] = piece
        total = total + jnp.sum(piece, axis=1, keepdims=True)
    mean = total * (1.0 / D)
    square = jnp.zeros((TOK, 1), F32)
    velocity = jnp.zeros((LAT, TOK), F32)
    for part in range(D // width):
        columns = slice(part * width, (part + 1) * width)
        center = hid_ref[:, columns] - mean
        square = square + jnp.sum(center * center, axis=1, keepdims=True)
        c_high, c_low = split(center)
        velocity = velocity + (mm_nt(hp_high[:, columns], c_high)
                               + (mm_nt(hp_high[:, columns], c_low) + mm_nt(hp_low[:, columns], c_high)))
    inv_dev = jnp.broadcast_to(lax.rsqrt(square * (1.0 / D) + EPSILON), (TOK, TOK)).T[0:1, :]
    vel_ref[...] = velocity * inv_dev + hp_const[...]
    swap = pltpu.make_async_remote_copy(
        src_ref=vel_ref, dst_ref=vel_in, send_sem=ps_sem, recv_sem=pr_sem,
        device_id={"pair": other}, device_id_type=mesh_ids)
    swap.start()

    own_rows = jnp.broadcast_to(own_ref[...], (TOK, TOK)).astype(F32)
    own_cols = own_rows.T
    earlier = (own_rows == own_cols) & (iota((TOK, TOK), 0) < iota((TOK, TOK), 1))
    rank = jnp.sum(jnp.where(earlier, 1.0, 0.0), axis=0, keepdims=True)
    ranked = rank == ((iota((TOK, TOK), 0) // LAT) % CAP).astype(F32)
    own96 = jnp.broadcast_to(own_ref[...], (3 * N_SEQ, TOK))
    owner = iota((3 * N_SEQ, TOK), 0)
    owner = jnp.where(owner < N_SEQ, owner, jnp.where(owner < 2 * N_SEQ, owner - N_SEQ - 1, owner - 2 * N_SEQ + 1))
    dispatch = jnp.where(own96 == owner, 1.0, 0.0).astype(BF16)
    for shift in range(1, NX):
        x_copy(shift).wait_send()
    for way in range(2):
        for hop in range(1, HOPS[way] + 1):
            z_copy(way, hop).wait_send()
    swap.wait()
    mine, theirs = vel_ref[...], vel_in[...]
    is_cond = pair == 0
    cond = jnp.where(is_cond, mine, theirs)
    uncond = jnp.where(is_cond, theirs, mine)
    clean = lat_ref[...] - step_ref[0] * (uncond + GUIDANCE * (cond - uncond))
    wide = jnp.where(ranked, jnp.concatenate([clean] * (TOK // LAT), axis=0), 0.0)
    wide_high, wide_low = split(wide)
    packed = mm_nt(dispatch, wide_high) + mm_nt(dispatch, wide_low)
    sendbuf[:, 0, :] = jnp.where(
        iota((N_SEQ, TOK), 1) < LAT * CAP, packed[0:N_SEQ, :], packed[N_SEQ : 2 * N_SEQ, :])
    sendbuf[:, 1, :] = packed[2 * N_SEQ :, :]

    for shift in range(1, N_SEQ):
        dest = (me + shift) % N_SEQ
        pltpu.make_async_remote_copy(
            src_ref=sendbuf.at[dest], dst_ref=rbuf.at[me], send_sem=as_sem.at[shift], recv_sem=ar_sem.at[shift],
            device_id={"seq": dest}, device_id_type=mesh_ids).start()
    keep = pltpu.make_async_copy(sendbuf.at[me], rbuf.at[me], lsem.at[14])
    keep.start()

    lower = jnp.maximum(me - 1, 0)
    upper = jnp.minimum(me + 1, N_SEQ - 1)
    nb_ref[0:1, :] = gath[lower % NZ, lower // NZ].astype(F32)[11:12, :]
    nb_ref[1:2, :] = gath[upper % NZ, upper // NZ].astype(F32)[11:12, :]
    nb_ref[2:8, :] = jnp.zeros((6, TOK), F32)
    loads[12].wait()
    index = km_ref[...]
    index = jnp.where(index < SLOTS, ((index & (CAP - 1)) << 5) + (index >> 3), index)
    spot_ref[...] = index & (TOK - 1)
    chunk_ref[...] = index >> 7
    near_ref[...] = jnp.minimum(index, 300).astype(F32)
    far_ref[...] = jnp.where(index >= SLOTS, jnp.minimum(index - SLOTS, 300), 300).astype(F32)
    loads[13].wait()
    keep.wait()
    for shift in range(1, N_SEQ):
        source = (me + N_SEQ - shift) % N_SEQ
        pltpu.make_async_remote_copy(
            src_ref=sendbuf.at[source], dst_ref=rbuf.at[source], send_sem=as_sem.at[shift], recv_sem=ar_sem.at[shift],
            device_id={"seq": me}, device_id_type=mesh_ids).wait()
    x_ref[...] = rbuf[...]


TRIPLE = 3
PARTS = KOFF // TRIPLE
BLOCKS = FINE // TOK
SHARED = 0


def conv_kernel(
    x_ref, nb_ref, wt, spot_ref, chunk_ref, near_ref, far_ref, dproj_hbm, owned_ref, dec_ref, dproj_ref, feats, prod_a,
    prod_b, acc_x, acc_m, lsem
):
    load = pltpu.make_async_copy(dproj_hbm, dproj_ref, lsem)
    load.start()
    x0 = x_ref[:, 0, :]
    x1 = x_ref[:, 1, :]

    pick = jnp.where(iota((N_SEQ, SLOTS), 1) // CAP == iota((N_SEQ, SLOTS), 0), 1.0, 0.0).astype(BF16)
    xt_high, xt_low = split(x0.T)
    spread = mm(xt_high, pick) + mm(xt_low, pick)
    spread = jnp.where(iota((TOK, SLOTS), 1) % CAP == iota((TOK, SLOTS), 0) // LAT, spread, 0.0)
    owned = spread[0:LAT, :]
    for rank in range(1, CAP):
        owned = owned + spread[rank * LAT : (rank + 1) * LAT, :]
    owned_ref[...] = owned

    lane = iota((SLOTS, TOK), 1)
    own_rows = jnp.where(lane // LAT == iota((SLOTS, TOK), 0) // N_SEQ, jnp.concatenate([x0] * CAP, axis=0), 0.0)
    sub = iota((HALO, TOK), 0)
    lane = iota((HALO, TOK), 1)
    parts = [own_rows]
    for side, x_side in ((0, x0), (1, x1)):
        blocks = jnp.broadcast_to(nb_ref[side : side + 1, :], (HALO, TOK))
        first = 8 if side == 0 else 0
        chosen = jnp.sum(jnp.where(lane == sub // BLK + first, blocks, 0.0), axis=1, keepdims=True)
        source = chosen * (BLK // CAP) + ((iota((HALO, 1), 0) % BLK) // CAP).astype(F32)
        pick = jnp.where(iota((HALO, N_SEQ), 1).astype(F32) == source, 1.0, 0.0).astype(BF16)
        x_high, x_low = split(x_side)
        rows = mm(pick, x_high) + mm(pick, x_low)
        offset = CAP if side == 0 else 0
        parts.append(jnp.where(lane // LAT == sub % CAP + offset, rows, 0.0))
    l_high, l_low = split(jnp.concatenate(parts, axis=0))
    load.wait()
    p_high, p_low = split(dproj_ref[...])
    p_high = jnp.concatenate([p_high.astype(F32)] * (TOK // LAT), axis=0).astype(BF16)
    p_low = jnp.concatenate([p_low.astype(F32)] * (TOK // LAT), axis=0).astype(BF16)
    value = mm(jnp.concatenate([l_high, l_low], axis=1), jnp.concatenate([p_high, p_high], axis=0)) + mm(l_high, p_low)
    half = value * 0.5
    feats[...] = (half * jnp.tanh(half) + half).astype(BF16)
    acc_x[...] = jnp.zeros((OUT_DEV, FINE), F32)
    acc_m[...] = jnp.zeros((OUT_DEV, FINE), F32)

    def product(part, half, target):
        rows = pl.ds(pl.multiple_of(part * (TRIPLE * OUT_DEV), TRIPLE * OUT_DEV), TRIPLE * OUT_DEV)
        table = slice(half * SLOTS, (half + 1) * SLOTS)
        target[:, table] = mm_nt(wt[rows, :], feats[table, :])

    def by_gather(number, source, block):
        columns = slice(block * TOK, (block + 1) * TOK)
        spot = jnp.broadcast_to(spot_ref[number, block : block + 1, :], (OUT_DEV, TOK))
        chunk = jnp.broadcast_to(chunk_ref[number, block : block + 1, :], (OUT_DEV, TOK))
        value = jnp.zeros((OUT_DEV, TOK), F32)
        for c in range(4):
            found = jnp.take_along_axis(source[:, c * TOK : (c + 1) * TOK], spot, axis=1, mode="promise_in_bounds")
            value = jnp.where(chunk == c, found, value)
        acc_x[:, columns] += value

    first_ids = iota((16, TOK), 0).astype(F32).astype(BF16)

    def hot_rows(number, blocks):
        columns = []
        for block in blocks:
            rows = []
            for which in (near_ref, far_ref):
                row = jnp.broadcast_to(which[number, block : block + 1, :], (16, TOK)).astype(BF16) - first_ids
                for j in range(SLOTS // 16):
                    rows.append(jnp.where(row == jnp.bfloat16(16 * j), jnp.bfloat16(1), jnp.bfloat16(0)))
            columns.append(jnp.concatenate(rows, axis=0))
        return jnp.concatenate(columns, axis=1)

    def pick_rows(part, source, target):
        first = part * TRIPLE
        for quarter in range(4):
            blocks = (2 * quarter, 2 * quarter + 1)
            columns = slice(quarter * 2 * TOK, (quarter + 1) * 2 * TOK)
            if target is not None and quarter % 2 == 0:
                product(part + 1, quarter // 2, target)
            found = mm(source[2 * OUT_DEV :, :].astype(BF16), hot_rows(first + 2, blocks))
            if quarter >= SHARED:
                found += mm(source[OUT_DEV : 2 * OUT_DEV, :].astype(BF16), hot_rows(first + 1, blocks))
            acc_m[:, columns] += found
            for block in blocks:
                by_gather(first, source.at[0:OUT_DEV], block)
                if quarter < SHARED:
                    by_gather(first + 1, source.at[OUT_DEV : 2 * OUT_DEV], block)

    for half in range(2):
        product(0, half, prod_a)

    def two_parts(i, carry):
        pick_rows(2 * i, prod_a, prod_b)
        pick_rows(2 * i + 1, prod_b, prod_a)
        return carry

    lax.fori_loop(0, PARTS // 2, two_parts, 0)
    pick_rows(PARTS - 1, prod_a, None)
    dec_ref[...] = (acc_x[...] + acc_m[...]).astype(BF16)


def vmem(count):
    return [pl.BlockSpec(memory_space=pltpu.VMEM)] * count


def in_hbm(*arrays):
    return [pltpu.with_memory_space_constraint(array, pltpu.HBM) for array in arrays]


def hbm(count):
    return [pl.BlockSpec(memory_space=pltpu.HBM)] * count


def per_device(
    latents, voxel_coords, owner_map, step_time, modulation, in_proj, qkv_proj, norm_gain, out_proj, head_proj,
    decoder_projection, border_blocks, kernel_map, conv_weight,
):
    table = centred_position_table()
    table_high = table.astype(jnp.bfloat16)
    table_low = (table - table_high.astype(np.float32)).astype(jnp.bfloat16)
    dma = pltpu.SemaphoreType.DMA
    conv_table = jax.ShapeDtypeStruct((KOFF, BLOCKS, TOK), jnp.int32)
    conv_row = jax.ShapeDtypeStruct((KOFF, BLOCKS, TOK), F32)
    handed = pl.pallas_call(
        flow_kernel,
        out_shape=(
            jax.ShapeDtypeStruct((N_SEQ, 2, TOK), F32), jax.ShapeDtypeStruct((8, TOK), F32),
            jax.ShapeDtypeStruct((KOFF * OUT_DEV, DEC), BF16), conv_table, conv_table, conv_row, conv_row),
        in_specs=hbm(3) + [pl.BlockSpec(memory_space=pltpu.SMEM)] + hbm(11),
        out_specs=tuple(vmem(7)),
        scratch_shapes=[
            pltpu.VMEM((LAT, TOK), F32),
            pltpu.VMEM((3, 1, TOK), jnp.int32),
            pltpu.VMEM((1, TOK), jnp.int32),
            pltpu.VMEM((5, 1, D), F32),
            pltpu.VMEM((LAT, D), F32),
            pltpu.VMEM((2, HW), F32),
            pltpu.VMEM((LAT, D), F32),
            pltpu.VMEM((2, 8), jnp.int32),
            pltpu.VMEM((3 * RES, D), BF16),
            pltpu.VMEM((3 * RES, D), BF16),
            pltpu.VMEM((D, 3 * HW), BF16),
            pltpu.VMEM((HW, D), BF16),
            pltpu.VMEM((KOFF, BLOCKS, TOK), jnp.int32),
            pltpu.VMEM((NZ, NX, 16, TOK), BF16),
            pltpu.VMEM((16, TOK), F32),
            pltpu.VMEM((FEAT, D), BF16),
            pltpu.VMEM((HW, FEAT), BF16),
            pltpu.VMEM((FEAT, HW), BF16),
            pltpu.VMEM((HEADS * TOK, FEAT), BF16),
            pltpu.VMEM((TOK, D), F32),
            pltpu.VMEM((2, FEAT, 2 * GROUP), BF16),
            pltpu.VMEM((2, FEAT, 2 * GROUP), BF16),
            pltpu.VMEM((HEADS * TOK, 2 * GROUP), BF16),
            pltpu.VMEM((HEADS * TOK, FEAT), F32),
            pltpu.VMEM((LAT, D), BF16),
            pltpu.VMEM((LAT, D), BF16),
            pltpu.VMEM((LAT, TOK), F32),
            pltpu.VMEM((LAT, TOK), F32),
            pltpu.VMEM((LAT, TOK), F32),
            pltpu.VMEM((N_SEQ, 2, TOK), F32),
            pltpu.VMEM((N_SEQ, 2, TOK), F32),
            dma((15,)), dma((NX - 1,)), dma((NX - 1,)), dma((2, 4)), dma((2, 4)), dma, dma, dma((N_SEQ,)), dma((N_SEQ,)),
        ],
        compiler_params=pltpu.CompilerParams(collective_id=0, has_side_effects=True, vmem_limit_bytes=40 << 20),
        name="flow",
    )(*in_hbm(
        latents[0], jnp.transpose(voxel_coords, (1, 0, 2)), owner_map.reshape(1, TOK)), step_time, *in_hbm(
        modulation.reshape(5, 1, D), in_proj, norm_gain, head_proj.T, border_blocks[0, 0], jnp.asarray(table_high),
        jnp.asarray(table_low), qkv_proj, out_proj,
        jnp.swapaxes(conv_weight, 1, 2).reshape(KOFF * OUT_DEV, DEC), kernel_map.reshape(KOFF, BLOCKS, TOK)),
    )
    owned, decoded = pl.pallas_call(
        conv_kernel,
        out_shape=(jax.ShapeDtypeStruct((LAT, SLOTS), F32), jax.ShapeDtypeStruct((OUT_DEV, FINE), BF16)),
        in_specs=vmem(7) + hbm(1),
        out_specs=tuple(vmem(2)),
        scratch_shapes=[
            pltpu.VMEM((LAT, DEC), F32),
            pltpu.VMEM((2 * SLOTS, DEC), BF16),
            pltpu.VMEM((TRIPLE * OUT_DEV, 2 * SLOTS), F32),
            pltpu.VMEM((TRIPLE * OUT_DEV, 2 * SLOTS), F32),
            pltpu.VMEM((OUT_DEV, FINE), F32),
            pltpu.VMEM((OUT_DEV, FINE), F32),
            dma,
        ],
        compiler_params=pltpu.CompilerParams(vmem_limit_bytes=40 << 20),
        name="conv",
    )(*handed, *in_hbm(decoder_projection))
    return owned[None, None], decoded.T[None, None]


def solution(mesh):
    placed = (
        P("asset", None, "seq"),
        P("asset", None, "seq"),
        P("asset", "seq", None),
        P("asset"),
        P("asset", "pair", None, None),
        P(),
        P(),
        P(),
        P(),
        P(),
        P(),
        P("asset", "seq", None, None),
        P("asset", "seq", None, None),
        P(None, None, "pair"),
    )
    return jax.shard_map(
        per_device,
        mesh=mesh,
        in_specs=placed,
        out_specs=(P("asset", "seq", None, None), P("asset", "seq", None, "pair")),
        check_vma=False,
    )
```

```python
import math

import jax
import jax.numpy as jnp
import numpy as np
from jax import lax
from jax.experimental import pallas as pl
from jax.experimental.pallas import tpu as pltpu
from jax.sharding import PartitionSpec as P

D = 1024
HEADS = 8
HEAD = 64
LAT = 8
DEC = 768
KOFF = 27
BLK = 16
RES = 64
TOK = 128
CAP = 8
SLOTS = 256
HALO = 128
FINE = 1024
HW = 512
NX = 4
NZ = 8
N_SEQ = 32
OUT_DEV = 96
GROUP = NX * TOK
FEAT = 256
TILES = ((0,), (1, 7), (2, 6), (3, 5), (4,))
NEAR_FIRST = tuple((dx, dz) for tile in TILES for dx in (0, 1, 3, 2) for dz in tile if dx or dz)
EPSILON = 1e-06
GUIDANCE = 3.0
LOG2E = 1.4426950408889634
F32 = jnp.float32
BF16 = jnp.bfloat16


def centred_position_table():
    freqs = D // 6
    omegas = np.exp(-math.log(10000.0) * (np.arange(freqs) / freqs))
    angles = np.arange(RES)[:, None] * omegas[None, :]
    halves = np.concatenate([np.sin(angles), np.cos(angles)], axis=1)
    table = np.zeros((3 * RES, D))
    for axis in range(3):
        table[axis * RES : (axis + 1) * RES, axis * 2 * freqs : (axis + 1) * 2 * freqs] = halves
    return (table - table.mean(axis=1, keepdims=True)).astype(np.float32)


def split(values):
    high = values.astype(BF16)
    return high, (values - high.astype(F32)).astype(BF16)


def mm(a, b):
    return lax.dot_general(a, b, (((1,), (0,)), ((), ())), preferred_element_type=F32)


def mm_nt(a, b):
    return lax.dot_general(a, b, (((1,), (1,)), ((), ())), preferred_element_type=F32)


def iota(shape, dim):
    return lax.broadcasted_iota(jnp.int32, shape, dim)


def one_hots(rows, width):
    ids = iota((RES, width), 0).astype(F32)
    return [jnp.where(ids == rows[c : c + 1, :], 1.0, 0.0) for c in range(3)]


def flow_kernel(
    lat_hbm, coord_hbm, own_hbm, step_ref, mod_hbm, inp_hbm, gain_hbm, head_hbm, bb_hbm, tabh_hbm, tabl_hbm, wqkv_hbm,
    wout_hbm, wt_hbm, km_hbm,
    x_ref, nb_ref, wt_ref, spot_ref, chunk_ref, near_ref, far_ref,
    lat_ref, coord_ref, own_ref, mod_ref, inp_ref, gain_ref, head_ref, bb_ref, tabh, tabl, wqkv, wout, km_ref,
    gath, stage, scaled, bkt, bv, umat, hid_ref, ft_ref, fs_ref, p_ref, acc, hp_high, hp_low, hp_const, vel_ref, vel_in,
    sendbuf, rbuf,
    lsem, gs_sem, gr_sem, ps_sem, pr_sem, as_sem, ar_sem,
):
    me = lax.axis_index("seq")
    pair = lax.axis_index("pair")
    other = 1 - pair
    x_me = me // NZ
    z_me = me % NZ
    mesh_ids = pl.DeviceIdType.MESH

    def ahead(dx, dz):
        return ((x_me + dx) % NX) * NZ + (z_me + dz) % NZ

    def behind(dx, dz):
        return ((x_me + NX - dx) % NX) * NZ + (z_me + NZ - dz) % NZ

    loads = [
        pltpu.make_async_copy(source, target, lsem.at[number])
        for number, (source, target) in enumerate((
            (lat_hbm, lat_ref), (coord_hbm, coord_ref), (own_hbm, own_ref), (mod_hbm, mod_ref), (inp_hbm, inp_ref),
            (gain_hbm, gain_ref), (head_hbm, head_ref), (bb_hbm, bb_ref), (tabh_hbm, tabh), (tabl_hbm, tabl),
            (wqkv_hbm, wqkv), (wout_hbm, wout), (km_hbm, km_ref), (wt_hbm, wt_ref)))
    ]
    for load in loads[:12]:
        load.start()

    barrier = pltpu.get_barrier_semaphore()
    for dx, dz in reversed(NEAR_FIRST):
        pl.semaphore_signal(barrier, inc=1, device_id={"seq": ahead(dx, dz)}, device_id_type=mesh_ids)
    pl.semaphore_signal(barrier, inc=1, device_id={"pair": other}, device_id_type=mesh_ids)
    for load in loads[:10]:
        load.wait()

    lat = lat_ref[...]
    stage[...] = jnp.zeros((16, TOK), F32)
    stage[0:8, :] = lat
    for axis in range(3):
        stage[8 + axis : 9 + axis, :] = coord_ref[axis].astype(F32)
    stage[11:12, 0:8] = bb_ref[0:1, :].astype(F32)
    stage[11:12, 8:16] = bb_ref[1:2, :].astype(F32)
    lat_high = lat.astype(BF16).astype(F32)
    zero8 = jnp.zeros((8, TOK), F32)
    own_feat = jnp.concatenate(
        one_hots(stage[8:11, :], TOK) + [lat_high, zero8, lat - lat_high, jnp.zeros((40, TOK), F32)], axis=0)
    own_feat = own_feat.T.astype(BF16)
    inp = inp_ref[...]
    inp = inp - jnp.mean(inp, axis=1, keepdims=True)
    inp_rows = jnp.concatenate([inp, jnp.zeros((8, D), F32), inp, jnp.zeros((40, D), F32)], axis=0)
    rows_high, rows_low = split(inp_rows)
    basis_high = jnp.concatenate([tabh[...], rows_high], axis=0)
    basis_low = jnp.concatenate([tabl[...], rows_low], axis=0)
    hidden = mm(own_feat, basis_high) + mm(own_feat, basis_low)
    hid_ref[...] = hidden
    center = hidden - jnp.mean(hidden, axis=1, keepdims=True)
    variance = jnp.mean(center * center, axis=1, keepdims=True)
    std = jnp.broadcast_to(jnp.sqrt(variance + EPSILON), (TOK, TOK)).T[0:1, :]
    std_high = std.astype(BF16).astype(F32)
    stage[12:13, :] = std_high
    stage[13:14, :] = std - std_high
    gath[me] = stage[...].astype(BF16)

    def g_copy(dx, dz):
        return pltpu.make_async_remote_copy(
            src_ref=gath.at[me], dst_ref=gath.at[me], send_sem=gs_sem.at[dx, dz], recv_sem=gr_sem.at[dx, dz],
            device_id={"seq": ahead(dx, dz)}, device_id_type=mesh_ids)

    pl.semaphore_wait(barrier, N_SEQ)
    for dx, dz in NEAR_FIRST:
        g_copy(dx, dz).start()

    scale1 = 1.0 + mod_ref[1]
    normed = (center * lax.rsqrt(variance + EPSILON) * scale1 + mod_ref[0]).astype(BF16)
    for axis in range(3):
        rows = slice(axis * RES, (axis + 1) * RES)
        scaled[rows, :] = ((tabh[rows, :].astype(F32) + tabl[rows, :].astype(F32)) * scale1).astype(BF16)
    shift_rows = jnp.where(iota((8, D), 0) < 2, jnp.broadcast_to(mod_ref[0], (8, D)), 0.0)
    scaled[3 * RES :, :] = jnp.concatenate([inp * scale1, shift_rows, jnp.zeros((48, D), F32)], axis=0).astype(BF16)
    loads[10].wait()
    queries = mm(normed, wqkv[:, 0:HW])
    per_head = jnp.where(iota((HW, HW), 0) // HEAD == iota((HW, HW), 1) // HEAD, 1.0 / HEAD, 0.0).astype(BF16)
    mean_sq = mm((queries * queries).astype(BF16), per_head)
    queries = queries * lax.rsqrt(mean_sq + EPSILON) * (
        gain_ref[0:1, :] * gain_ref[1:2, :] * (HEAD ** (-0.5) * LOG2E))
    bkt[...] = mm(scaled[...], wqkv[:, HW : 2 * HW]).T.astype(BF16)
    first_half = iota((TOK, 2 * HEAD), 1) < HEAD
    for two in range(HEADS // 2):
        columns = slice(two * 2 * HEAD, (two + 1) * 2 * HEAD)
        both = queries[:, columns]
        mine = jnp.concatenate([jnp.where(first_half, both, 0.0), jnp.where(first_half, 0.0, both)], axis=0)
        umat[two * 256 : (two + 1) * 256, :] = mm(mine.astype(BF16), bkt[columns, :]).astype(BF16)
    bv[...] = mm(scaled[...], wqkv[:, 2 * HW : 3 * HW]).astype(BF16)
    head_scaled = head_ref[...] * (1.0 + mod_ref[4])
    hp_high[...], hp_low[...] = split(head_scaled)
    hp_const[...] = jnp.broadcast_to(jnp.sum(head_ref[...] * mod_ref[3], axis=1, keepdims=True), (LAT, TOK))
    loads[12].start()
    loads[13].start()

    def features(number):
        sources = []
        for dz in TILES[number]:
            for dx in range(NX):
                source = behind(dx, dz)
                sources.append(source)
                if dx > 0 or dz > 0:
                    pltpu.make_async_remote_copy(
                        src_ref=gath.at[source], dst_ref=gath.at[source], send_sem=gs_sem.at[dx, dz],
                        recv_sem=gr_sem.at[dx, dz], device_id={"seq": me}, device_id_type=mesh_ids).wait_recv()
        width = TOK * len(sources)
        rows = jnp.concatenate([gath[source].astype(F32) for source in sources], axis=1)
        std_high, std_low = rows[12:13, :], rows[13:14, :]
        std = std_high + std_low
        inv_std = 1.0 / std
        which = iota((8, width), 0)
        ids = iota((RES, width), 0).astype(F32)
        ft, fs = ft_ref.at[number % 2], fs_ref.at[number % 2]
        for c in range(3):
            hit = ids == rows[8 + c : 9 + c, :]
            ft[c * RES : (c + 1) * RES, 0:width] = jnp.where(hit, 1.0, 0.0).astype(BF16)
            fs[c * RES : (c + 1) * RES, 0:width] = jnp.where(hit, inv_std, 0.0).astype(BF16)
        std_rows = jnp.where(which == 0, std_high, jnp.where(which == 1, std_low, 0.0))
        pad = jnp.zeros((48, width), F32)
        ft[3 * RES :, 0:width] = jnp.concatenate([rows[0:8, :], std_rows, pad], axis=0).astype(BF16)
        fs[3 * RES :, 0:width] = jnp.concatenate(
            [rows[0:8, :] * inv_std, jnp.where(which == 0, 1.0, 0.0), pad], axis=0).astype(BF16)
        return width, EPSILON * (std * std)

    width, eps_var = features(0)
    for number in range(len(TILES)):
        ft, fs = ft_ref[number % 2, :, 0:width], fs_ref[number % 2, :, 0:width]
        used, used_var = width, eps_var
        keys = mm(bkt[...], ft)
        scores = mm(umat[...], ft)
        for head in range(HEADS):
            keys_h = keys[head * HEAD : (head + 1) * HEAD, :]
            mean_h = jnp.sum(keys_h * keys_h, axis=0, keepdims=True) * (1.0 / HEAD)
            inv = lax.rsqrt(mean_h + used_var)
            p_ref[head * TOK : (head + 1) * TOK, 0:used] = jnp.exp2(
                scores[head * TOK : (head + 1) * TOK, :] * inv).astype(BF16)
        if number + 1 < len(TILES):
            width, eps_var = features(number + 1)
        found = mm_nt(p_ref[:, 0:used], fs)
        if number > 0:
            found += acc[...]
        acc[...] = found

    loads[11].wait()
    lane = iota((TOK, FEAT), 1)
    pieces = []
    for two in range(HEADS // 2):
        columns = slice(two * 2 * HEAD, (two + 1) * 2 * HEAD)
        halves = []
        for odd in range(2):
            head = 2 * two + odd
            total = acc[head * TOK : (head + 1) * TOK, :]
            denom = jnp.sum(jnp.where(lane == 200, total, 0.0), axis=1, keepdims=True)
            halves.append((total * (1.0 / denom)).astype(BF16))
        found = mm(jnp.concatenate(halves, axis=0), bv[:, columns])
        pieces.append(jnp.where(first_half, found[0:TOK, :], found[TOK : 2 * TOK, :]))
    attended = jnp.concatenate(pieces, axis=1).astype(BF16)
    width = 256
    total = jnp.zeros((TOK, 1), F32)
    for part in range(D // width):
        columns = slice(part * width, (part + 1) * width)
        piece = hid_ref[:, columns] + mod_ref[2][:, columns] * mm(attended, wout[:, columns])
        hid_ref[:, columns] = piece
        total = total + jnp.sum(piece, axis=1, keepdims=True)
    mean = total * (1.0 / D)
    square = jnp.zeros((TOK, 1), F32)
    velocity = jnp.zeros((LAT, TOK), F32)
    for part in range(D // width):
        columns = slice(part * width, (part + 1) * width)
        center = hid_ref[:, columns] - mean
        square = square + jnp.sum(center * center, axis=1, keepdims=True)
        c_high, c_low = split(center)
        velocity = velocity + (mm_nt(hp_high[:, columns], c_high)
                               + (mm_nt(hp_high[:, columns], c_low) + mm_nt(hp_low[:, columns], c_high)))
    inv_dev = jnp.broadcast_to(lax.rsqrt(square * (1.0 / D) + EPSILON), (TOK, TOK)).T[0:1, :]
    vel_ref[...] = velocity * inv_dev + hp_const[...]
    swap = pltpu.make_async_remote_copy(
        src_ref=vel_ref, dst_ref=vel_in, send_sem=ps_sem, recv_sem=pr_sem,
        device_id={"pair": other}, device_id_type=mesh_ids)
    swap.start()

    own_rows = jnp.broadcast_to(own_ref[...], (TOK, TOK)).astype(F32)
    own_cols = own_rows.T
    earlier = (own_rows == own_cols) & (iota((TOK, TOK), 0) < iota((TOK, TOK), 1))
    rank = jnp.sum(jnp.where(earlier, 1.0, 0.0), axis=0, keepdims=True)
    ranked = rank == ((iota((TOK, TOK), 0) // LAT) % CAP).astype(F32)
    own96 = jnp.broadcast_to(own_ref[...], (3 * N_SEQ, TOK))
    owner = iota((3 * N_SEQ, TOK), 0)
    owner = jnp.where(owner < N_SEQ, owner, jnp.where(owner < 2 * N_SEQ, owner - N_SEQ - 1, owner - 2 * N_SEQ + 1))
    dispatch = jnp.where(own96 == owner, 1.0, 0.0).astype(BF16)
    for dx, dz in NEAR_FIRST:
        g_copy(dx, dz).wait_send()
    swap.wait()
    mine, theirs = vel_ref[...], vel_in[...]
    is_cond = pair == 0
    cond = jnp.where(is_cond, mine, theirs)
    uncond = jnp.where(is_cond, theirs, mine)
    clean = lat_ref[...] - step_ref[0] * (uncond + GUIDANCE * (cond - uncond))
    wide = jnp.where(ranked, jnp.concatenate([clean] * (TOK // LAT), axis=0), 0.0)
    wide_high, wide_low = split(wide)
    packed = mm_nt(dispatch, wide_high) + mm_nt(dispatch, wide_low)
    sendbuf[:, 0, :] = jnp.where(
        iota((N_SEQ, TOK), 1) < LAT * CAP, packed[0:N_SEQ, :], packed[N_SEQ : 2 * N_SEQ, :])
    sendbuf[:, 1, :] = packed[2 * N_SEQ :, :]

    for shift in range(1, N_SEQ):
        dest = (me + shift) % N_SEQ
        pltpu.make_async_remote_copy(
            src_ref=sendbuf.at[dest], dst_ref=rbuf.at[me], send_sem=as_sem.at[shift], recv_sem=ar_sem.at[shift],
            device_id={"seq": dest}, device_id_type=mesh_ids).start()
    keep = pltpu.make_async_copy(sendbuf.at[me], rbuf.at[me], lsem.at[14])
    keep.start()

    lower = jnp.maximum(me - 1, 0)
    upper = jnp.minimum(me + 1, N_SEQ - 1)
    nb_ref[0:1, :] = gath[lower].astype(F32)[11:12, :]
    nb_ref[1:2, :] = gath[upper].astype(F32)[11:12, :]
    nb_ref[2:8, :] = jnp.zeros((6, TOK), F32)
    loads[12].wait()
    index = km_ref[...]
    index = jnp.where(index < SLOTS, ((index & (CAP - 1)) << 5) + (index >> 3), index)
    spot_ref[...] = index & (TOK - 1)
    chunk_ref[...] = index >> 7
    near_ref[...] = jnp.minimum(index, 300).astype(F32)
    far_ref[...] = jnp.where(index >= SLOTS, jnp.minimum(index - SLOTS, 300), 300).astype(F32)
    loads[13].wait()
    keep.wait()
    for shift in range(1, N_SEQ):
        source = (me + N_SEQ - shift) % N_SEQ
        pltpu.make_async_remote_copy(
            src_ref=sendbuf.at[source], dst_ref=rbuf.at[source], send_sem=as_sem.at[shift], recv_sem=ar_sem.at[shift],
            device_id={"seq": me}, device_id_type=mesh_ids).wait()
    x_ref[...] = rbuf[...]


TRIPLE = 3
PARTS = KOFF // TRIPLE
BLOCKS = FINE // TOK
SHARED = 0


def conv_kernel(
    x_ref, nb_ref, wt, spot_ref, chunk_ref, near_ref, far_ref, dproj_hbm, owned_ref, dec_ref, dproj_ref, feats, prod_a,
    prod_b, acc_x, acc_m, lsem
):
    load = pltpu.make_async_copy(dproj_hbm, dproj_ref, lsem)
    load.start()
    x0 = x_ref[:, 0, :]
    x1 = x_ref[:, 1, :]

    pick = jnp.where(iota((N_SEQ, SLOTS), 1) // CAP == iota((N_SEQ, SLOTS), 0), 1.0, 0.0).astype(BF16)
    xt_high, xt_low = split(x0.T)
    spread = mm(xt_high, pick) + mm(xt_low, pick)
    spread = jnp.where(iota((TOK, SLOTS), 1) % CAP == iota((TOK, SLOTS), 0) // LAT, spread, 0.0)
    owned = spread[0:LAT, :]
    for rank in range(1, CAP):
        owned = owned + spread[rank * LAT : (rank + 1) * LAT, :]
    owned_ref[...] = owned

    lane = iota((SLOTS, TOK), 1)
    own_rows = jnp.where(lane // LAT == iota((SLOTS, TOK), 0) // N_SEQ, jnp.concatenate([x0] * CAP, axis=0), 0.0)
    sub = iota((HALO, TOK), 0)
    lane = iota((HALO, TOK), 1)
    parts = [own_rows]
    for side, x_side in ((0, x0), (1, x1)):
        blocks = jnp.broadcast_to(nb_ref[side : side + 1, :], (HALO, TOK))
        first = 8 if side == 0 else 0
        chosen = jnp.sum(jnp.where(lane == sub // BLK + first, blocks, 0.0), axis=1, keepdims=True)
        source = chosen * (BLK // CAP) + ((iota((HALO, 1), 0) % BLK) // CAP).astype(F32)
        pick = jnp.where(iota((HALO, N_SEQ), 1).astype(F32) == source, 1.0, 0.0).astype(BF16)
        x_high, x_low = split(x_side)
        rows = mm(pick, x_high) + mm(pick, x_low)
        offset = CAP if side == 0 else 0
        parts.append(jnp.where(lane // LAT == sub % CAP + offset, rows, 0.0))
    l_high, l_low = split(jnp.concatenate(parts, axis=0))
    load.wait()
    p_high, p_low = split(dproj_ref[...])
    p_high = jnp.concatenate([p_high.astype(F32)] * (TOK // LAT), axis=0).astype(BF16)
    p_low = jnp.concatenate([p_low.astype(F32)] * (TOK // LAT), axis=0).astype(BF16)
    value = mm(jnp.concatenate([l_high, l_low], axis=1), jnp.concatenate([p_high, p_high], axis=0)) + mm(l_high, p_low)
    half = value * 0.5
    feats[...] = (half * jnp.tanh(half) + half).astype(BF16)
    acc_x[...] = jnp.zeros((OUT_DEV, FINE), F32)
    acc_m[...] = jnp.zeros((OUT_DEV, FINE), F32)

    def product(part, half, target):
        rows = pl.ds(pl.multiple_of(part * (TRIPLE * OUT_DEV), TRIPLE * OUT_DEV), TRIPLE * OUT_DEV)
        table = slice(half * SLOTS, (half + 1) * SLOTS)
        target[:, table] = mm_nt(wt[rows, :], feats[table, :])

    def by_gather(number, source, block):
        columns = slice(block * TOK, (block + 1) * TOK)
        spot = jnp.broadcast_to(spot_ref[number, block : block + 1, :], (OUT_DEV, TOK))
        chunk = jnp.broadcast_to(chunk_ref[number, block : block + 1, :], (OUT_DEV, TOK))
        value = jnp.zeros((OUT_DEV, TOK), F32)
        for c in range(4):
            found = jnp.take_along_axis(source[:, c * TOK : (c + 1) * TOK], spot, axis=1, mode="promise_in_bounds")
            value = jnp.where(chunk == c, found, value)
        acc_x[:, columns] += value

    first_ids = iota((16, TOK), 0).astype(F32).astype(BF16)

    def hot_rows(number, blocks):
        columns = []
        for block in blocks:
            rows = []
            for which in (near_ref, far_ref):
                row = jnp.broadcast_to(which[number, block : block + 1, :], (16, TOK)).astype(BF16) - first_ids
                for j in range(SLOTS // 16):
                    rows.append(jnp.where(row == jnp.bfloat16(16 * j), jnp.bfloat16(1), jnp.bfloat16(0)))
            columns.append(jnp.concatenate(rows, axis=0))
        return jnp.concatenate(columns, axis=1)

    def pick_rows(part, source, target):
        first = part * TRIPLE
        for quarter in range(4):
            blocks = (2 * quarter, 2 * quarter + 1)
            columns = slice(quarter * 2 * TOK, (quarter + 1) * 2 * TOK)
            if target is not None and quarter % 2 == 0:
                product(part + 1, quarter // 2, target)
            found = mm(source[2 * OUT_DEV :, :].astype(BF16), hot_rows(first + 2, blocks))
            if quarter >= SHARED:
                found += mm(source[OUT_DEV : 2 * OUT_DEV, :].astype(BF16), hot_rows(first + 1, blocks))
            acc_m[:, columns] += found
            for block in blocks:
                by_gather(first, source.at[0:OUT_DEV], block)
                if quarter < SHARED:
                    by_gather(first + 1, source.at[OUT_DEV : 2 * OUT_DEV], block)

    for half in range(2):
        product(0, half, prod_a)

    def two_parts(i, carry):
        pick_rows(2 * i, prod_a, prod_b)
        pick_rows(2 * i + 1, prod_b, prod_a)
        return carry

    lax.fori_loop(0, PARTS // 2, two_parts, 0)
    pick_rows(PARTS - 1, prod_a, None)
    dec_ref[...] = (acc_x[...] + acc_m[...]).astype(BF16)


def vmem(count):
    return [pl.BlockSpec(memory_space=pltpu.VMEM)] * count


def in_hbm(*arrays):
    return [pltpu.with_memory_space_constraint(array, pltpu.HBM) for array in arrays]


def hbm(count):
    return [pl.BlockSpec(memory_space=pltpu.HBM)] * count


def per_device(
    latents, voxel_coords, owner_map, step_time, modulation, in_proj, qkv_proj, norm_gain, out_proj, head_proj,
    decoder_projection, border_blocks, kernel_map, conv_weight,
):
    table = centred_position_table()
    table_high = table.astype(jnp.bfloat16)
    table_low = (table - table_high.astype(np.float32)).astype(jnp.bfloat16)
    dma = pltpu.SemaphoreType.DMA
    conv_table = jax.ShapeDtypeStruct((KOFF, BLOCKS, TOK), jnp.int32)
    conv_row = jax.ShapeDtypeStruct((KOFF, BLOCKS, TOK), F32)
    handed = pl.pallas_call(
        flow_kernel,
        out_shape=(
            jax.ShapeDtypeStruct((N_SEQ, 2, TOK), F32), jax.ShapeDtypeStruct((8, TOK), F32),
            jax.ShapeDtypeStruct((KOFF * OUT_DEV, DEC), BF16), conv_table, conv_table, conv_row, conv_row),
        in_specs=hbm(3) + [pl.BlockSpec(memory_space=pltpu.SMEM)] + hbm(11),
        out_specs=tuple(vmem(7)),
        scratch_shapes=[
            pltpu.VMEM((LAT, TOK), F32),
            pltpu.VMEM((3, 1, TOK), jnp.int32),
            pltpu.VMEM((1, TOK), jnp.int32),
            pltpu.VMEM((5, 1, D), F32),
            pltpu.VMEM((LAT, D), F32),
            pltpu.VMEM((2, HW), F32),
            pltpu.VMEM((LAT, D), F32),
            pltpu.VMEM((2, 8), jnp.int32),
            pltpu.VMEM((3 * RES, D), BF16),
            pltpu.VMEM((3 * RES, D), BF16),
            pltpu.VMEM((D, 3 * HW), BF16),
            pltpu.VMEM((HW, D), BF16),
            pltpu.VMEM((KOFF, BLOCKS, TOK), jnp.int32),
            pltpu.VMEM((N_SEQ, 16, TOK), BF16),
            pltpu.VMEM((16, TOK), F32),
            pltpu.VMEM((FEAT, D), BF16),
            pltpu.VMEM((HW, FEAT), BF16),
            pltpu.VMEM((FEAT, HW), BF16),
            pltpu.VMEM((HEADS * TOK, FEAT), BF16),
            pltpu.VMEM((TOK, D), F32),
            pltpu.VMEM((2, FEAT, 2 * GROUP), BF16),
            pltpu.VMEM((2, FEAT, 2 * GROUP), BF16),
            pltpu.VMEM((HEADS * TOK, 2 * GROUP), BF16),
            pltpu.VMEM((HEADS * TOK, FEAT), F32),
            pltpu.VMEM((LAT, D), BF16),
            pltpu.VMEM((LAT, D), BF16),
            pltpu.VMEM((LAT, TOK), F32),
            pltpu.VMEM((LAT, TOK), F32),
            pltpu.VMEM((LAT, TOK), F32),
            pltpu.VMEM((N_SEQ, 2, TOK), F32),
            pltpu.VMEM((N_SEQ, 2, TOK), F32),
            dma((15,)), dma((NX, NZ)), dma((NX, NZ)), dma, dma, dma((N_SEQ,)), dma((N_SEQ,)),
        ],
        compiler_params=pltpu.CompilerParams(collective_id=0, has_side_effects=True, vmem_limit_bytes=40 << 20),
        name="flow",
    )(*in_hbm(
        latents[0], jnp.transpose(voxel_coords, (1, 0, 2)), owner_map.reshape(1, TOK)), step_time, *in_hbm(
        modulation.reshape(5, 1, D), in_proj, norm_gain, head_proj.T, border_blocks[0, 0], jnp.asarray(table_high),
        jnp.asarray(table_low), qkv_proj, out_proj,
        jnp.swapaxes(conv_weight, 1, 2).reshape(KOFF * OUT_DEV, DEC), kernel_map.reshape(KOFF, BLOCKS, TOK)),
    )
    owned, decoded = pl.pallas_call(
        conv_kernel,
        out_shape=(jax.ShapeDtypeStruct((LAT, SLOTS), F32), jax.ShapeDtypeStruct((OUT_DEV, FINE), BF16)),
        in_specs=vmem(7) + hbm(1),
        out_specs=tuple(vmem(2)),
        scratch_shapes=[
            pltpu.VMEM((LAT, DEC), F32),
            pltpu.VMEM((2 * SLOTS, DEC), BF16),
            pltpu.VMEM((TRIPLE * OUT_DEV, 2 * SLOTS), F32),
            pltpu.VMEM((TRIPLE * OUT_DEV, 2 * SLOTS), F32),
            pltpu.VMEM((OUT_DEV, FINE), F32),
            pltpu.VMEM((OUT_DEV, FINE), F32),
            dma,
        ],
        compiler_params=pltpu.CompilerParams(vmem_limit_bytes=40 << 20),
        name="conv",
    )(*handed, *in_hbm(decoder_projection))
    return owned[None, None], decoded.T[None, None]


def solution(mesh):
    placed = (
        P("asset", None, "seq"),
        P("asset", None, "seq"),
        P("asset", "seq", None),
        P("asset"),
        P("asset", "pair", None, None),
        P(),
        P(),
        P(),
        P(),
        P(),
        P(),
        P("asset", "seq", None, None),
        P("asset", "seq", None, None),
        P(None, None, "pair"),
    )
    return jax.shard_map(
        per_device,
        mesh=mesh,
        in_specs=placed,
        out_specs=(P("asset", "seq", None, None), P("asset", "seq", None, "pair")),
        check_vma=False,
    )
```

```python
import math

import jax
import jax.numpy as jnp
import numpy as np
from jax import lax
from jax.experimental import pallas as pl
from jax.experimental.pallas import tpu as pltpu
from jax.sharding import PartitionSpec as P

D = 1024
HEADS = 8
HEAD = 64
LAT = 8
DEC = 768
KOFF = 27
BLK = 16
RES = 64
TOK = 128
CAP = 8
SLOTS = 256
HALO = 128
FINE = 1024
HW = 512
NX = 4
NZ = 8
N_SEQ = 32
OUT_DEV = 96
GROUP = NX * TOK
FEAT = 256
TILES = ((0,), (1, 7), (2, 6), (3, 5), (4,))
NEAR_FIRST = tuple((dx, dz) for tile in TILES for dx in (0, 1, 3, 2) for dz in tile if dx or dz)
EPSILON = 1e-06
GUIDANCE = 3.0
LOG2E = 1.4426950408889634
F32 = jnp.float32
BF16 = jnp.bfloat16


def centred_position_table():
    freqs = D // 6
    omegas = np.exp(-math.log(10000.0) * (np.arange(freqs) / freqs))
    angles = np.arange(RES)[:, None] * omegas[None, :]
    halves = np.concatenate([np.sin(angles), np.cos(angles)], axis=1)
    table = np.zeros((3 * RES, D))
    for axis in range(3):
        table[axis * RES : (axis + 1) * RES, axis * 2 * freqs : (axis + 1) * 2 * freqs] = halves
    return (table - table.mean(axis=1, keepdims=True)).astype(np.float32)


def split(values):
    high = values.astype(BF16)
    return high, (values - high.astype(F32)).astype(BF16)


def mm(a, b):
    return lax.dot_general(a, b, (((1,), (0,)), ((), ())), preferred_element_type=F32)


def mm_nt(a, b):
    return lax.dot_general(a, b, (((1,), (1,)), ((), ())), preferred_element_type=F32)


def iota(shape, dim):
    return lax.broadcasted_iota(jnp.int32, shape, dim)


def one_hots(rows, width):
    ids = iota((RES, width), 0).astype(F32)
    return [jnp.where(ids == rows[c : c + 1, :], 1.0, 0.0) for c in range(3)]


def flow_kernel(
    lat_hbm, coord_hbm, own_hbm, step_ref, mod_hbm, inp_hbm, gain_hbm, head_hbm, bb_hbm, tabh_hbm, tabl_hbm, wqkv_hbm,
    wout_hbm, wt_hbm, km_hbm,
    x_ref, nb_ref, wt_ref, spot_ref, chunk_ref, near_ref, far_ref,
    lat_ref, coord_ref, own_ref, mod_ref, inp_ref, gain_ref, head_ref, bb_ref, tabh, tabl, wqkv, wout, km_ref,
    gath, stage, scaled, bkt, bv, umat, hid_ref, ft_ref, fs_ref, p_ref, acc, hp_high, hp_low, hp_const, ranked, dispatch,
    sendbuf, rbuf,
    lsem, gs_sem, gr_sem, as_sem, ar_sem,
):
    me = lax.axis_index("seq")
    pair = lax.axis_index("pair")
    other = 1 - pair
    x_me = me // NZ
    z_me = me % NZ
    mesh_ids = pl.DeviceIdType.MESH

    def ahead(dx, dz):
        return ((x_me + dx) % NX) * NZ + (z_me + dz) % NZ

    def behind(dx, dz):
        return ((x_me + NX - dx) % NX) * NZ + (z_me + NZ - dz) % NZ

    loads = [
        pltpu.make_async_copy(source, target, lsem.at[number])
        for number, (source, target) in enumerate((
            (lat_hbm, lat_ref), (coord_hbm, coord_ref), (own_hbm, own_ref), (mod_hbm, mod_ref), (inp_hbm, inp_ref),
            (gain_hbm, gain_ref), (head_hbm, head_ref), (bb_hbm, bb_ref), (tabh_hbm, tabh), (tabl_hbm, tabl),
            (wqkv_hbm, wqkv), (wout_hbm, wout), (km_hbm, km_ref), (wt_hbm, wt_ref)))
    ]
    for load in loads[:12]:
        load.start()

    barrier = pltpu.get_barrier_semaphore()
    for dx, dz in reversed(NEAR_FIRST):
        pl.semaphore_signal(barrier, inc=1, device_id={"seq": ahead(dx, dz)}, device_id_type=mesh_ids)
    pl.semaphore_signal(barrier, inc=1, device_id={"pair": other}, device_id_type=mesh_ids)
    for load in loads[:10]:
        load.wait()

    lat = lat_ref[...]
    stage[...] = jnp.zeros((16, TOK), F32)
    stage[0:8, :] = lat
    for axis in range(3):
        stage[8 + axis : 9 + axis, :] = coord_ref[axis].astype(F32)
    stage[11:12, 0:8] = bb_ref[0:1, :].astype(F32)
    stage[11:12, 8:16] = bb_ref[1:2, :].astype(F32)
    lat_high = lat.astype(BF16).astype(F32)
    zero8 = jnp.zeros((8, TOK), F32)
    own_feat = jnp.concatenate(
        one_hots(stage[8:11, :], TOK) + [lat_high, zero8, lat - lat_high, jnp.zeros((40, TOK), F32)], axis=0)
    own_feat = own_feat.T.astype(BF16)
    inp = inp_ref[...]
    inp = inp - jnp.mean(inp, axis=1, keepdims=True)
    inp_rows = jnp.concatenate([inp, jnp.zeros((8, D), F32), inp, jnp.zeros((40, D), F32)], axis=0)
    rows_high, rows_low = split(inp_rows)
    basis_high = jnp.concatenate([tabh[...], rows_high], axis=0)
    basis_low = jnp.concatenate([tabl[...], rows_low], axis=0)
    hidden = mm(own_feat, basis_high) + mm(own_feat, basis_low)
    hid_ref[...] = hidden
    center = hidden - jnp.mean(hidden, axis=1, keepdims=True)
    variance = jnp.mean(center * center, axis=1, keepdims=True)
    std = jnp.broadcast_to(jnp.sqrt(variance + EPSILON), (TOK, TOK)).T[0:1, :]
    std_high = std.astype(BF16).astype(F32)
    stage[12:13, :] = std_high
    stage[13:14, :] = std - std_high
    gath[me] = stage[...].astype(BF16)

    def g_copy(dx, dz):
        return pltpu.make_async_remote_copy(
            src_ref=gath.at[me], dst_ref=gath.at[me], send_sem=gs_sem.at[dx, dz], recv_sem=gr_sem.at[dx, dz],
            device_id={"seq": ahead(dx, dz)}, device_id_type=mesh_ids)

    pl.semaphore_wait(barrier, N_SEQ)
    for dx, dz in NEAR_FIRST:
        g_copy(dx, dz).start()

    own_rows = jnp.broadcast_to(own_ref[...], (TOK, TOK)).astype(F32)
    own_cols = own_rows.T
    earlier = (own_rows == own_cols) & (iota((TOK, TOK), 0) < iota((TOK, TOK), 1))
    rank = jnp.sum(jnp.where(earlier, 1.0, 0.0), axis=0, keepdims=True)
    ranked[...] = jnp.where(rank == ((iota((TOK, TOK), 0) // LAT) % CAP).astype(F32), 1.0, 0.0)
    own96 = jnp.broadcast_to(own_ref[...], (3 * N_SEQ, TOK))
    owner = iota((3 * N_SEQ, TOK), 0)
    owner = jnp.where(owner < N_SEQ, owner, jnp.where(owner < 2 * N_SEQ, owner - N_SEQ - 1, owner - 2 * N_SEQ + 1))
    dispatch[...] = jnp.where(own96 == owner, 1.0, 0.0).astype(BF16)

    scale1 = 1.0 + mod_ref[1]
    normed = (center * lax.rsqrt(variance + EPSILON) * scale1 + mod_ref[0]).astype(BF16)
    for axis in range(3):
        rows = slice(axis * RES, (axis + 1) * RES)
        scaled[rows, :] = ((tabh[rows, :].astype(F32) + tabl[rows, :].astype(F32)) * scale1).astype(BF16)
    shift_rows = jnp.where(iota((8, D), 0) < 2, jnp.broadcast_to(mod_ref[0], (8, D)), 0.0)
    scaled[3 * RES :, :] = jnp.concatenate([inp * scale1, shift_rows, jnp.zeros((48, D), F32)], axis=0).astype(BF16)
    loads[10].wait()
    queries = mm(normed, wqkv[:, 0:HW])
    per_head = jnp.where(iota((HW, HW), 0) // HEAD == iota((HW, HW), 1) // HEAD, 1.0 / HEAD, 0.0).astype(BF16)
    mean_sq = mm((queries * queries).astype(BF16), per_head)
    queries = queries * lax.rsqrt(mean_sq + EPSILON) * (
        gain_ref[0:1, :] * gain_ref[1:2, :] * (HEAD ** (-0.5) * LOG2E))
    bkt[...] = mm(scaled[...], wqkv[:, HW : 2 * HW]).T.astype(BF16)
    first_half = iota((TOK, 2 * HEAD), 1) < HEAD
    for two in range(HEADS // 2):
        columns = slice(two * 2 * HEAD, (two + 1) * 2 * HEAD)
        both = queries[:, columns]
        mine = jnp.concatenate([jnp.where(first_half, both, 0.0), jnp.where(first_half, 0.0, both)], axis=0)
        umat[two * 256 : (two + 1) * 256, :] = mm(mine.astype(BF16), bkt[columns, :]).astype(BF16)
    bv[...] = mm(scaled[...], wqkv[:, 2 * HW : 3 * HW]).astype(BF16)
    head_scaled = head_ref[...] * (1.0 + mod_ref[4])
    hp_high[...], hp_low[...] = split(head_scaled)
    hp_const[...] = jnp.broadcast_to(jnp.sum(head_ref[...] * mod_ref[3], axis=1, keepdims=True), (LAT, TOK))
    loads[12].start()
    loads[13].start()

    def features(number):
        sources = []
        for dz in TILES[number]:
            for dx in range(NX):
                source = behind(dx, dz)
                sources.append(source)
                if dx > 0 or dz > 0:
                    pltpu.make_async_remote_copy(
                        src_ref=gath.at[source], dst_ref=gath.at[source], send_sem=gs_sem.at[dx, dz],
                        recv_sem=gr_sem.at[dx, dz], device_id={"seq": me}, device_id_type=mesh_ids).wait_recv()
        width = TOK * len(sources)
        rows = jnp.concatenate([gath[source].astype(F32) for source in sources], axis=1)
        std_high, std_low = rows[12:13, :], rows[13:14, :]
        std = std_high + std_low
        inv_std = 1.0 / std
        which = iota((8, width), 0)
        ids = iota((RES, width), 0).astype(F32)
        ft, fs = ft_ref.at[number % 2], fs_ref.at[number % 2]
        for c in range(3):
            hit = ids == rows[8 + c : 9 + c, :]
            ft[c * RES : (c + 1) * RES, 0:width] = jnp.where(hit, 1.0, 0.0).astype(BF16)
            fs[c * RES : (c + 1) * RES, 0:width] = jnp.where(hit, inv_std, 0.0).astype(BF16)
        std_rows = jnp.where(which == 0, std_high, jnp.where(which == 1, std_low, 0.0))
        pad = jnp.zeros((48, width), F32)
        ft[3 * RES :, 0:width] = jnp.concatenate([rows[0:8, :], std_rows, pad], axis=0).astype(BF16)
        fs[3 * RES :, 0:width] = jnp.concatenate(
            [rows[0:8, :] * inv_std, jnp.where(which == 0, 1.0, 0.0), pad], axis=0).astype(BF16)
        return width, EPSILON * (std * std)

    width, eps_var = features(0)
    for number in range(len(TILES)):
        ft, fs = ft_ref[number % 2, :, 0:width], fs_ref[number % 2, :, 0:width]
        used, used_var = width, eps_var
        keys = mm(bkt[...], ft)
        scores = mm(umat[...], ft)
        for head in range(HEADS):
            keys_h = keys[head * HEAD : (head + 1) * HEAD, :]
            mean_h = jnp.sum(keys_h * keys_h, axis=0, keepdims=True) * (1.0 / HEAD)
            inv = lax.rsqrt(mean_h + used_var)
            p_ref[head * TOK : (head + 1) * TOK, 0:used] = jnp.exp2(
                scores[head * TOK : (head + 1) * TOK, :] * inv).astype(BF16)
        if number + 1 < len(TILES):
            width, eps_var = features(number + 1)
        found = mm_nt(p_ref[:, 0:used], fs)
        if number > 0:
            found += acc[...]
        acc[...] = found

    loads[11].wait()
    lane = iota((TOK, FEAT), 1)
    pieces = []
    for two in range(HEADS // 2):
        columns = slice(two * 2 * HEAD, (two + 1) * 2 * HEAD)
        halves = []
        for odd in range(2):
            head = 2 * two + odd
            total = acc[head * TOK : (head + 1) * TOK, :]
            denom = jnp.sum(jnp.where(lane == 200, total, 0.0), axis=1, keepdims=True)
            halves.append((total * (1.0 / denom)).astype(BF16))
        found = mm(jnp.concatenate(halves, axis=0), bv[:, columns])
        pieces.append(jnp.where(first_half, found[0:TOK, :], found[TOK : 2 * TOK, :]))
    attended = jnp.concatenate(pieces, axis=1).astype(BF16)
    width = 256
    total = jnp.zeros((TOK, 1), F32)
    for part in range(D // width):
        columns = slice(part * width, (part + 1) * width)
        piece = hid_ref[:, columns] + mod_ref[2][:, columns] * mm(attended, wout[:, columns])
        hid_ref[:, columns] = piece
        total = total + jnp.sum(piece, axis=1, keepdims=True)
    mean = total * (1.0 / D)
    square = jnp.zeros((TOK, 1), F32)
    velocity = jnp.zeros((LAT, TOK), F32)
    for part in range(D // width):
        columns = slice(part * width, (part + 1) * width)
        center = hid_ref[:, columns] - mean
        square = square + jnp.sum(center * center, axis=1, keepdims=True)
        c_high, c_low = split(center)
        velocity = velocity + (mm_nt(hp_high[:, columns], c_high)
                               + (mm_nt(hp_high[:, columns], c_low) + mm_nt(hp_low[:, columns], c_high)))
    inv_dev = jnp.broadcast_to(lax.rsqrt(square * (1.0 / D) + EPSILON), (TOK, TOK)).T[0:1, :]
    velocity = velocity * inv_dev + hp_const[...]

    is_cond = pair == 0
    share = jnp.where(is_cond, 1.0, 0.0) * lat_ref[...] + (
        step_ref[0] * jnp.where(is_cond, -GUIDANCE, GUIDANCE - 1.0)) * velocity
    wide = jnp.concatenate([share] * (TOK // LAT), axis=0) * ranked[...]
    wide_high, wide_low = split(wide)
    packed = mm_nt(dispatch[...], wide_high) + mm_nt(dispatch[...], wide_low)
    sendbuf[:, 0, :] = jnp.where(
        iota((N_SEQ, TOK), 1) < LAT * CAP, packed[0:N_SEQ, :], packed[N_SEQ : 2 * N_SEQ, :])
    sendbuf[:, 1, :] = packed[2 * N_SEQ :, :]

    def a_copy(core, dx, dz):
        dest = ahead(dx, dz)
        return pltpu.make_async_remote_copy(
            src_ref=sendbuf.at[dest], dst_ref=rbuf.at[pair, me], send_sem=as_sem.at[core, dx, dz],
            recv_sem=ar_sem.at[core, dx, dz], device_id={"pair": pair if core == 0 else other, "seq": dest},
            device_id_type=mesh_ids)

    def a_arrival(core, dx, dz):
        source = behind(dx, dz)
        return pltpu.make_async_remote_copy(
            src_ref=sendbuf.at[source], dst_ref=rbuf.at[pair if core == 0 else other, source],
            send_sem=as_sem.at[core, dx, dz], recv_sem=ar_sem.at[core, dx, dz], device_id={"seq": me},
            device_id_type=mesh_ids)

    far_first = [(core, dx, dz) for dx, dz in reversed(NEAR_FIRST) for core in range(2)] + [(1, 0, 0)]
    for core, dx, dz in far_first:
        a_copy(core, dx, dz).start()
    keep = pltpu.make_async_copy(sendbuf.at[me], rbuf.at[pair, me], lsem.at[14])
    keep.start()
    for dx, dz in NEAR_FIRST:
        g_copy(dx, dz).wait_send()

    lower = jnp.maximum(me - 1, 0)
    upper = jnp.minimum(me + 1, N_SEQ - 1)
    nb_ref[0:1, :] = gath[lower].astype(F32)[11:12, :]
    nb_ref[1:2, :] = gath[upper].astype(F32)[11:12, :]
    nb_ref[2:8, :] = jnp.zeros((6, TOK), F32)
    loads[12].wait()
    index = km_ref[...]
    index = jnp.where(index < SLOTS, ((index & (CAP - 1)) << 5) + (index >> 3), index)
    spot_ref[...] = index & (TOK - 1)
    chunk_ref[...] = index >> 7
    near_ref[...] = jnp.minimum(index, 300).astype(F32)
    far_ref[...] = jnp.where(index >= SLOTS, jnp.minimum(index - SLOTS, 300), 300).astype(F32)
    loads[13].wait()
    keep.wait()
    for core, dx, dz in far_first:
        a_arrival(core, dx, dz).wait()
    x_ref[...] = rbuf[0] + rbuf[1]


TRIPLE = 3
PARTS = KOFF // TRIPLE
BLOCKS = FINE // TOK
SHARED = 0


def conv_kernel(
    x_ref, nb_ref, wt, spot_ref, chunk_ref, near_ref, far_ref, dproj_hbm, owned_ref, dec_ref, dproj_ref, feats, prod_a,
    prod_b, acc_x, acc_m, lsem
):
    load = pltpu.make_async_copy(dproj_hbm, dproj_ref, lsem)
    load.start()
    x0 = x_ref[:, 0, :]
    x1 = x_ref[:, 1, :]

    pick = jnp.where(iota((N_SEQ, SLOTS), 1) // CAP == iota((N_SEQ, SLOTS), 0), 1.0, 0.0).astype(BF16)
    xt_high, xt_low = split(x0.T)
    spread = mm(xt_high, pick) + mm(xt_low, pick)
    spread = jnp.where(iota((TOK, SLOTS), 1) % CAP == iota((TOK, SLOTS), 0) // LAT, spread, 0.0)
    owned = spread[0:LAT, :]
    for rank in range(1, CAP):
        owned = owned + spread[rank * LAT : (rank + 1) * LAT, :]
    owned_ref[...] = owned

    lane = iota((SLOTS, TOK), 1)
    own_rows = jnp.where(lane // LAT == iota((SLOTS, TOK), 0) // N_SEQ, jnp.concatenate([x0] * CAP, axis=0), 0.0)
    sub = iota((HALO, TOK), 0)
    lane = iota((HALO, TOK), 1)
    parts = [own_rows]
    for side, x_side in ((0, x0), (1, x1)):
        blocks = jnp.broadcast_to(nb_ref[side : side + 1, :], (HALO, TOK))
        first = 8 if side == 0 else 0
        chosen = jnp.sum(jnp.where(lane == sub // BLK + first, blocks, 0.0), axis=1, keepdims=True)
        source = chosen * (BLK // CAP) + ((iota((HALO, 1), 0) % BLK) // CAP).astype(F32)
        pick = jnp.where(iota((HALO, N_SEQ), 1).astype(F32) == source, 1.0, 0.0).astype(BF16)
        x_high, x_low = split(x_side)
        rows = mm(pick, x_high) + mm(pick, x_low)
        offset = CAP if side == 0 else 0
        parts.append(jnp.where(lane // LAT == sub % CAP + offset, rows, 0.0))
    l_high, l_low = split(jnp.concatenate(parts, axis=0))
    load.wait()
    p_high, p_low = split(dproj_ref[...])
    p_high = jnp.concatenate([p_high.astype(F32)] * (TOK // LAT), axis=0).astype(BF16)
    p_low = jnp.concatenate([p_low.astype(F32)] * (TOK // LAT), axis=0).astype(BF16)
    value = mm(jnp.concatenate([l_high, l_low], axis=1), jnp.concatenate([p_high, p_high], axis=0)) + mm(l_high, p_low)
    half = value * 0.5
    feats[...] = (half * jnp.tanh(half) + half).astype(BF16)
    acc_x[...] = jnp.zeros((OUT_DEV, FINE), F32)
    acc_m[...] = jnp.zeros((OUT_DEV, FINE), F32)

    def product(part, half, target):
        rows = pl.ds(pl.multiple_of(part * (TRIPLE * OUT_DEV), TRIPLE * OUT_DEV), TRIPLE * OUT_DEV)
        table = slice(half * SLOTS, (half + 1) * SLOTS)
        target[:, table] = mm_nt(wt[rows, :], feats[table, :])

    def by_gather(number, source, block):
        columns = slice(block * TOK, (block + 1) * TOK)
        spot = jnp.broadcast_to(spot_ref[number, block : block + 1, :], (OUT_DEV, TOK))
        chunk = jnp.broadcast_to(chunk_ref[number, block : block + 1, :], (OUT_DEV, TOK))
        value = jnp.zeros((OUT_DEV, TOK), F32)
        for c in range(4):
            found = jnp.take_along_axis(source[:, c * TOK : (c + 1) * TOK], spot, axis=1, mode="promise_in_bounds")
            value = jnp.where(chunk == c, found, value)
        acc_x[:, columns] += value

    first_ids = iota((16, TOK), 0).astype(F32).astype(BF16)

    def hot_rows(number, blocks):
        columns = []
        for block in blocks:
            rows = []
            for which in (near_ref, far_ref):
                row = jnp.broadcast_to(which[number, block : block + 1, :], (16, TOK)).astype(BF16) - first_ids
                for j in range(SLOTS // 16):
                    rows.append(jnp.where(row == jnp.bfloat16(16 * j), jnp.bfloat16(1), jnp.bfloat16(0)))
            columns.append(jnp.concatenate(rows, axis=0))
        return jnp.concatenate(columns, axis=1)

    def pick_rows(part, source, target):
        first = part * TRIPLE
        for quarter in range(4):
            blocks = (2 * quarter, 2 * quarter + 1)
            columns = slice(quarter * 2 * TOK, (quarter + 1) * 2 * TOK)
            if target is not None and quarter % 2 == 0:
                product(part + 1, quarter // 2, target)
            found = mm(source[2 * OUT_DEV :, :].astype(BF16), hot_rows(first + 2, blocks))
            if quarter >= SHARED:
                found += mm(source[OUT_DEV : 2 * OUT_DEV, :].astype(BF16), hot_rows(first + 1, blocks))
            acc_m[:, columns] += found
            for block in blocks:
                by_gather(first, source.at[0:OUT_DEV], block)
                if quarter < SHARED:
                    by_gather(first + 1, source.at[OUT_DEV : 2 * OUT_DEV], block)

    for half in range(2):
        product(0, half, prod_a)

    def two_parts(i, carry):
        pick_rows(2 * i, prod_a, prod_b)
        pick_rows(2 * i + 1, prod_b, prod_a)
        return carry

    lax.fori_loop(0, PARTS // 2, two_parts, 0)
    pick_rows(PARTS - 1, prod_a, None)
    dec_ref[...] = (acc_x[...] + acc_m[...]).astype(BF16)


def vmem(count):
    return [pl.BlockSpec(memory_space=pltpu.VMEM)] * count


def in_hbm(*arrays):
    return [pltpu.with_memory_space_constraint(array, pltpu.HBM) for array in arrays]


def hbm(count):
    return [pl.BlockSpec(memory_space=pltpu.HBM)] * count


def per_device(
    latents, voxel_coords, owner_map, step_time, modulation, in_proj, qkv_proj, norm_gain, out_proj, head_proj,
    decoder_projection, border_blocks, kernel_map, conv_weight,
):
    table = centred_position_table()
    table_high = table.astype(jnp.bfloat16)
    table_low = (table - table_high.astype(np.float32)).astype(jnp.bfloat16)
    dma = pltpu.SemaphoreType.DMA
    conv_table = jax.ShapeDtypeStruct((KOFF, BLOCKS, TOK), jnp.int32)
    conv_row = jax.ShapeDtypeStruct((KOFF, BLOCKS, TOK), F32)
    handed = pl.pallas_call(
        flow_kernel,
        out_shape=(
            jax.ShapeDtypeStruct((N_SEQ, 2, TOK), F32), jax.ShapeDtypeStruct((8, TOK), F32),
            jax.ShapeDtypeStruct((KOFF * OUT_DEV, DEC), BF16), conv_table, conv_table, conv_row, conv_row),
        in_specs=hbm(3) + [pl.BlockSpec(memory_space=pltpu.SMEM)] + hbm(11),
        out_specs=tuple(vmem(7)),
        scratch_shapes=[
            pltpu.VMEM((LAT, TOK), F32),
            pltpu.VMEM((3, 1, TOK), jnp.int32),
            pltpu.VMEM((1, TOK), jnp.int32),
            pltpu.VMEM((5, 1, D), F32),
            pltpu.VMEM((LAT, D), F32),
            pltpu.VMEM((2, HW), F32),
            pltpu.VMEM((LAT, D), F32),
            pltpu.VMEM((2, 8), jnp.int32),
            pltpu.VMEM((3 * RES, D), BF16),
            pltpu.VMEM((3 * RES, D), BF16),
            pltpu.VMEM((D, 3 * HW), BF16),
            pltpu.VMEM((HW, D), BF16),
            pltpu.VMEM((KOFF, BLOCKS, TOK), jnp.int32),
            pltpu.VMEM((N_SEQ, 16, TOK), BF16),
            pltpu.VMEM((16, TOK), F32),
            pltpu.VMEM((FEAT, D), BF16),
            pltpu.VMEM((HW, FEAT), BF16),
            pltpu.VMEM((FEAT, HW), BF16),
            pltpu.VMEM((HEADS * TOK, FEAT), BF16),
            pltpu.VMEM((TOK, D), F32),
            pltpu.VMEM((2, FEAT, 2 * GROUP), BF16),
            pltpu.VMEM((2, FEAT, 2 * GROUP), BF16),
            pltpu.VMEM((HEADS * TOK, 2 * GROUP), BF16),
            pltpu.VMEM((HEADS * TOK, FEAT), F32),
            pltpu.VMEM((LAT, D), BF16),
            pltpu.VMEM((LAT, D), BF16),
            pltpu.VMEM((LAT, TOK), F32),
            pltpu.VMEM((TOK, TOK), F32),
            pltpu.VMEM((3 * N_SEQ, TOK), BF16),
            pltpu.VMEM((N_SEQ, 2, TOK), F32),
            pltpu.VMEM((2, N_SEQ, 2, TOK), F32),
            dma((15,)), dma((NX, NZ)), dma((NX, NZ)), dma((2, NX, NZ)), dma((2, NX, NZ)),
        ],
        compiler_params=pltpu.CompilerParams(collective_id=0, has_side_effects=True, vmem_limit_bytes=40 << 20),
        name="flow",
    )(*in_hbm(
        latents[0], jnp.transpose(voxel_coords, (1, 0, 2)), owner_map.reshape(1, TOK)), step_time, *in_hbm(
        modulation.reshape(5, 1, D), in_proj, norm_gain, head_proj.T, border_blocks[0, 0], jnp.asarray(table_high),
        jnp.asarray(table_low), qkv_proj, out_proj,
        jnp.swapaxes(conv_weight, 1, 2).reshape(KOFF * OUT_DEV, DEC), kernel_map.reshape(KOFF, BLOCKS, TOK)),
    )
    owned, decoded = pl.pallas_call(
        conv_kernel,
        out_shape=(jax.ShapeDtypeStruct((LAT, SLOTS), F32), jax.ShapeDtypeStruct((OUT_DEV, FINE), BF16)),
        in_specs=vmem(7) + hbm(1),
        out_specs=tuple(vmem(2)),
        scratch_shapes=[
            pltpu.VMEM((LAT, DEC), F32),
            pltpu.VMEM((2 * SLOTS, DEC), BF16),
            pltpu.VMEM((TRIPLE * OUT_DEV, 2 * SLOTS), F32),
            pltpu.VMEM((TRIPLE * OUT_DEV, 2 * SLOTS), F32),
            pltpu.VMEM((OUT_DEV, FINE), F32),
            pltpu.VMEM((OUT_DEV, FINE), F32),
            dma,
        ],
        compiler_params=pltpu.CompilerParams(vmem_limit_bytes=40 << 20),
        name="conv",
    )(*handed, *in_hbm(decoder_projection))
    return owned[None, None], decoded.T[None, None]


def solution(mesh):
    placed = (
        P("asset", None, "seq"),
        P("asset", None, "seq"),
        P("asset", "seq", None),
        P("asset"),
        P("asset", "pair", None, None),
        P(),
        P(),
        P(),
        P(),
        P(),
        P(),
        P("asset", "seq", None, None),
        P("asset", "seq", None, None),
        P(None, None, "pair"),
    )
    return jax.shard_map(
        per_device,
        mesh=mesh,
        in_specs=placed,
        out_specs=(P("asset", "seq", None, None), P("asset", "seq", None, "pair")),
        check_vma=False,
    )
```

```python
import math

import jax
import jax.numpy as jnp
import numpy as np
from jax import lax
from jax.experimental import pallas as pl
from jax.experimental.pallas import tpu as pltpu
from jax.sharding import PartitionSpec as P

D = 1024
HEADS = 8
HEAD = 64
LAT = 8
DEC = 768
KOFF = 27
BLK = 16
RES = 64
TOK = 128
CAP = 8
SLOTS = 256
HALO = 128
FINE = 1024
HW = 512
NX = 4
NZ = 8
N_SEQ = 32
OUT_DEV = 96
GROUP = NX * TOK
FEAT = 256
TILES = ((0,), (1, 7), (2, 6), (3, 5), (4,))
NEAR_FIRST = tuple((dx, dz) for tile in TILES for dx in (0, 1, 3, 2) for dz in tile if dx or dz)
EPSILON = 1e-06
GUIDANCE = 3.0
LOG2E = 1.4426950408889634
F32 = jnp.float32
BF16 = jnp.bfloat16


def centred_position_table():
    freqs = D // 6
    omegas = np.exp(-math.log(10000.0) * (np.arange(freqs) / freqs))
    angles = np.arange(RES)[:, None] * omegas[None, :]
    halves = np.concatenate([np.sin(angles), np.cos(angles)], axis=1)
    table = np.zeros((3 * RES, D))
    for axis in range(3):
        table[axis * RES : (axis + 1) * RES, axis * 2 * freqs : (axis + 1) * 2 * freqs] = halves
    return (table - table.mean(axis=1, keepdims=True)).astype(np.float32)


def split(values):
    high = values.astype(BF16)
    return high, (values - high.astype(F32)).astype(BF16)


def mm(a, b):
    return lax.dot_general(a, b, (((1,), (0,)), ((), ())), preferred_element_type=F32)


def mm_nt(a, b):
    return lax.dot_general(a, b, (((1,), (1,)), ((), ())), preferred_element_type=F32)


def iota(shape, dim):
    return lax.broadcasted_iota(jnp.int32, shape, dim)


def one_hots(rows, width):
    ids = iota((RES, width), 0).astype(F32)
    return [jnp.where(ids == rows[c : c + 1, :], 1.0, 0.0) for c in range(3)]


def flow_kernel(
    lat_hbm, coord_hbm, own_hbm, step_ref, mod_hbm, inp_hbm, gain_hbm, head_hbm, bb_hbm, tabh_hbm, tabl_hbm, wqkv_hbm,
    wout_hbm, wt_hbm, km_hbm, dproj_hbm,
    x_ref, pick_ref, wt_ref, spot_ref, chunk_ref, near_ref, far_ref, dh_ref, dl_ref,
    lat_ref, coord_ref, own_ref, mod_ref, inp_ref, gain_ref, head_ref, bb_ref, tabh, tabl, wqkv, wout, km_ref, dproj_ref,
    gath, stage, scaled, bkt, bv, umat, hid_ref, ft_ref, fs_ref, p_ref, acc, hp_high, hp_low, hp_const, ranked, dispatch,
    sendbuf, rbuf,
    lsem, gs_sem, gr_sem, as_sem, ar_sem,
):
    me = lax.axis_index("seq")
    pair = lax.axis_index("pair")
    other = 1 - pair
    x_me = me // NZ
    z_me = me % NZ
    mesh_ids = pl.DeviceIdType.MESH

    def ahead(dx, dz):
        return ((x_me + dx) % NX) * NZ + (z_me + dz) % NZ

    def behind(dx, dz):
        return ((x_me + NX - dx) % NX) * NZ + (z_me + NZ - dz) % NZ

    loads = [
        pltpu.make_async_copy(source, target, lsem.at[number])
        for number, (source, target) in enumerate((
            (lat_hbm, lat_ref), (coord_hbm, coord_ref), (own_hbm, own_ref), (mod_hbm, mod_ref), (inp_hbm, inp_ref),
            (gain_hbm, gain_ref), (head_hbm, head_ref), (bb_hbm, bb_ref), (tabh_hbm, tabh), (tabl_hbm, tabl),
            (wqkv_hbm, wqkv), (wout_hbm, wout), (km_hbm, km_ref), (wt_hbm, wt_ref), (dproj_hbm, dproj_ref)))
    ]
    for load in loads[:12]:
        load.start()

    barrier = pltpu.get_barrier_semaphore()
    for dx, dz in reversed(NEAR_FIRST):
        pl.semaphore_signal(barrier, inc=1, device_id={"seq": ahead(dx, dz)}, device_id_type=mesh_ids)
    pl.semaphore_signal(barrier, inc=1, device_id={"pair": other}, device_id_type=mesh_ids)
    for load in loads[:10]:
        load.wait()

    lat = lat_ref[...]
    stage[...] = jnp.zeros((16, TOK), F32)
    stage[0:8, :] = lat
    for axis in range(3):
        stage[8 + axis : 9 + axis, :] = coord_ref[axis].astype(F32)
    stage[11:12, 0:8] = bb_ref[0:1, :].astype(F32)
    stage[11:12, 8:16] = bb_ref[1:2, :].astype(F32)
    lat_high = lat.astype(BF16).astype(F32)
    zero8 = jnp.zeros((8, TOK), F32)
    own_feat = jnp.concatenate(
        one_hots(stage[8:11, :], TOK) + [lat_high, zero8, lat - lat_high, jnp.zeros((40, TOK), F32)], axis=0)
    own_feat = own_feat.T.astype(BF16)
    inp = inp_ref[...]
    inp = inp - jnp.mean(inp, axis=1, keepdims=True)
    inp_rows = jnp.concatenate([inp, jnp.zeros((8, D), F32), inp, jnp.zeros((40, D), F32)], axis=0)
    rows_high, rows_low = split(inp_rows)
    basis_high = jnp.concatenate([tabh[...], rows_high], axis=0)
    basis_low = jnp.concatenate([tabl[...], rows_low], axis=0)
    hidden = mm(own_feat, basis_high) + mm(own_feat, basis_low)
    hid_ref[...] = hidden
    center = hidden - jnp.mean(hidden, axis=1, keepdims=True)
    variance = jnp.mean(center * center, axis=1, keepdims=True)
    std = jnp.broadcast_to(jnp.sqrt(variance + EPSILON), (TOK, TOK)).T[0:1, :]
    std_high = std.astype(BF16).astype(F32)
    stage[12:13, :] = std_high
    stage[13:14, :] = std - std_high
    gath[me] = stage[...].astype(BF16)

    def g_copy(dx, dz):
        return pltpu.make_async_remote_copy(
            src_ref=gath.at[me], dst_ref=gath.at[me], send_sem=gs_sem.at[dx, dz], recv_sem=gr_sem.at[dx, dz],
            device_id={"seq": ahead(dx, dz)}, device_id_type=mesh_ids)

    pl.semaphore_wait(barrier, N_SEQ)
    for dx, dz in NEAR_FIRST:
        g_copy(dx, dz).start()

    own_rows = jnp.broadcast_to(own_ref[...], (TOK, TOK)).astype(F32)
    own_cols = own_rows.T
    earlier = (own_rows == own_cols) & (iota((TOK, TOK), 0) < iota((TOK, TOK), 1))
    rank = jnp.sum(jnp.where(earlier, 1.0, 0.0), axis=0, keepdims=True)
    ranked[...] = jnp.where(rank == ((iota((TOK, TOK), 0) // LAT) % CAP).astype(F32), 1.0, 0.0)
    own96 = jnp.broadcast_to(own_ref[...], (3 * N_SEQ, TOK))
    owner = iota((3 * N_SEQ, TOK), 0)
    owner = jnp.where(owner < N_SEQ, owner, jnp.where(owner < 2 * N_SEQ, owner - N_SEQ - 1, owner - 2 * N_SEQ + 1))
    dispatch[...] = jnp.where(own96 == owner, 1.0, 0.0).astype(BF16)

    scale1 = 1.0 + mod_ref[1]
    normed = (center * lax.rsqrt(variance + EPSILON) * scale1 + mod_ref[0]).astype(BF16)
    for axis in range(3):
        rows = slice(axis * RES, (axis + 1) * RES)
        scaled[rows, :] = ((tabh[rows, :].astype(F32) + tabl[rows, :].astype(F32)) * scale1).astype(BF16)
    shift_rows = jnp.where(iota((8, D), 0) < 2, jnp.broadcast_to(mod_ref[0], (8, D)), 0.0)
    scaled[3 * RES :, :] = jnp.concatenate([inp * scale1, shift_rows, jnp.zeros((48, D), F32)], axis=0).astype(BF16)
    loads[10].wait()
    queries = mm(normed, wqkv[:, 0:HW])
    per_head = jnp.where(iota((HW, HW), 0) // HEAD == iota((HW, HW), 1) // HEAD, 1.0 / HEAD, 0.0).astype(BF16)
    mean_sq = mm((queries * queries).astype(BF16), per_head)
    queries = queries * lax.rsqrt(mean_sq + EPSILON) * (
        gain_ref[0:1, :] * gain_ref[1:2, :] * (HEAD ** (-0.5) * LOG2E))
    bkt[...] = mm(scaled[...], wqkv[:, HW : 2 * HW]).T.astype(BF16)
    first_half = iota((TOK, 2 * HEAD), 1) < HEAD
    for two in range(HEADS // 2):
        columns = slice(two * 2 * HEAD, (two + 1) * 2 * HEAD)
        both = queries[:, columns]
        mine = jnp.concatenate([jnp.where(first_half, both, 0.0), jnp.where(first_half, 0.0, both)], axis=0)
        umat[two * 256 : (two + 1) * 256, :] = mm(mine.astype(BF16), bkt[columns, :]).astype(BF16)
    bv[...] = mm(scaled[...], wqkv[:, 2 * HW : 3 * HW]).astype(BF16)
    head_scaled = head_ref[...] * (1.0 + mod_ref[4])
    hp_high[...], hp_low[...] = split(head_scaled)
    hp_const[...] = jnp.broadcast_to(jnp.sum(head_ref[...] * mod_ref[3], axis=1, keepdims=True), (LAT, TOK))
    for load in loads[12:]:
        load.start()

    def features(number):
        sources = []
        for dz in TILES[number]:
            for dx in range(NX):
                source = behind(dx, dz)
                sources.append(source)
                if dx > 0 or dz > 0:
                    pltpu.make_async_remote_copy(
                        src_ref=gath.at[source], dst_ref=gath.at[source], send_sem=gs_sem.at[dx, dz],
                        recv_sem=gr_sem.at[dx, dz], device_id={"seq": me}, device_id_type=mesh_ids).wait_recv()
        width = TOK * len(sources)
        rows = jnp.concatenate([gath[source].astype(F32) for source in sources], axis=1)
        std_high, std_low = rows[12:13, :], rows[13:14, :]
        std = std_high + std_low
        inv_std = 1.0 / std
        which = iota((8, width), 0)
        ids = iota((RES, width), 0).astype(F32)
        ft, fs = ft_ref.at[number % 2], fs_ref.at[number % 2]
        for c in range(3):
            hit = ids == rows[8 + c : 9 + c, :]
            ft[c * RES : (c + 1) * RES, 0:width] = jnp.where(hit, 1.0, 0.0).astype(BF16)
            fs[c * RES : (c + 1) * RES, 0:width] = jnp.where(hit, inv_std, 0.0).astype(BF16)
        std_rows = jnp.where(which == 0, std_high, jnp.where(which == 1, std_low, 0.0))
        pad = jnp.zeros((48, width), F32)
        ft[3 * RES :, 0:width] = jnp.concatenate([rows[0:8, :], std_rows, pad], axis=0).astype(BF16)
        fs[3 * RES :, 0:width] = jnp.concatenate(
            [rows[0:8, :] * inv_std, jnp.where(which == 0, 1.0, 0.0), pad], axis=0).astype(BF16)
        return width, EPSILON * (std * std)

    width, eps_var = features(0)
    for number in range(len(TILES)):
        ft, fs = ft_ref[number % 2, :, 0:width], fs_ref[number % 2, :, 0:width]
        used, used_var = width, eps_var
        keys = mm(bkt[...], ft)
        scores = mm(umat[...], ft)
        for head in range(HEADS):
            keys_h = keys[head * HEAD : (head + 1) * HEAD, :]
            mean_h = jnp.sum(keys_h * keys_h, axis=0, keepdims=True) * (1.0 / HEAD)
            inv = lax.rsqrt(mean_h + used_var)
            p_ref[head * TOK : (head + 1) * TOK, 0:used] = jnp.exp2(
                scores[head * TOK : (head + 1) * TOK, :] * inv).astype(BF16)
        if number + 1 < len(TILES):
            width, eps_var = features(number + 1)
        found = mm_nt(p_ref[:, 0:used], fs)
        if number > 0:
            found += acc[...]
        acc[...] = found

    loads[11].wait()
    lane = iota((TOK, FEAT), 1)
    pieces = []
    for two in range(HEADS // 2):
        columns = slice(two * 2 * HEAD, (two + 1) * 2 * HEAD)
        halves = []
        for odd in range(2):
            head = 2 * two + odd
            total = acc[head * TOK : (head + 1) * TOK, :]
            denom = jnp.sum(jnp.where(lane == 200, total, 0.0), axis=1, keepdims=True)
            halves.append((total * (1.0 / denom)).astype(BF16))
        found = mm(jnp.concatenate(halves, axis=0), bv[:, columns])
        pieces.append(jnp.where(first_half, found[0:TOK, :], found[TOK : 2 * TOK, :]))
    attended = jnp.concatenate(pieces, axis=1).astype(BF16)
    width = 256
    total = jnp.zeros((TOK, 1), F32)
    for part in range(D // width):
        columns = slice(part * width, (part + 1) * width)
        piece = hid_ref[:, columns] + mod_ref[2][:, columns] * mm(attended, wout[:, columns])
        hid_ref[:, columns] = piece
        total = total + jnp.sum(piece, axis=1, keepdims=True)
    mean = total * (1.0 / D)
    square = jnp.zeros((TOK, 1), F32)
    velocity = jnp.zeros((LAT, TOK), F32)
    for part in range(D // width):
        columns = slice(part * width, (part + 1) * width)
        center = hid_ref[:, columns] - mean
        square = square + jnp.sum(center * center, axis=1, keepdims=True)
        c_high, c_low = split(center)
        velocity = velocity + (mm_nt(hp_high[:, columns], c_high)
                               + (mm_nt(hp_high[:, columns], c_low) + mm_nt(hp_low[:, columns], c_high)))
    inv_dev = jnp.broadcast_to(lax.rsqrt(square * (1.0 / D) + EPSILON), (TOK, TOK)).T[0:1, :]
    velocity = velocity * inv_dev + hp_const[...]

    is_cond = pair == 0
    share = jnp.where(is_cond, 1.0, 0.0) * lat_ref[...] + (
        step_ref[0] * jnp.where(is_cond, -GUIDANCE, GUIDANCE - 1.0)) * velocity
    wide = jnp.concatenate([share] * (TOK // LAT), axis=0) * ranked[...]
    wide_high, wide_low = split(wide)
    packed = mm_nt(dispatch[...], wide_high) + mm_nt(dispatch[...], wide_low)
    sendbuf[:, 0, :] = jnp.where(
        iota((N_SEQ, TOK), 1) < LAT * CAP, packed[0:N_SEQ, :], packed[N_SEQ : 2 * N_SEQ, :])
    sendbuf[:, 1, :] = packed[2 * N_SEQ :, :]

    def a_copy(core, dx, dz):
        dest = ahead(dx, dz)
        return pltpu.make_async_remote_copy(
            src_ref=sendbuf.at[dest], dst_ref=rbuf.at[pair, me], send_sem=as_sem.at[core, dx, dz],
            recv_sem=ar_sem.at[core, dx, dz], device_id={"pair": pair if core == 0 else other, "seq": dest},
            device_id_type=mesh_ids)

    def a_arrival(core, dx, dz):
        source = behind(dx, dz)
        return pltpu.make_async_remote_copy(
            src_ref=sendbuf.at[source], dst_ref=rbuf.at[pair if core == 0 else other, source],
            send_sem=as_sem.at[core, dx, dz], recv_sem=ar_sem.at[core, dx, dz], device_id={"seq": me},
            device_id_type=mesh_ids)

    far_first = [(core, dx, dz) for dx, dz in reversed(NEAR_FIRST) for core in range(2)] + [(1, 0, 0)]
    for core, dx, dz in far_first:
        a_copy(core, dx, dz).start()
    keep = pltpu.make_async_copy(sendbuf.at[me], rbuf.at[pair, me], lsem.at[15])
    keep.start()
    for dx, dz in NEAR_FIRST:
        g_copy(dx, dz).wait_send()

    lower = jnp.maximum(me - 1, 0)
    upper = jnp.minimum(me + 1, N_SEQ - 1)
    sub = iota((HALO, TOK), 0)
    lane = iota((HALO, TOK), 1)
    for side, neighbour in ((0, lower), (1, upper)):
        blocks = jnp.broadcast_to(gath[neighbour].astype(F32)[11:12, :], (HALO, TOK))
        first = 8 if side == 0 else 0
        chosen = jnp.sum(jnp.where(lane == sub // BLK + first, blocks, 0.0), axis=1, keepdims=True)
        source = chosen * (BLK // CAP) + ((iota((HALO, 1), 0) % BLK) // CAP).astype(F32)
        pick_ref[side] = jnp.where(iota((HALO, N_SEQ), 1).astype(F32) == source, 1.0, 0.0).astype(BF16)
    loads[14].wait()
    d_high, d_low = split(dproj_ref[...])
    dh_ref[...] = jnp.concatenate([d_high.astype(F32)] * (TOK // LAT), axis=0).astype(BF16)
    dl_ref[...] = jnp.concatenate([d_low.astype(F32)] * (TOK // LAT), axis=0).astype(BF16)
    loads[12].wait()
    index = km_ref[...]
    index = jnp.where(index < SLOTS, ((index & (CAP - 1)) << 5) + (index >> 3), index)
    spot_ref[...] = index & (TOK - 1)
    chunk_ref[...] = index >> 7
    near_ref[...] = jnp.minimum(index, 300).astype(F32)
    far_ref[...] = jnp.where(index >= SLOTS, jnp.minimum(index - SLOTS, 300), 300).astype(F32)
    loads[13].wait()
    keep.wait()
    for core, dx, dz in far_first:
        a_arrival(core, dx, dz).wait()
    x_ref[...] = rbuf[0] + rbuf[1]


TRIPLE = 3
PARTS = KOFF // TRIPLE
BLOCKS = FINE // TOK
SHARED = 0


def conv_kernel(
    x_ref, pick_ref, wt, spot_ref, chunk_ref, near_ref, far_ref, dh_ref, dl_ref, owned_ref, dec_ref, feats, prod_a,
    prod_b, acc_x, acc_m
):
    x0 = x_ref[:, 0, :]
    x1 = x_ref[:, 1, :]

    pick = jnp.where(iota((N_SEQ, SLOTS), 1) // CAP == iota((N_SEQ, SLOTS), 0), 1.0, 0.0).astype(BF16)
    xt_high, xt_low = split(x0.T)
    spread = mm(xt_high, pick) + mm(xt_low, pick)
    spread = jnp.where(iota((TOK, SLOTS), 1) % CAP == iota((TOK, SLOTS), 0) // LAT, spread, 0.0)
    owned = spread[0:LAT, :]
    for rank in range(1, CAP):
        owned = owned + spread[rank * LAT : (rank + 1) * LAT, :]
    owned_ref[...] = owned

    lane = iota((SLOTS, TOK), 1)
    own_rows = jnp.where(lane // LAT == iota((SLOTS, TOK), 0) // N_SEQ, jnp.concatenate([x0] * CAP, axis=0), 0.0)
    sub = iota((HALO, TOK), 0)
    lane = iota((HALO, TOK), 1)
    parts = [own_rows]
    for side, x_side in ((0, x0), (1, x1)):
        pick = pick_ref[side]
        x_high, x_low = split(x_side)
        rows = mm(pick, x_high) + mm(pick, x_low)
        offset = CAP if side == 0 else 0
        parts.append(jnp.where(lane // LAT == sub % CAP + offset, rows, 0.0))
    l_high, l_low = split(jnp.concatenate(parts, axis=0))
    p_high, p_low = dh_ref[...], dl_ref[...]
    value = mm(jnp.concatenate([l_high, l_low], axis=1), jnp.concatenate([p_high, p_high], axis=0)) + mm(l_high, p_low)
    half = value * 0.5
    feats[...] = (half * jnp.tanh(half) + half).astype(BF16)
    acc_x[...] = jnp.zeros((OUT_DEV, FINE), F32)
    acc_m[...] = jnp.zeros((OUT_DEV, FINE), F32)

    def product(part, half, target):
        rows = pl.ds(pl.multiple_of(part * (TRIPLE * OUT_DEV), TRIPLE * OUT_DEV), TRIPLE * OUT_DEV)
        table = slice(half * SLOTS, (half + 1) * SLOTS)
        target[:, table] = mm_nt(wt[rows, :], feats[table, :])

    def by_gather(number, source, block):
        columns = slice(block * TOK, (block + 1) * TOK)
        spot = jnp.broadcast_to(spot_ref[number, block : block + 1, :], (OUT_DEV, TOK))
        chunk = jnp.broadcast_to(chunk_ref[number, block : block + 1, :], (OUT_DEV, TOK))
        value = jnp.zeros((OUT_DEV, TOK), F32)
        for c in range(4):
            found = jnp.take_along_axis(source[:, c * TOK : (c + 1) * TOK], spot, axis=1, mode="promise_in_bounds")
            value = jnp.where(chunk == c, found, value)
        acc_x[:, columns] += value

    first_ids = iota((16, TOK), 0).astype(F32).astype(BF16)

    def hot_rows(number, blocks):
        columns = []
        for block in blocks:
            rows = []
            for which in (near_ref, far_ref):
                row = jnp.broadcast_to(which[number, block : block + 1, :], (16, TOK)).astype(BF16) - first_ids
                for j in range(SLOTS // 16):
                    rows.append(jnp.where(row == jnp.bfloat16(16 * j), jnp.bfloat16(1), jnp.bfloat16(0)))
            columns.append(jnp.concatenate(rows, axis=0))
        return jnp.concatenate(columns, axis=1)

    def pick_rows(part, source, target):
        first = part * TRIPLE
        for quarter in range(4):
            blocks = (2 * quarter, 2 * quarter + 1)
            columns = slice(quarter * 2 * TOK, (quarter + 1) * 2 * TOK)
            if target is not None and quarter % 2 == 0:
                product(part + 1, quarter // 2, target)
            found = mm(source[2 * OUT_DEV :, :].astype(BF16), hot_rows(first + 2, blocks))
            if quarter >= SHARED:
                found += mm(source[OUT_DEV : 2 * OUT_DEV, :].astype(BF16), hot_rows(first + 1, blocks))
            acc_m[:, columns] += found
            for block in blocks:
                by_gather(first, source.at[0:OUT_DEV], block)
                if quarter < SHARED:
                    by_gather(first + 1, source.at[OUT_DEV : 2 * OUT_DEV], block)

    for half in range(2):
        product(0, half, prod_a)

    def two_parts(i, carry):
        pick_rows(2 * i, prod_a, prod_b)
        pick_rows(2 * i + 1, prod_b, prod_a)
        return carry

    lax.fori_loop(0, PARTS // 2, two_parts, 0)
    pick_rows(PARTS - 1, prod_a, None)
    dec_ref[...] = (acc_x[...] + acc_m[...]).astype(BF16)


def vmem(count):
    return [pl.BlockSpec(memory_space=pltpu.VMEM)] * count


def in_hbm(*arrays):
    return [pltpu.with_memory_space_constraint(array, pltpu.HBM) for array in arrays]


def hbm(count):
    return [pl.BlockSpec(memory_space=pltpu.HBM)] * count


def per_device(
    latents, voxel_coords, owner_map, step_time, modulation, in_proj, qkv_proj, norm_gain, out_proj, head_proj,
    decoder_projection, border_blocks, kernel_map, conv_weight,
):
    table = centred_position_table()
    table_high = table.astype(jnp.bfloat16)
    table_low = (table - table_high.astype(np.float32)).astype(jnp.bfloat16)
    dma = pltpu.SemaphoreType.DMA
    conv_table = jax.ShapeDtypeStruct((KOFF, BLOCKS, TOK), jnp.int32)
    conv_row = jax.ShapeDtypeStruct((KOFF, BLOCKS, TOK), F32)
    handed = pl.pallas_call(
        flow_kernel,
        out_shape=(
            jax.ShapeDtypeStruct((N_SEQ, 2, TOK), F32), jax.ShapeDtypeStruct((2, HALO, N_SEQ), BF16),
            jax.ShapeDtypeStruct((KOFF * OUT_DEV, DEC), BF16), conv_table, conv_table, conv_row, conv_row,
            jax.ShapeDtypeStruct((TOK, DEC), BF16), jax.ShapeDtypeStruct((TOK, DEC), BF16)),
        in_specs=hbm(3) + [pl.BlockSpec(memory_space=pltpu.SMEM)] + hbm(12),
        out_specs=tuple(vmem(9)),
        scratch_shapes=[
            pltpu.VMEM((LAT, TOK), F32),
            pltpu.VMEM((3, 1, TOK), jnp.int32),
            pltpu.VMEM((1, TOK), jnp.int32),
            pltpu.VMEM((5, 1, D), F32),
            pltpu.VMEM((LAT, D), F32),
            pltpu.VMEM((2, HW), F32),
            pltpu.VMEM((LAT, D), F32),
            pltpu.VMEM((2, 8), jnp.int32),
            pltpu.VMEM((3 * RES, D), BF16),
            pltpu.VMEM((3 * RES, D), BF16),
            pltpu.VMEM((D, 3 * HW), BF16),
            pltpu.VMEM((HW, D), BF16),
            pltpu.VMEM((KOFF, BLOCKS, TOK), jnp.int32),
            pltpu.VMEM((LAT, DEC), F32),
            pltpu.VMEM((N_SEQ, 16, TOK), BF16),
            pltpu.VMEM((16, TOK), F32),
            pltpu.VMEM((FEAT, D), BF16),
            pltpu.VMEM((HW, FEAT), BF16),
            pltpu.VMEM((FEAT, HW), BF16),
            pltpu.VMEM((HEADS * TOK, FEAT), BF16),
            pltpu.VMEM((TOK, D), F32),
            pltpu.VMEM((2, FEAT, 2 * GROUP), BF16),
            pltpu.VMEM((2, FEAT, 2 * GROUP), BF16),
            pltpu.VMEM((HEADS * TOK, 2 * GROUP), BF16),
            pltpu.VMEM((HEADS * TOK, FEAT), F32),
            pltpu.VMEM((LAT, D), BF16),
            pltpu.VMEM((LAT, D), BF16),
            pltpu.VMEM((LAT, TOK), F32),
            pltpu.VMEM((TOK, TOK), F32),
            pltpu.VMEM((3 * N_SEQ, TOK), BF16),
            pltpu.VMEM((N_SEQ, 2, TOK), F32),
            pltpu.VMEM((2, N_SEQ, 2, TOK), F32),
            dma((16,)), dma((NX, NZ)), dma((NX, NZ)), dma((2, NX, NZ)), dma((2, NX, NZ)),
        ],
        compiler_params=pltpu.CompilerParams(collective_id=0, has_side_effects=True, vmem_limit_bytes=40 << 20),
        name="flow",
    )(*in_hbm(
        latents[0], jnp.transpose(voxel_coords, (1, 0, 2)), owner_map.reshape(1, TOK)), step_time, *in_hbm(
        modulation.reshape(5, 1, D), in_proj, norm_gain, head_proj.T, border_blocks[0, 0], jnp.asarray(table_high),
        jnp.asarray(table_low), qkv_proj, out_proj,
        jnp.swapaxes(conv_weight, 1, 2).reshape(KOFF * OUT_DEV, DEC), kernel_map.reshape(KOFF, BLOCKS, TOK), decoder_projection),
    )
    owned, decoded = pl.pallas_call(
        conv_kernel,
        out_shape=(jax.ShapeDtypeStruct((LAT, SLOTS), F32), jax.ShapeDtypeStruct((OUT_DEV, FINE), BF16)),
        in_specs=vmem(9),
        out_specs=tuple(vmem(2)),
        scratch_shapes=[
            pltpu.VMEM((2 * SLOTS, DEC), BF16),
            pltpu.VMEM((TRIPLE * OUT_DEV, 2 * SLOTS), F32),
            pltpu.VMEM((TRIPLE * OUT_DEV, 2 * SLOTS), F32),
            pltpu.VMEM((OUT_DEV, FINE), F32),
            pltpu.VMEM((OUT_DEV, FINE), F32),
        ],
        compiler_params=pltpu.CompilerParams(vmem_limit_bytes=40 << 20),
        name="conv",
    )(*handed)
    return owned[None, None], decoded.T[None, None]


def solution(mesh):
    placed = (
        P("asset", None, "seq"),
        P("asset", None, "seq"),
        P("asset", "seq", None),
        P("asset"),
        P("asset", "pair", None, None),
        P(),
        P(),
        P(),
        P(),
        P(),
        P(),
        P("asset", "seq", None, None),
        P("asset", "seq", None, None),
        P(None, None, "pair"),
    )
    return jax.shard_map(
        per_device,
        mesh=mesh,
        in_specs=placed,
        out_specs=(P("asset", "seq", None, None), P("asset", "seq", None, "pair")),
        check_vma=False,
    )
```

```python
import math

import jax
import jax.numpy as jnp
import numpy as np
from jax import lax
from jax.experimental import pallas as pl
from jax.experimental.pallas import tpu as pltpu
from jax.sharding import PartitionSpec as P

D = 1024
HEADS = 8
HEAD = 64
LAT = 8
DEC = 768
KOFF = 27
BLK = 16
RES = 64
TOK = 128
CAP = 8
SLOTS = 256
HALO = 128
FINE = 1024
HW = 512
NX = 4
NZ = 8
N_SEQ = 32
OUT_DEV = 96
GROUP = NX * TOK
FEAT = 256
TILES = ((0,), (1, 7), (2, 6), (3, 5), (4,))
NEAR_FIRST = tuple((dx, dz) for tile in TILES for dx in (0, 1, 3, 2) for dz in tile if dx or dz)
EPSILON = 1e-06
GUIDANCE = 3.0
LOG2E = 1.4426950408889634
F32 = jnp.float32
BF16 = jnp.bfloat16


def centred_position_table():
    freqs = D // 6
    omegas = np.exp(-math.log(10000.0) * (np.arange(freqs) / freqs))
    angles = np.arange(RES)[:, None] * omegas[None, :]
    halves = np.concatenate([np.sin(angles), np.cos(angles)], axis=1)
    table = np.zeros((3 * RES, D))
    for axis in range(3):
        table[axis * RES : (axis + 1) * RES, axis * 2 * freqs : (axis + 1) * 2 * freqs] = halves
    return (table - table.mean(axis=1, keepdims=True)).astype(np.float32)


def split(values):
    high = values.astype(BF16)
    return high, (values - high.astype(F32)).astype(BF16)


def mm(a, b):
    return lax.dot_general(a, b, (((1,), (0,)), ((), ())), preferred_element_type=F32)


def mm_nt(a, b):
    return lax.dot_general(a, b, (((1,), (1,)), ((), ())), preferred_element_type=F32)


def iota(shape, dim):
    return lax.broadcasted_iota(jnp.int32, shape, dim)


def one_hots(rows, width):
    ids = iota((RES, width), 0).astype(F32)
    return [jnp.where(ids == rows[c : c + 1, :], 1.0, 0.0) for c in range(3)]


def flow_kernel(
    lat_hbm, coord_hbm, own_hbm, step_ref, mod_hbm, inp_hbm, gain_hbm, head_hbm, bb_hbm, tabh_hbm, tabl_hbm, wqkv_hbm,
    wout_hbm, wt_hbm, km_hbm, dproj_hbm,
    x_ref, pick_ref, wt_ref, spot_ref, chunk_ref, near_ref, far_ref, dh_ref, dl_ref,
    lat_ref, coord_ref, own_ref, mod_ref, inp_ref, gain_ref, head_ref, bb_ref, tabh, tabl, wqkv, wout, km_ref, dproj_ref,
    gath, stage, scaled, bkt, bv, umat, hid_ref, ft_ref, fs_ref, p_ref, acc, hp_high, hp_low, hp_const, ranked, dispatch,
    sendbuf, rbuf,
    lsem, gs_sem, gr_sem, as_sem, ar_sem,
):
    me = lax.axis_index("seq")
    pair = lax.axis_index("pair")
    other = 1 - pair
    x_me = me // NZ
    z_me = me % NZ
    mesh_ids = pl.DeviceIdType.MESH

    def ahead(dx, dz):
        return ((x_me + dx) % NX) * NZ + (z_me + dz) % NZ

    def behind(dx, dz):
        return ((x_me + NX - dx) % NX) * NZ + (z_me + NZ - dz) % NZ

    loads = [
        pltpu.make_async_copy(source, target, lsem.at[number])
        for number, (source, target) in enumerate((
            (lat_hbm, lat_ref), (coord_hbm, coord_ref), (own_hbm, own_ref), (mod_hbm, mod_ref), (inp_hbm, inp_ref),
            (gain_hbm, gain_ref), (head_hbm, head_ref), (bb_hbm, bb_ref), (tabh_hbm, tabh), (tabl_hbm, tabl),
            (wqkv_hbm, wqkv), (wout_hbm, wout), (km_hbm, km_ref), (wt_hbm, wt_ref), (dproj_hbm, dproj_ref)))
    ]
    for load in loads[:12]:
        load.start()

    barrier = pltpu.get_barrier_semaphore()
    for dx, dz in reversed(NEAR_FIRST):
        pl.semaphore_signal(barrier, inc=1, device_id={"seq": ahead(dx, dz)}, device_id_type=mesh_ids)
    pl.semaphore_signal(barrier, inc=1, device_id={"pair": other}, device_id_type=mesh_ids)
    for load in loads[:10]:
        load.wait()

    lat = lat_ref[...]
    stage[...] = jnp.zeros((16, TOK), F32)
    stage[0:8, :] = lat
    for axis in range(3):
        stage[8 + axis : 9 + axis, :] = coord_ref[axis].astype(F32)
    stage[11:12, 0:8] = bb_ref[0:1, :].astype(F32)
    stage[11:12, 8:16] = bb_ref[1:2, :].astype(F32)
    lat_high = lat.astype(BF16).astype(F32)
    zero8 = jnp.zeros((8, TOK), F32)
    own_feat = jnp.concatenate(
        one_hots(stage[8:11, :], TOK) + [lat_high, zero8, lat - lat_high, jnp.zeros((40, TOK), F32)], axis=0)
    own_feat = own_feat.T.astype(BF16)
    inp = inp_ref[...]
    inp = inp - jnp.mean(inp, axis=1, keepdims=True)
    inp_rows = jnp.concatenate([inp, jnp.zeros((8, D), F32), inp, jnp.zeros((40, D), F32)], axis=0)
    rows_high, rows_low = split(inp_rows)
    basis_high = jnp.concatenate([tabh[...], rows_high], axis=0)
    basis_low = jnp.concatenate([tabl[...], rows_low], axis=0)
    hidden = mm(own_feat, basis_high) + mm(own_feat, basis_low)
    hid_ref[...] = hidden
    center = hidden - jnp.mean(hidden, axis=1, keepdims=True)
    variance = jnp.mean(center * center, axis=1, keepdims=True)
    std = jnp.broadcast_to(jnp.sqrt(variance + EPSILON), (TOK, TOK)).T[0:1, :]
    std_high = std.astype(BF16).astype(F32)
    stage[12:13, :] = std_high
    stage[13:14, :] = std - std_high
    gath[me] = stage[...].astype(BF16)

    def g_copy(dx, dz):
        return pltpu.make_async_remote_copy(
            src_ref=gath.at[me], dst_ref=gath.at[me], send_sem=gs_sem.at[dx, dz], recv_sem=gr_sem.at[dx, dz],
            device_id={"seq": ahead(dx, dz)}, device_id_type=mesh_ids)

    own_rows = jnp.broadcast_to(own_ref[...], (TOK, TOK)).astype(F32)
    own_cols = own_rows.T
    earlier = (own_rows == own_cols) & (iota((TOK, TOK), 0) < iota((TOK, TOK), 1))
    rank = jnp.sum(jnp.where(earlier, 1.0, 0.0), axis=0, keepdims=True)
    ranked[...] = jnp.where(rank == ((iota((TOK, TOK), 0) // LAT) % CAP).astype(F32), 1.0, 0.0)
    own96 = jnp.broadcast_to(own_ref[...], (3 * N_SEQ, TOK))
    owner = iota((3 * N_SEQ, TOK), 0)
    owner = jnp.where(owner < N_SEQ, owner, jnp.where(owner < 2 * N_SEQ, owner - N_SEQ - 1, owner - 2 * N_SEQ + 1))
    dispatch[...] = jnp.where(own96 == owner, 1.0, 0.0).astype(BF16)

    scale1 = 1.0 + mod_ref[1]
    normed = (center * lax.rsqrt(variance + EPSILON) * scale1 + mod_ref[0]).astype(BF16)
    for axis in range(3):
        rows = slice(axis * RES, (axis + 1) * RES)
        scaled[rows, :] = ((tabh[rows, :].astype(F32) + tabl[rows, :].astype(F32)) * scale1).astype(BF16)
    shift_rows = jnp.where(iota((8, D), 0) < 2, jnp.broadcast_to(mod_ref[0], (8, D)), 0.0)
    scaled[3 * RES :, :] = jnp.concatenate([inp * scale1, shift_rows, jnp.zeros((48, D), F32)], axis=0).astype(BF16)
    loads[10].wait()
    queries = mm(normed, wqkv[:, 0:HW])
    per_head = jnp.where(iota((HW, HW), 0) // HEAD == iota((HW, HW), 1) // HEAD, 1.0 / HEAD, 0.0).astype(BF16)
    mean_sq = mm((queries * queries).astype(BF16), per_head)
    queries = queries * lax.rsqrt(mean_sq + EPSILON) * (
        gain_ref[0:1, :] * gain_ref[1:2, :] * (HEAD ** (-0.5) * LOG2E))
    bkt[...] = mm(scaled[...], wqkv[:, HW : 2 * HW]).T.astype(BF16)
    first_half = iota((TOK, 2 * HEAD), 1) < HEAD
    for two in range(HEADS // 2):
        columns = slice(two * 2 * HEAD, (two + 1) * 2 * HEAD)
        both = queries[:, columns]
        mine = jnp.concatenate([jnp.where(first_half, both, 0.0), jnp.where(first_half, 0.0, both)], axis=0)
        umat[two * 256 : (two + 1) * 256, :] = mm(mine.astype(BF16), bkt[columns, :]).astype(BF16)

    pl.semaphore_wait(barrier, N_SEQ)
    for dx, dz in NEAR_FIRST:
        g_copy(dx, dz).start()

    bv[...] = mm(scaled[...], wqkv[:, 2 * HW : 3 * HW]).astype(BF16)
    head_scaled = head_ref[...] * (1.0 + mod_ref[4])
    hp_high[...], hp_low[...] = split(head_scaled)
    hp_const[...] = jnp.broadcast_to(jnp.sum(head_ref[...] * mod_ref[3], axis=1, keepdims=True), (LAT, TOK))
    for load in loads[12:]:
        load.start()

    def features(number):
        sources = []
        for dz in TILES[number]:
            for dx in range(NX):
                source = behind(dx, dz)
                sources.append(source)
                if dx > 0 or dz > 0:
                    pltpu.make_async_remote_copy(
                        src_ref=gath.at[source], dst_ref=gath.at[source], send_sem=gs_sem.at[dx, dz],
                        recv_sem=gr_sem.at[dx, dz], device_id={"seq": me}, device_id_type=mesh_ids).wait_recv()
        width = TOK * len(sources)
        rows = jnp.concatenate([gath[source].astype(F32) for source in sources], axis=1)
        std_high, std_low = rows[12:13, :], rows[13:14, :]
        std = std_high + std_low
        inv_std = 1.0 / std
        which = iota((8, width), 0)
        ids = iota((RES, width), 0).astype(F32)
        ft, fs = ft_ref.at[number % 2], fs_ref.at[number % 2]
        for c in range(3):
            hit = ids == rows[8 + c : 9 + c, :]
            ft[c * RES : (c + 1) * RES, 0:width] = jnp.where(hit, 1.0, 0.0).astype(BF16)
            fs[c * RES : (c + 1) * RES, 0:width] = jnp.where(hit, inv_std, 0.0).astype(BF16)
        std_rows = jnp.where(which == 0, std_high, jnp.where(which == 1, std_low, 0.0))
        pad = jnp.zeros((48, width), F32)
        ft[3 * RES :, 0:width] = jnp.concatenate([rows[0:8, :], std_rows, pad], axis=0).astype(BF16)
        fs[3 * RES :, 0:width] = jnp.concatenate(
            [rows[0:8, :] * inv_std, jnp.where(which == 0, 1.0, 0.0), pad], axis=0).astype(BF16)
        return width, EPSILON * (std * std)

    width, eps_var = features(0)
    for number in range(len(TILES)):
        ft, fs = ft_ref[number % 2, :, 0:width], fs_ref[number % 2, :, 0:width]
        used, used_var = width, eps_var
        keys = mm(bkt[...], ft)
        scores = mm(umat[...], ft)
        for head in range(HEADS):
            keys_h = keys[head * HEAD : (head + 1) * HEAD, :]
            mean_h = jnp.sum(keys_h * keys_h, axis=0, keepdims=True) * (1.0 / HEAD)
            inv = lax.rsqrt(mean_h + used_var)
            p_ref[head * TOK : (head + 1) * TOK, 0:used] = jnp.exp2(
                scores[head * TOK : (head + 1) * TOK, :] * inv).astype(BF16)
        if number + 1 < len(TILES):
            width, eps_var = features(number + 1)
        found = mm_nt(p_ref[:, 0:used], fs)
        if number > 0:
            found += acc[...]
        acc[...] = found

    loads[11].wait()
    lane = iota((TOK, FEAT), 1)
    pieces = []
    for two in range(HEADS // 2):
        columns = slice(two * 2 * HEAD, (two + 1) * 2 * HEAD)
        halves = []
        for odd in range(2):
            head = 2 * two + odd
            total = acc[head * TOK : (head + 1) * TOK, :]
            denom = jnp.sum(jnp.where(lane == 200, total, 0.0), axis=1, keepdims=True)
            halves.append((total * (1.0 / denom)).astype(BF16))
        found = mm(jnp.concatenate(halves, axis=0), bv[:, columns])
        pieces.append(jnp.where(first_half, found[0:TOK, :], found[TOK : 2 * TOK, :]))
    attended = jnp.concatenate(pieces, axis=1).astype(BF16)
    width = 256
    total = jnp.zeros((TOK, 1), F32)
    for part in range(D // width):
        columns = slice(part * width, (part + 1) * width)
        piece = hid_ref[:, columns] + mod_ref[2][:, columns] * mm(attended, wout[:, columns])
        hid_ref[:, columns] = piece
        total = total + jnp.sum(piece, axis=1, keepdims=True)
    mean = total * (1.0 / D)
    square = jnp.zeros((TOK, 1), F32)
    velocity = jnp.zeros((LAT, TOK), F32)
    for part in range(D // width):
        columns = slice(part * width, (part + 1) * width)
        center = hid_ref[:, columns] - mean
        square = square + jnp.sum(center * center, axis=1, keepdims=True)
        c_high, c_low = split(center)
        velocity = velocity + (mm_nt(hp_high[:, columns], c_high)
                               + (mm_nt(hp_high[:, columns], c_low) + mm_nt(hp_low[:, columns], c_high)))
    inv_dev = jnp.broadcast_to(lax.rsqrt(square * (1.0 / D) + EPSILON), (TOK, TOK)).T[0:1, :]
    velocity = velocity * inv_dev + hp_const[...]

    is_cond = pair == 0
    share = jnp.where(is_cond, 1.0, 0.0) * lat_ref[...] + (
        step_ref[0] * jnp.where(is_cond, -GUIDANCE, GUIDANCE - 1.0)) * velocity
    wide = jnp.concatenate([share] * (TOK // LAT), axis=0) * ranked[...]
    wide_high, wide_low = split(wide)
    packed = mm_nt(dispatch[...], wide_high) + mm_nt(dispatch[...], wide_low)
    sendbuf[:, 0, :] = jnp.where(
        iota((N_SEQ, TOK), 1) < LAT * CAP, packed[0:N_SEQ, :], packed[N_SEQ : 2 * N_SEQ, :])
    sendbuf[:, 1, :] = packed[2 * N_SEQ :, :]

    def a_copy(core, dx, dz):
        dest = ahead(dx, dz)
        return pltpu.make_async_remote_copy(
            src_ref=sendbuf.at[dest], dst_ref=rbuf.at[pair, me], send_sem=as_sem.at[core, dx, dz],
            recv_sem=ar_sem.at[core, dx, dz], device_id={"pair": pair if core == 0 else other, "seq": dest},
            device_id_type=mesh_ids)

    def a_arrival(core, dx, dz):
        source = behind(dx, dz)
        return pltpu.make_async_remote_copy(
            src_ref=sendbuf.at[source], dst_ref=rbuf.at[pair if core == 0 else other, source],
            send_sem=as_sem.at[core, dx, dz], recv_sem=ar_sem.at[core, dx, dz], device_id={"seq": me},
            device_id_type=mesh_ids)

    far_first = [(core, dx, dz) for dx, dz in reversed(NEAR_FIRST) for core in range(2)] + [(1, 0, 0)]
    for core, dx, dz in far_first:
        a_copy(core, dx, dz).start()
    keep = pltpu.make_async_copy(sendbuf.at[me], rbuf.at[pair, me], lsem.at[15])
    keep.start()
    for dx, dz in NEAR_FIRST:
        g_copy(dx, dz).wait_send()

    lower = jnp.maximum(me - 1, 0)
    upper = jnp.minimum(me + 1, N_SEQ - 1)
    sub = iota((HALO, TOK), 0)
    lane = iota((HALO, TOK), 1)
    for side, neighbour in ((0, lower), (1, upper)):
        blocks = jnp.broadcast_to(gath[neighbour].astype(F32)[11:12, :], (HALO, TOK))
        first = 8 if side == 0 else 0
        chosen = jnp.sum(jnp.where(lane == sub // BLK + first, blocks, 0.0), axis=1, keepdims=True)
        source = chosen * (BLK // CAP) + ((iota((HALO, 1), 0) % BLK) // CAP).astype(F32)
        pick_ref[side] = jnp.where(iota((HALO, N_SEQ), 1).astype(F32) == source, 1.0, 0.0).astype(BF16)
    loads[14].wait()
    d_high, d_low = split(dproj_ref[...])
    dh_ref[...] = jnp.concatenate([d_high.astype(F32)] * (TOK // LAT), axis=0).astype(BF16)
    dl_ref[...] = jnp.concatenate([d_low.astype(F32)] * (TOK // LAT), axis=0).astype(BF16)
    loads[12].wait()
    index = km_ref[...]
    index = jnp.where(index < SLOTS, ((index & (CAP - 1)) << 5) + (index >> 3), index)
    spot_ref[...] = index & (TOK - 1)
    chunk_ref[...] = index >> 7
    near_ref[...] = jnp.minimum(index, 300).astype(F32)
    far_ref[...] = jnp.where(index >= SLOTS, jnp.minimum(index - SLOTS, 300), 300).astype(F32)
    loads[13].wait()
    keep.wait()
    for core, dx, dz in far_first:
        a_arrival(core, dx, dz).wait()
    x_ref[...] = rbuf[0] + rbuf[1]


TRIPLE = 3
PARTS = KOFF // TRIPLE
BLOCKS = FINE // TOK
SHARED = 0


def conv_kernel(
    x_ref, pick_ref, wt, spot_ref, chunk_ref, near_ref, far_ref, dh_ref, dl_ref, owned_ref, dec_ref, feats, prod_a,
    prod_b, acc_x, acc_m
):
    x0 = x_ref[:, 0, :]
    x1 = x_ref[:, 1, :]

    pick = jnp.where(iota((N_SEQ, SLOTS), 1) // CAP == iota((N_SEQ, SLOTS), 0), 1.0, 0.0).astype(BF16)
    xt_high, xt_low = split(x0.T)
    spread = mm(xt_high, pick) + mm(xt_low, pick)
    spread = jnp.where(iota((TOK, SLOTS), 1) % CAP == iota((TOK, SLOTS), 0) // LAT, spread, 0.0)
    owned = spread[0:LAT, :]
    for rank in range(1, CAP):
        owned = owned + spread[rank * LAT : (rank + 1) * LAT, :]
    owned_ref[...] = owned

    lane = iota((SLOTS, TOK), 1)
    own_rows = jnp.where(lane // LAT == iota((SLOTS, TOK), 0) // N_SEQ, jnp.concatenate([x0] * CAP, axis=0), 0.0)
    sub = iota((HALO, TOK), 0)
    lane = iota((HALO, TOK), 1)
    parts = [own_rows]
    for side, x_side in ((0, x0), (1, x1)):
        pick = pick_ref[side]
        x_high, x_low = split(x_side)
        rows = mm(pick, x_high) + mm(pick, x_low)
        offset = CAP if side == 0 else 0
        parts.append(jnp.where(lane // LAT == sub % CAP + offset, rows, 0.0))
    l_high, l_low = split(jnp.concatenate(parts, axis=0))
    p_high, p_low = dh_ref[...], dl_ref[...]
    value = mm(jnp.concatenate([l_high, l_low], axis=1), jnp.concatenate([p_high, p_high], axis=0)) + mm(l_high, p_low)
    half = value * 0.5
    feats[...] = (half * jnp.tanh(half) + half).astype(BF16)
    acc_x[...] = jnp.zeros((OUT_DEV, FINE), F32)
    acc_m[...] = jnp.zeros((OUT_DEV, FINE), F32)

    def product(part, half, target):
        rows = pl.ds(pl.multiple_of(part * (TRIPLE * OUT_DEV), TRIPLE * OUT_DEV), TRIPLE * OUT_DEV)
        table = slice(half * SLOTS, (half + 1) * SLOTS)
        target[:, table] = mm_nt(wt[rows, :], feats[table, :])

    def by_gather(number, source, block):
        columns = slice(block * TOK, (block + 1) * TOK)
        spot = jnp.broadcast_to(spot_ref[number, block : block + 1, :], (OUT_DEV, TOK))
        chunk = jnp.broadcast_to(chunk_ref[number, block : block + 1, :], (OUT_DEV, TOK))
        value = jnp.zeros((OUT_DEV, TOK), F32)
        for c in range(4):
            found = jnp.take_along_axis(source[:, c * TOK : (c + 1) * TOK], spot, axis=1, mode="promise_in_bounds")
            value = jnp.where(chunk == c, found, value)
        acc_x[:, columns] += value

    first_ids = iota((16, TOK), 0).astype(F32).astype(BF16)

    def hot_rows(number, blocks):
        columns = []
        for block in blocks:
            rows = []
            for which in (near_ref, far_ref):
                row = jnp.broadcast_to(which[number, block : block + 1, :], (16, TOK)).astype(BF16) - first_ids
                for j in range(SLOTS // 16):
                    rows.append(jnp.where(row == jnp.bfloat16(16 * j), jnp.bfloat16(1), jnp.bfloat16(0)))
            columns.append(jnp.concatenate(rows, axis=0))
        return jnp.concatenate(columns, axis=1)

    def pick_rows(part, source, target):
        first = part * TRIPLE
        for quarter in range(4):
            blocks = (2 * quarter, 2 * quarter + 1)
            columns = slice(quarter * 2 * TOK, (quarter + 1) * 2 * TOK)
            if target is not None and quarter % 2 == 0:
                product(part + 1, quarter // 2, target)
            found = mm(source[2 * OUT_DEV :, :].astype(BF16), hot_rows(first + 2, blocks))
            if quarter >= SHARED:
                found += mm(source[OUT_DEV : 2 * OUT_DEV, :].astype(BF16), hot_rows(first + 1, blocks))
            acc_m[:, columns] += found
            for block in blocks:
                by_gather(first, source.at[0:OUT_DEV], block)
                if quarter < SHARED:
                    by_gather(first + 1, source.at[OUT_DEV : 2 * OUT_DEV], block)

    for half in range(2):
        product(0, half, prod_a)

    def two_parts(i, carry):
        pick_rows(2 * i, prod_a, prod_b)
        pick_rows(2 * i + 1, prod_b, prod_a)
        return carry

    lax.fori_loop(0, PARTS // 2, two_parts, 0)
    pick_rows(PARTS - 1, prod_a, None)
    dec_ref[...] = (acc_x[...] + acc_m[...]).astype(BF16)


def vmem(count):
    return [pl.BlockSpec(memory_space=pltpu.VMEM)] * count


def in_hbm(*arrays):
    return [pltpu.with_memory_space_constraint(array, pltpu.HBM) for array in arrays]


def hbm(count):
    return [pl.BlockSpec(memory_space=pltpu.HBM)] * count


def per_device(
    latents, voxel_coords, owner_map, step_time, modulation, in_proj, qkv_proj, norm_gain, out_proj, head_proj,
    decoder_projection, border_blocks, kernel_map, conv_weight,
):
    table = centred_position_table()
    table_high = table.astype(jnp.bfloat16)
    table_low = (table - table_high.astype(np.float32)).astype(jnp.bfloat16)
    dma = pltpu.SemaphoreType.DMA
    conv_table = jax.ShapeDtypeStruct((KOFF, BLOCKS, TOK), jnp.int32)
    conv_row = jax.ShapeDtypeStruct((KOFF, BLOCKS, TOK), F32)
    handed = pl.pallas_call(
        flow_kernel,
        out_shape=(
            jax.ShapeDtypeStruct((N_SEQ, 2, TOK), F32), jax.ShapeDtypeStruct((2, HALO, N_SEQ), BF16),
            jax.ShapeDtypeStruct((KOFF * OUT_DEV, DEC), BF16), conv_table, conv_table, conv_row, conv_row,
            jax.ShapeDtypeStruct((TOK, DEC), BF16), jax.ShapeDtypeStruct((TOK, DEC), BF16)),
        in_specs=hbm(3) + [pl.BlockSpec(memory_space=pltpu.SMEM)] + hbm(12),
        out_specs=tuple(vmem(9)),
        scratch_shapes=[
            pltpu.VMEM((LAT, TOK), F32),
            pltpu.VMEM((3, 1, TOK), jnp.int32),
            pltpu.VMEM((1, TOK), jnp.int32),
            pltpu.VMEM((5, 1, D), F32),
            pltpu.VMEM((LAT, D), F32),
            pltpu.VMEM((2, HW), F32),
            pltpu.VMEM((LAT, D), F32),
            pltpu.VMEM((2, 8), jnp.int32),
            pltpu.VMEM((3 * RES, D), BF16),
            pltpu.VMEM((3 * RES, D), BF16),
            pltpu.VMEM((D, 3 * HW), BF16),
            pltpu.VMEM((HW, D), BF16),
            pltpu.VMEM((KOFF, BLOCKS, TOK), jnp.int32),
            pltpu.VMEM((LAT, DEC), F32),
            pltpu.VMEM((N_SEQ, 16, TOK), BF16),
            pltpu.VMEM((16, TOK), F32),
            pltpu.VMEM((FEAT, D), BF16),
            pltpu.VMEM((HW, FEAT), BF16),
            pltpu.VMEM((FEAT, HW), BF16),
            pltpu.VMEM((HEADS * TOK, FEAT), BF16),
            pltpu.VMEM((TOK, D), F32),
            pltpu.VMEM((2, FEAT, 2 * GROUP), BF16),
            pltpu.VMEM((2, FEAT, 2 * GROUP), BF16),
            pltpu.VMEM((HEADS * TOK, 2 * GROUP), BF16),
            pltpu.VMEM((HEADS * TOK, FEAT), F32),
            pltpu.VMEM((LAT, D), BF16),
            pltpu.VMEM((LAT, D), BF16),
            pltpu.VMEM((LAT, TOK), F32),
            pltpu.VMEM((TOK, TOK), F32),
            pltpu.VMEM((3 * N_SEQ, TOK), BF16),
            pltpu.VMEM((N_SEQ, 2, TOK), F32),
            pltpu.VMEM((2, N_SEQ, 2, TOK), F32),
            dma((16,)), dma((NX, NZ)), dma((NX, NZ)), dma((2, NX, NZ)), dma((2, NX, NZ)),
        ],
        compiler_params=pltpu.CompilerParams(collective_id=0, has_side_effects=True, vmem_limit_bytes=40 << 20),
        name="flow",
    )(*in_hbm(
        latents[0], jnp.transpose(voxel_coords, (1, 0, 2)), owner_map.reshape(1, TOK)), step_time, *in_hbm(
        modulation.reshape(5, 1, D), in_proj, norm_gain, head_proj.T, border_blocks[0, 0], jnp.asarray(table_high),
        jnp.asarray(table_low), qkv_proj, out_proj,
        jnp.swapaxes(conv_weight, 1, 2).reshape(KOFF * OUT_DEV, DEC), kernel_map.reshape(KOFF, BLOCKS, TOK), decoder_projection),
    )
    owned, decoded = pl.pallas_call(
        conv_kernel,
        out_shape=(jax.ShapeDtypeStruct((LAT, SLOTS), F32), jax.ShapeDtypeStruct((OUT_DEV, FINE), BF16)),
        in_specs=vmem(9),
        out_specs=tuple(vmem(2)),
        scratch_shapes=[
            pltpu.VMEM((2 * SLOTS, DEC), BF16),
            pltpu.VMEM((TRIPLE * OUT_DEV, 2 * SLOTS), F32),
            pltpu.VMEM((TRIPLE * OUT_DEV, 2 * SLOTS), F32),
            pltpu.VMEM((OUT_DEV, FINE), F32),
            pltpu.VMEM((OUT_DEV, FINE), F32),
        ],
        compiler_params=pltpu.CompilerParams(vmem_limit_bytes=40 << 20),
        name="conv",
    )(*handed)
    return owned[None, None], decoded.T[None, None]


def solution(mesh):
    placed = (
        P("asset", None, "seq"),
        P("asset", None, "seq"),
        P("asset", "seq", None),
        P("asset"),
        P("asset", "pair", None, None),
        P(),
        P(),
        P(),
        P(),
        P(),
        P(),
        P("asset", "seq", None, None),
        P("asset", "seq", None, None),
        P(None, None, "pair"),
    )
    return jax.shard_map(
        per_device,
        mesh=mesh,
        in_specs=placed,
        out_specs=(P("asset", "seq", None, None), P("asset", "seq", None, "pair")),
        check_vma=False,
    )
```
